32 devices in a mesh: dp: 16 (over z, y, core), tensor: 2 (over x).
Axes of the slice: x: 2, y: 2, z: 4, core: 2. Of those that a mesh axis runs over, the one named last changes fastest.
Arguments:
- tokens: bfloat16 [16384, 1024], P('dp'), may hold values from -6 to 6
- segment_ids: int32 [16, 1024], P('dp'), may hold values from 0 to 4, never falling along the last dimension, each value on 1 to 384 neighbouring positions
- decay_rate: float32 [8], P('tensor'), may hold values from 0.00029296876 to 0.08
- query_weight: bfloat16 [1024, 1024], P(None, 'tensor'), may hold values from -0.1875 to 0.1875
- key_weight: bfloat16 [1024, 1024], P(None, 'tensor'), may hold values from -0.1875 to 0.1875
- value_weight: bfloat16 [1024, 1024], P(None, 'tensor'), may hold values from -0.1875 to 0.1875
- gate_weight: bfloat16 [1024, 1024], P(None, 'tensor'), may hold values from -0.1875 to 0.1875
- output_weight: bfloat16 [1024, 1024], P('tensor'), may hold values from -0.1875 to 0.1875
- norm_gain: bfloat16 [8, 128], P('tensor'), may hold values from 0.099609375 to 1.8984375
- left_weight: bfloat16 [1024, 2816], P(None, 'tensor'), may hold values from -0.1875 to 0.1875
- right_weight: bfloat16 [1024, 2816], P(None, 'tensor'), may hold values from -0.1875 to 0.1875
- down_weight: bfloat16 [2816, 1024], P('tensor'), may hold values from -0.109375 to 0.109375
- cotangent: bfloat16 [16384, 1024], P('dp'), may hold values from -6 to 6
Outputs:
- block_out: bfloat16 [16384, 1024], P('dp')
- tokens_grad: float32 [16384, 1024], P('dp')
- query_grad: float32 [1024, 1024], P('dp', 'tensor')
- key_grad: float32 [1024, 1024], P('dp', 'tensor')
- value_grad: float32 [1024, 1024], P('dp', 'tensor')
- gate_grad: float32 [1024, 1024], P('dp', 'tensor')
- output_grad: float32 [1024, 1024], P('tensor', 'dp')
- gain_grad: float32 [8, 128], P('tensor', 'dp')
- left_grad: float32 [1024, 2816], P('dp', 'tensor')
- right_grad: float32 [1024, 2816], P('dp', 'tensor')
- down_grad: float32 [2816, 1024], P('tensor', 'dp')
The draws below stay inside these ranges and needn't reach their ends.
Inputs may be any that keep to these rules, and one draw needn't show every extreme that they name: `segment_ids`: along each packed sequence the ids never fall; a document holds at most 384 tokens, and some document holds exactly that many.
All inputs are finite; a program needn't handle non-finite values.
Results may differ from the reference program's by a relative error of at most 0.014.
Values may be sent and summed in bfloat16 or wider, within the bound.
A program may use at most 192 MiB of HBM per device.

```python
import math
import jax
import jax.numpy as jnp
import numpy as np
from jax import lax

D = 1024
H = 8
HEAD = 128
FF = 2816
LEN = 1024
HD = 1024
SEQS = 16
TOKENS = 16384


def level_of(key, dims, shards, low, top_value):
    def one(axis_at, parts):
        draws = jax.random.uniform(jax.random.fold_in(jax.random.fold_in(key, 6), axis_at), (parts,), jnp.float32, low / len(shards), top_value / len(shards))
        return jnp.repeat(jnp.exp(draws), dims[axis_at] // parts).reshape((-1,) + (1,) * (len(dims) - axis_at - 1))

    loudness = one(*shards[0])
    for cut in shards[1:]:
        loudness = loudness * one(*cut)
    return loudness


def split_up(amount, total, bound, skew):
    loads = [(1 << 20) // math.isqrt(standing ** skew) + 1 for standing in range(2, amount + 1)]
    surplus, holding = total - bound - (amount - 1), [1] * (amount - 1)
    while surplus > 0:
        free = [i for i in range(amount - 1) if holding[i] < bound]
        mass, left = sum([loads[i] for i in free]), surplus
        for i in free:
            addition = min(bound - holding[i], max(1, left * loads[i] // mass), surplus)
            holding[i] = holding[i] + addition
            surplus = surplus - addition
    return np.array([bound] + holding)


def uneven(own_key, number_of, total, limit, slope):
    if number_of == 2:
        one = jax.random.randint(own_key, (), max(1, total - limit), min(limit, total - 1) + 1)
        return jnp.stack([one, total - one])
    sizes = jnp.asarray(split_up(number_of, total, limit, slope), jnp.int32)
    couples = (number_of - 1) // 2
    donor, taker = sizes[1:1 + 2 * couples:2], sizes[2:2 + 2 * couples:2]
    margin = jnp.minimum(donor - 1, limit - taker)
    passed = jax.random.randint(jax.random.fold_in(own_key, 1), (couples,), 0, 1 << 20) % (margin + 1)
    sizes = sizes.at[1:1 + 2 * couples:2].set(donor - passed).at[2:2 + 2 * couples:2].set(taker + passed)
    return sizes[jax.random.permutation(jax.random.fold_in(own_key, 2), number_of)]


def scatter_about(rng, extent, scale, limit, split=(), dtype=jnp.bfloat16):
    drawn = jax.random.normal(rng, extent, jnp.float32) * scale
    if len(split) > 0:
        drawn = level_of(rng, extent, split, -0.22, 0.18) * drawn
    return jnp.clip(drawn, min=-limit, max=limit).astype(dtype)


def setup_inputs(seed: int = 0) -> dict:
    seeds = jax.random.split(jax.random.key(seed), 14)
    tokens = scatter_about(seeds[0], (TOKENS, D), 1.0, 6.0, ((0, 16),))
    segment_ids = jax.vmap(lambda own: jnp.searchsorted(jnp.cumsum(uneven(own, 5, LEN, LEN * 3 // 8, 1)), jnp.arange(LEN), side="right"))(jax.random.split(seeds[1], SEQS)).reshape((SEQS, LEN)).astype(jnp.int32)
    decay_rate = jnp.clip(jnp.exp(math.log(0.08) - 5.609716 * jax.random.uniform(seeds[2], (H,), jnp.float32) ** level_of(seeds[2], (H,), ((0, 2),), -0.2, 0.2)), 0.00029296876, 0.08)
    query_weight = scatter_about(seeds[3], (D, HD), D ** -0.5, 0.1875, ((1, 2),))
    key_weight = scatter_about(seeds[4], (D, HD), D ** -0.5, 0.1875, ((1, 2),))
    value_weight = scatter_about(seeds[5], (D, HD), D ** -0.5, 0.1875, ((1, 2),))
    gate_weight = scatter_about(seeds[6], (D, HD), D ** -0.5, 0.1875, ((1, 2),))
    output_weight = scatter_about(seeds[7], (HD, D), HD ** -0.5, 0.1875, ((0, 2),))
    norm_gain = jnp.clip(1.0 + 0.18 * jax.random.normal(seeds[8], (H, HEAD), jnp.float32), 0.099609375, 1.8984375).astype(jnp.bfloat16)
    left_weight = scatter_about(seeds[9], (D, FF), D ** -0.5, 0.1875, ((1, 2),))
    right_weight = scatter_about(seeds[10], (D, FF), D ** -0.5, 0.1875, ((1, 2),))
    down_weight = scatter_about(seeds[11], (FF, D), FF ** -0.5, 0.109375, ((0, 2),))
    cotangent = scatter_about(seeds[12], (TOKENS, D), 1.0, 6.0, ((0, 16),))
    return dict(tokens=tokens, segment_ids=segment_ids, decay_rate=decay_rate, query_weight=query_weight, key_weight=key_weight, value_weight=value_weight, gate_weight=gate_weight, output_weight=output_weight, norm_gain=norm_gain, left_weight=left_weight, right_weight=right_weight, down_weight=down_weight, cotangent=cotangent)


@jax.custom_vjp
def low(v):
    return lax.optimization_barrier(v.astype(jnp.bfloat16)).astype(jnp.float32)

@jax.custom_vjp
def low_back(v):
    return v

def low_keep(v):
    return (low(v), None)

def low_pass(kept, grad):
    return (grad,)

def back_keep(v):
    return (v, None)

def back_low(kept, grad):
    return (low(grad),)
low.defvjp(low_keep, low_pass)
low_back.defvjp(back_keep, back_low)
eps = 1e-06

def product(left_op, right_op):
    return jnp.dot(left_op, right_op, precision=lax.Precision.HIGHEST, preferred_element_type=jnp.float32)

def layer(source, segment, decays, query_weight, key_weight, value_weight, gate_weight, output_weight, norm_gain, left_weight, right_weight, down_weight):
    scale_in = lax.rsqrt(lax.optimization_barrier(jnp.mean(source * source, axis=1, keepdims=True)) + eps)
    normed = low(source * scale_in)
    queries = low(jax.nn.silu(low_back(product(normed, query_weight))))
    key_rows = low(jax.nn.silu(low_back(product(normed, key_weight))))
    value_rows = low(low_back(product(normed, value_weight)))
    gate_act = low_back(product(normed, gate_weight))
    positions = jnp.arange(LEN)
    distance = positions[:, None] - positions[None, :]
    allowed = (distance >= 0) & (segment[:, None] == segment[None, :])
    falloff = jnp.exp(-decays[:, None, None] * jnp.maximum(distance, 0).astype(jnp.float32)[None])
    masking = jnp.where(allowed[None], falloff, jnp.float32(0.0))
    query_heads = queries.reshape(LEN, H, HEAD)
    key_heads = key_rows.reshape(LEN, H, HEAD)
    value_heads = value_rows.reshape(LEN, H, HEAD)
    scores = low_back(jnp.einsum('qhd,khd->hqk', query_heads, key_heads, precision=lax.Precision.HIGHEST))
    weighted = low(scores * masking)
    heads_out = low_back(jnp.einsum('hqk,khd->qhd', weighted, value_heads, precision=lax.Precision.HIGHEST)).reshape(LEN, H * HEAD)
    scale_out = lax.rsqrt(lax.optimization_barrier(jnp.mean(heads_out * heads_out, axis=1, keepdims=True)) + eps)
    mixed = low(heads_out * scale_out * norm_gain.reshape(H * HEAD) * gate_act)
    hidden = source + low_back(product(mixed, output_weight))
    scale_mid = lax.rsqrt(lax.optimization_barrier(jnp.mean(hidden * hidden, axis=1, keepdims=True)) + eps)
    lifted = low(hidden * scale_mid)
    left_act = low_back(product(lifted, left_weight))
    right_act = low_back(product(lifted, right_weight))
    joined = low(left_act * right_act)
    return hidden + low_back(product(joined, down_weight))

def reference(tokens, segment_ids, decay_rate, query_weight, key_weight, value_weight, gate_weight, output_weight, norm_gain, left_weight, right_weight, down_weight, cotangent):
    weights = tuple((matrix.astype(jnp.float32) for matrix in (query_weight, key_weight, value_weight, gate_weight, output_weight, norm_gain, left_weight, right_weight, down_weight)))
    sources = tokens.astype(jnp.float32).reshape(SEQS, LEN, D)
    pulls = cotangent.astype(jnp.float32).reshape(SEQS, LEN, D)
    decays = decay_rate.astype(jnp.float32)

    def one_sequence(totals, entries):
        source, segment, pull = entries

        def forward(source_in, *params):
            return layer(source_in, segment, decays, *params)
        result, backward = jax.vjp(forward, source, *weights)
        grads = backward(pull)
        totals = tuple((total + grad for total, grad in zip(totals, grads[1:])))
        return (totals, (result.astype(jnp.bfloat16), grads[0]))
    start = tuple((jnp.zeros(matrix.shape, jnp.float32) for matrix in weights))
    totals, (results, input_grads) = lax.scan(one_sequence, start, (sources, segment_ids, pulls))
    return (results.reshape(TOKENS, D), input_grads.reshape(TOKENS, D), totals[0], totals[1], totals[2], totals[3], totals[4], totals[5], totals[6], totals[7], totals[8])
```

```python
import jax
import jax.numpy as jnp
from jax import lax
from jax.sharding import PartitionSpec as P

eps = 1e-06


def product(left_op, right_op):
    return jnp.dot(left_op, right_op, preferred_element_type=jnp.float32)


def product_tn(left_op, right_op):
    return lax.dot_general(
        left_op, right_op, (((0,), (0,)), ((), ())), preferred_element_type=jnp.float32
    )


def product_nt(left_op, right_op):
    return lax.dot_general(
        left_op, right_op, (((1,), (1,)), ((), ())), preferred_element_type=jnp.float32
    )


def rms_scale(values):
    return lax.rsqrt(jnp.mean(values * values, axis=1, keepdims=True) + eps)


def rms_back(values, scale, grads):
    return scale * grads - values * (scale * scale * scale) * jnp.mean(
        values * grads, axis=1, keepdims=True
    )


def silu_slope(values):
    sigma = jax.nn.sigmoid(values)
    return sigma * (1.0 + values * (1.0 - sigma))


def swap_half(values):
    return lax.ppermute(values, "tensor", [(0, 1), (1, 0)])


def sum_half(values, side):
    half = values.shape[0] // 2
    halves = values.reshape(2, half, values.shape[1])
    other = lax.dynamic_index_in_dim(halves, 1 - side, 0, keepdims=False).astype(jnp.bfloat16)
    own = lax.dynamic_index_in_dim(halves, side, 0, keepdims=False)
    return own + swap_half(other).astype(jnp.float32)


def join_halves(own, side):
    other = swap_half(own)
    first = jnp.where(side == 0, own, other)
    second = jnp.where(side == 0, other, own)
    return jnp.concatenate([first, second], axis=0)


def row_stat(values):
    return values + lax.ppermute(values, "tensor", [(0, 1), (1, 0)])


def decay_mask(segment, decays, offset, height):
    length = segment.shape[0]
    rows_at = offset + jnp.arange(height)
    cols_at = jnp.arange(length)
    distance = rows_at[:, None] - cols_at[None, :]
    same_doc = segment[offset : offset + height][:, None] == segment[None, :]
    allowed = (distance >= 0) & same_doc
    falloff = jnp.exp(-decays[:, None, None] * jnp.maximum(distance, 0).astype(jnp.float32)[None])
    return jnp.where(allowed[None], falloff, jnp.float32(0.0))


def forward_heads(queries, key_rows, value_rows, segments, decays):
    length = segments.shape[1]
    height = min(512, length)

    def forward_one_sequence(entries):
        seq_query, seq_key, seq_value, segment = entries
        outputs = []
        for offset in range(0, length, height):
            masking = decay_mask(segment, decays, offset, height)
            scores = jnp.einsum(
                "qhd,khd->hqk",
                seq_query[offset : offset + height],
                seq_key,
                preferred_element_type=jnp.float32,
            )
            weighted = (scores * masking).astype(jnp.bfloat16)
            outputs.append(
                jnp.einsum("hqk,khd->qhd", weighted, seq_value, preferred_element_type=jnp.float32)
            )
        return jnp.concatenate(outputs, axis=0)

    return lax.map(forward_one_sequence, (queries, key_rows, value_rows, segments))


def backward_heads(queries, key_rows, value_rows, segments, grad_heads, decays):
    length = segments.shape[1]
    height = min(512, length)

    def backward_one_sequence(entries):
        seq_query, seq_key, seq_value, segment, seq_grad = entries
        grad_key = jnp.zeros(seq_key.shape, jnp.float32)
        grad_value = jnp.zeros(seq_value.shape, jnp.float32)
        grad_parts = []
        for offset in range(0, length, height):
            masking = decay_mask(segment, decays, offset, height)
            rows_query = seq_query[offset : offset + height]
            rows_grad = seq_grad[offset : offset + height]
            scores = jnp.einsum(
                "qhd,khd->hqk", rows_query, seq_key, preferred_element_type=jnp.float32
            )
            weighted = (scores * masking).astype(jnp.bfloat16)
            grad_weighted = jnp.einsum(
                "qhd,khd->hqk", rows_grad, seq_value, preferred_element_type=jnp.float32
            )
            grad_scores = (grad_weighted * masking).astype(jnp.bfloat16)
            grad_parts.append(
                jnp.einsum("hqk,khd->qhd", grad_scores, seq_key, preferred_element_type=jnp.float32)
            )
            grad_key = grad_key + jnp.einsum(
                "hqk,qhd->khd", grad_scores, rows_query, preferred_element_type=jnp.float32
            )
            grad_value = grad_value + jnp.einsum(
                "hqk,qhd->khd", weighted, rows_grad, preferred_element_type=jnp.float32
            )
        return (jnp.concatenate(grad_parts, axis=0), grad_key, grad_value)

    return lax.map(backward_one_sequence, (queries, key_rows, value_rows, segments, grad_heads))


def local(
    tokens,
    segment_ids,
    decay_rate,
    query_weight,
    key_weight,
    value_weight,
    gate_weight,
    output_weight,
    norm_gain,
    left_weight,
    right_weight,
    down_weight,
    cotangent,
):
    seq_count, length = segment_ids.shape
    local_heads, head_size = norm_gain.shape
    rows_total = tokens.shape[0]
    inner_width = local_heads * head_size
    full_inner = inner_width * lax.axis_size("tensor")
    gain_flat = norm_gain.astype(jnp.float32).reshape(inner_width)

    def by_head(values):
        return values.reshape(seq_count, length, local_heads, head_size)

    source = tokens.astype(jnp.float32)
    scale_in = rms_scale(source)
    normed = (source * scale_in).astype(jnp.bfloat16)
    pre_query = product(normed, query_weight)
    pre_key = product(normed, key_weight)
    queries = jax.nn.silu(pre_query).astype(jnp.bfloat16)
    key_rows = jax.nn.silu(pre_key).astype(jnp.bfloat16)
    value_rows = product(normed, value_weight).astype(jnp.bfloat16)
    gate_act = product(normed, gate_weight)
    heads_out = forward_heads(
        by_head(queries), by_head(key_rows), by_head(value_rows), segment_ids, decay_rate
    ).reshape(rows_total, inner_width)
    square_total = row_stat(jnp.sum(heads_out * heads_out, axis=1))
    scale_out = lax.rsqrt(square_total / full_inner + eps)[:, None]
    normed_heads = heads_out * scale_out
    scaled_heads = normed_heads * gain_flat
    mixed = (scaled_heads * gate_act).astype(jnp.bfloat16)
    side = lax.axis_index("tensor")
    half_rows = rows_total // 2

    def own_half(values):
        return lax.dynamic_slice_in_dim(values, side * half_rows, half_rows, 0)

    attn_part = product(mixed, output_weight)
    hidden = own_half(tokens).astype(jnp.float32) + sum_half(attn_part, side)
    scale_mid = rms_scale(hidden)
    lifted_own = (hidden * scale_mid).astype(jnp.bfloat16)
    lifted = join_halves(lifted_own, side)
    left_act = product(lifted, left_weight)
    right_act = product(lifted, right_weight)
    joined = (left_act * right_act).astype(jnp.bfloat16)
    grad_joined = product_nt(cotangent, down_weight)
    grad_left = (grad_joined * right_act).astype(jnp.bfloat16)
    grad_right = (grad_joined * left_act).astype(jnp.bfloat16)
    lifted_part = product_nt(grad_left, left_weight) + product_nt(grad_right, right_weight)
    grad_lifted = sum_half(lifted_part, side)
    down_part = product(joined, down_weight)
    block_out = join_halves((hidden + sum_half(down_part, side)).astype(jnp.bfloat16), side)
    down_grad = product_tn(cotangent, joined)
    left_grad = product_tn(lifted, grad_left)
    right_grad = product_tn(lifted, grad_right)
    ffn_total = lax.psum_scatter(
        jnp.concatenate([left_grad, right_grad, down_grad], axis=1).astype(jnp.bfloat16),
        "dp", scatter_dimension=0, tiled=True,
    ).astype(jnp.float32)
    grad_hidden = own_half(cotangent).astype(jnp.float32) + rms_back(hidden, scale_mid, grad_lifted)
    grad_low = join_halves(grad_hidden.astype(jnp.bfloat16), side)
    output_grad = product_tn(grad_low, mixed)
    grad_mixed = product_nt(grad_low, output_weight)
    grad_scaled = grad_mixed * gate_act
    grad_gate = (grad_mixed * scaled_heads).astype(jnp.bfloat16)
    gain_grad = jnp.sum(grad_scaled * normed_heads, axis=0).reshape(local_heads, head_size)
    grad_normed = grad_scaled * gain_flat
    cross_total = row_stat(jnp.sum(heads_out * grad_normed, axis=1))[:, None]
    grad_heads = (
        scale_out * grad_normed
        - heads_out * (scale_out * scale_out * scale_out) * (cross_total / full_inner)
    ).astype(jnp.bfloat16)
    grad_query, grad_key, grad_value = backward_heads(
        by_head(queries),
        by_head(key_rows),
        by_head(value_rows),
        segment_ids,
        by_head(grad_heads),
        decay_rate,
    )
    query_pull = (grad_query.reshape(rows_total, inner_width) * silu_slope(pre_query)).astype(
        jnp.bfloat16
    )
    key_pull = (grad_key.reshape(rows_total, inner_width) * silu_slope(pre_key)).astype(
        jnp.bfloat16
    )
    value_pull = grad_value.reshape(rows_total, inner_width).astype(jnp.bfloat16)
    query_grad = product_tn(normed, query_pull)
    key_grad = product_tn(normed, key_pull)
    value_grad = product_tn(normed, value_pull)
    gate_grad = product_tn(normed, grad_gate)
    normed_part = (
        product_nt(query_pull, query_weight)
        + product_nt(key_pull, key_weight)
        + product_nt(value_pull, value_weight)
        + product_nt(grad_gate, gate_weight)
    )
    tokens_own = grad_hidden + rms_back(own_half(source), own_half(scale_in), sum_half(normed_part, side))
    tokens_grad = join_halves(tokens_own.astype(jnp.bfloat16), side).astype(jnp.float32)
    dp = lax.axis_size("dp")
    gain_rows = gain_grad.reshape(local_heads, dp, head_size // dp).transpose(1, 0, 2).reshape(dp, -1)
    gain_rows = jnp.pad(gain_rows, ((0, 0), (0, query_grad.shape[0] // dp - gain_rows.shape[1])))
    gain_block = jnp.pad(gain_rows.reshape(-1, 1), ((0, 0), (0, 127)))
    attn_total = lax.psum_scatter(
        jnp.concatenate(
            [query_grad, key_grad, value_grad, gate_grad, output_grad, gain_block], axis=1
        ).astype(jnp.bfloat16),
        "dp", scatter_dimension=0, tiled=True,
    ).astype(jnp.float32)
    query_total, key_total, value_total, gate_total, output_turned = (
        attn_total[:, at * inner_width : (at + 1) * inner_width] for at in range(5)
    )
    output_total = output_turned.T
    width = head_size // dp
    gain_total = attn_total[: local_heads * width, 5 * inner_width].reshape(local_heads, width)
    units = left_weight.shape[1]
    left_total, right_total = ffn_total[:, :units], ffn_total[:, units : 2 * units]
    down_total = ffn_total[:, 2 * units :].T
    return (
        block_out,
        tokens_grad,
        query_total,
        key_total,
        value_total,
        gate_total,
        output_total,
        gain_total,
        left_total,
        right_total,
        down_total,
    )


def solution(mesh):
    in_specs = (
        P("dp", None),
        P("dp", None),
        P("tensor"),
        P(None, "tensor"),
        P(None, "tensor"),
        P(None, "tensor"),
        P(None, "tensor"),
        P("tensor", None),
        P("tensor", None),
        P(None, "tensor"),
        P(None, "tensor"),
        P("tensor", None),
        P("dp", None),
    )
    out_specs = (
        P("dp", None),
        P("dp", None),
        P("dp", "tensor"),
        P("dp", "tensor"),
        P("dp", "tensor"),
        P("dp", "tensor"),
        P("tensor", "dp"),
        P("tensor", "dp"),
        P("dp", "tensor"),
        P("dp", "tensor"),
        P("tensor", "dp"),
    )
    return jax.shard_map(local, mesh=mesh, in_specs=in_specs, out_specs=out_specs, check_vma=False)
```

```python
import functools

import jax
import jax.numpy as jnp
from jax import lax
from jax.experimental import pallas as pl
from jax.experimental.pallas import tpu as pltpu
from jax.sharding import PartitionSpec as P

MESH = pl.DeviceIdType.MESH
eps = 1e-06
BAND = 384
BLOCK = 256
SPAN = BAND + BLOCK
F32 = jnp.float32
BF16 = jnp.bfloat16
VMEM_LIMIT = 62 * 1024 * 1024


def nn(left_op, right_op):
    return jnp.dot(left_op, right_op, preferred_element_type=F32)


def nt(left_op, right_op):
    return lax.dot_general(
        left_op, right_op, (((1,), (1,)), ((), ())), preferred_element_type=F32
    )


def at(start):
    return pl.ds(pl.multiple_of(start, BLOCK), BLOCK)


def rms_scale(values):
    return lax.rsqrt(jnp.mean(values * values, axis=1, keepdims=True) + eps)


def rms_back(values, scale, grads):
    return scale * grads - values * (scale * scale * scale) * jnp.mean(
        values * grads, axis=1, keepdims=True
    )


def eye():
    shape = (128, 128)
    return lax.broadcasted_iota(jnp.int32, shape, 0) == lax.broadcasted_iota(jnp.int32, shape, 1)


def to_column(rows):
    parts = [
        jnp.sum(jnp.where(eye(), rows[i : i + 1, :], 0.0), axis=1, keepdims=True)
        for i in range(rows.shape[0])
    ]
    return jnp.concatenate(parts, axis=0)


def to_rows(column):
    parts = [
        jnp.sum(jnp.where(eye(), column[i : i + 128, :], 0.0), axis=0, keepdims=True)
        for i in range(0, column.shape[0], 128)
    ]
    return jnp.concatenate(parts, axis=0)


def iota_f32(shape, axis):
    return lax.broadcasted_iota(jnp.int32, shape, axis).astype(F32)


def attend(
    seg_ref, decay_ref, tok_ref, wq_ref, wk_ref, wv_ref, wg_ref, gain_ref,
    u_ref, heads_ref, gate_ref, q_ref, k_ref, v_ref, sq_ref, sk_ref, sums_ref,
    k_all, v_all,
):
    step = pl.program_id(0)
    width = q_ref.shape[1]

    @pl.when(step == 0)
    def _():
        k_all[:BAND, :] = jnp.zeros((BAND, width), BF16)
        v_all[:BAND, :] = jnp.zeros((BAND, width), BF16)

    source = tok_ref[...].astype(F32)
    normed = (source * rms_scale(source)).astype(BF16)
    pre = nn(normed, wk_ref[...])
    sigma = jax.nn.sigmoid(pre)
    key_rows = (pre * sigma).astype(BF16)
    sk_ref[...] = (sigma * (1.0 + pre * (1.0 - sigma))).astype(BF16)
    k_ref[...] = key_rows
    here = pl.ds(pl.multiple_of(BAND + step * BLOCK, 128), BLOCK)
    k_all[here, :] = key_rows
    value_rows = nn(normed, wv_ref[...]).astype(BF16)
    v_ref[...] = value_rows
    v_all[here, :] = value_rows
    pre = nn(normed, wq_ref[...])
    sigma = jax.nn.sigmoid(pre)
    queries = (pre * sigma).astype(BF16)
    sq_ref[...] = (sigma * (1.0 + pre * (1.0 - sigma))).astype(BF16)
    q_ref[...] = queries
    gate = nn(normed, wg_ref[...])
    gate_ref[...] = gate.astype(BF16)

    span = pl.ds(pl.multiple_of(step * BLOCK, BLOCK), SPAN)
    seg_keys = seg_ref[0:1, span]
    seg_rows = to_column(
        jnp.concatenate(
            [
                seg_ref[0:1, pl.ds(pl.multiple_of(BAND + step * BLOCK + i, 128), 128)]
                for i in range(0, BLOCK, 128)
            ],
            axis=0,
        )
    )
    row_at = iota_f32((BLOCK, 1), 0)
    key_at = iota_f32((1, SPAN), 1) - float(BAND)
    allowed = (seg_rows == seg_keys) & (row_at >= key_at)
    total = jnp.zeros((BLOCK, 1), F32)
    for head in range(width // 128):
        lanes = slice(head * 128, head * 128 + 128)
        decay = decay_ref[head]
        scores = nt(queries[:, lanes], k_all[span, lanes])
        falloff = jnp.exp(-decay * row_at) * jnp.exp(decay * key_at)
        weighted = jnp.where(allowed, scores * falloff, 0.0).astype(BF16)
        heads = nn(weighted, v_all[span, lanes])
        total = total + jnp.sum(heads * heads, axis=1, keepdims=True)
        heads_ref[:, lanes] = heads.astype(BF16)
        u_ref[:, lanes] = (heads * gain_ref[0:1, lanes] * gate[:, lanes]).astype(BF16)
    for part in range(BLOCK // 128):
        sums_ref[pl.ds(step * (BLOCK // 128) + part, 1), :] = to_rows(
            total[part * 128 : part * 128 + 128, :]
        )


def run_attend(segments, decays, tokens, wq, wk, wv, wg, gain):
    rows, features = tokens.shape
    width = wq.shape[1]
    whole = lambda *shape: pl.BlockSpec(shape, lambda i: (0,) * len(shape))
    block = lambda columns: pl.BlockSpec((BLOCK, columns), lambda i: (i, 0))
    return pl.pallas_call(
        attend,
        grid=(rows // BLOCK,),
        in_specs=[
            whole(*segments.shape),
            pl.BlockSpec(memory_space=pltpu.SMEM),
            block(features),
            whole(features, width), whole(features, width), whole(features, width), whole(features, width),
            whole(1, width),
        ],
        out_specs=[block(width)] * 8 + [whole(rows // 128, 128)],
        out_shape=[jax.ShapeDtypeStruct((rows, width), BF16)] * 8
        + [jax.ShapeDtypeStruct((rows // 128, 128), F32)],
        scratch_shapes=[pltpu.VMEM((BAND + rows, width), BF16)] * 2,
        compiler_params=pltpu.CompilerParams(vmem_limit_bytes=VMEM_LIMIT),
        cost_estimate=pl.CostEstimate(flops=6 * 10**9, bytes_accessed=15 * 2**20, transcendentals=10**6),
        name="attend",
    )(segments, decays, tokens, wq, wk, wv, wg, gain)


def tiles(extent, most=512):
    return [(start, min(most, extent - start)) for start in range(0, extent, most)]


def rest(
    ways,
    seg_ref, decay_ref, sums_ref, gain_ref, tok, cot, u, wo, wo_part, wl, wr, wd, wq, wk, wv, wg,
    heads, gate, q, k, v, sq, sk,
    out_ref, tg_ref, ffn_ref, attn_ref, gain_out,
    lifted, u_in, wo_peer, sum_in, back_in, down_in, mixed_grad, cross, norm_in, turn_in,
    ffn_c, ffn_y, ffn_z, att_c, att_y, att_z, gain_in,
    u_own, wo_own, mixed_out, down_out, hidden, grad_hidden, scale_rows, core_out, gain_sum, turn_out,
    send, recv, dp_send, dp_recv, z_send, z_recv, local,
):
    dp, side = lax.axis_index("dp"), lax.axis_index("tensor")
    core, second, third = lax.rem(dp, 2), lax.rem(lax.div(dp, 2), 2), lax.div(dp, 4)
    rows, features = tok.shape
    width = wq.shape[1]
    units = wl.shape[1]
    half = rows // 2
    thirds = ways // 4
    share = features // ways
    full_inner = float(2 * width)
    own0, other0 = side * half, (1 - side) * half
    across = (dp, 1 - side)
    sibling = (dp + 1 - 2 * core, side)
    beside = (dp + 2 - 4 * second, side)

    def far(hop):
        return (lax.rem(third + hop, thirds) * 4 + second * 2 + core, side)

    def remote(source, target, send_sem, recv_sem, device):
        return pltpu.make_async_remote_copy(
            src_ref=source, dst_ref=target, send_sem=send_sem, recv_sem=recv_sem,
            device_id=device, device_id_type=MESH,
        )

    def over_x(index, source, target):
        return remote(source, target, send.at[index], recv.at[index], across)

    def load(index, source, target):
        copy = pltpu.make_async_copy(source, target, local.at[index])
        copy.start()
        return copy

    def put_turned(target, block, column):
        turned = jnp.transpose(block)
        for owner in range(ways):
            place = (owner % 2) * (ways // 2) + (owner // 2 % 2) * (ways // 4) + owner // 4
            target[place * share : (place + 1) * share, column] = turned[
                owner * share : (owner + 1) * share, :
            ]

    def chunk(part):
        return at(part * BLOCK)

    def u_copy(part):
        return over_x(part, u.at[at(other0 + part * BLOCK), :], u_in.at[chunk(part), :])

    def lifted_copy(part):
        place = lifted.at[at(own0 + part * BLOCK), :]
        return over_x(4 + part, place, place)

    def back_copy(source, part):
        return over_x(6 + part, source.at[chunk(part), :], back_in.at[chunk(part), :])

    def mixed_copy(part):
        return over_x(
            8 + part, mixed_out.at[chunk(part), :], mixed_grad.at[at(own0 + part * BLOCK), :]
        )

    def down_copy(part):
        return over_x(11 + part, down_out.at[chunk(part), :], down_in.at[chunk(part), :])

    def norm_copy(source, part):
        return over_x(13 + part, source.at[chunk(part), :], norm_in.at[chunk(part), :])

    def out_copy(source, part):
        return over_x(15 + part, source.at[chunk(part), :], out_ref.at[at(own0 + part * BLOCK), :])

    def tg_copy(source, part):
        return over_x(17 + part, source.at[chunk(part), :], tg_ref.at[at(own0 + part * BLOCK), :])

    def core_copy(first, block, landing, columns):
        return remote(
            core_out.at[:, pl.ds(0, columns)], landing.at[block],
            dp_send.at[0, first + block], dp_recv.at[0, first + block], sibling,
        )

    def second_copy(first, block, summed, landing):
        return remote(
            summed.at[block, at((1 - second) * BLOCK), :], landing.at[block],
            dp_send.at[1, first + block], dp_recv.at[1, first + block], beside,
        )

    def third_copy(first, block, hop, summed, landing):
        piece = pl.ds(pl.multiple_of(lax.rem(third + hop, thirds) * share, share), share)
        return remote(
            summed.at[block, piece, :], landing.at[block, hop - 1],
            z_send.at[first + block, hop - 1], z_recv.at[first + block, hop - 1], far(hop),
        )

    def stage_send(turned, grads, columns, copy):
        def one(part, carry):
            left_op = turned[at((1 - core) * 2 * BLOCK + part * BLOCK), :]
            for start, size in tiles(columns):
                core_out[chunk(part), start : start + size] = nn(
                    left_op, grads[:, start : start + size]
                ).astype(BF16)
            return carry

        lax.fori_loop(0, 2, one, 0)
        copy.start()

    def stage_core(turned, grads, columns, copy, landing, onward):
        copy.wait()

        def one(part, carry):
            left_op = turned[at(core * 2 * BLOCK + part * BLOCK), :]
            for start, size in tiles(columns):
                cut = slice(start, start + size)
                total = nn(left_op, grads[:, cut]) + landing[chunk(part), cut].astype(F32)
                landing[chunk(part), cut] = total.astype(BF16)
            return carry

        lax.fori_loop(0, 2, one, 0)
        onward.start()

    def stage_second(first, block, summed, landing, group_out):
        copy = second_copy(first, block, summed, landing)
        copy.wait()
        for start, size in tiles(landing.shape[2]):
            cut = slice(start, start + size)
            total = (
                summed[block, at(second * BLOCK), cut].astype(F32)
                + landing[block, :, cut].astype(F32)
            )
            landing[block, :, cut] = total.astype(BF16)
        for hop in range(1, thirds):
            third_copy(first, block, hop, landing, group_out).start()

    def stage_third(first, block, summed, landing):
        mine = pl.ds(pl.multiple_of(third * share, share), share)
        total = summed[block, mine, :].astype(F32)
        for hop in range(1, thirds):
            third_copy(first, block, hop, summed, landing).wait()
            total = total + landing[block, hop - 1].astype(F32)
        return total

    def gain_copy(stage, slot, device):
        return remote(
            gain_sum.at[stage], gain_in.at[slot], z_send.at[6, slot], z_recv.at[6, slot], device
        )

    barrier = pltpu.get_barrier_semaphore()
    partners = [across, sibling, beside] + [far(hop) for hop in range(1, thirds)]
    for device in partners:
        pl.semaphore_signal(barrier, inc=1, device_id=device, device_id_type=MESH)
    pl.semaphore_wait(barrier, len(partners))

    def middle(tok_own, cot_all, turned, w_left, w_right, w_down, hidden_units, back_out, low_turned, mixed):
        part_copy = load(1, wo_part, wo_peer.at[at(core * BLOCK), :])
        loads = [
            load(0, wo, wo_own),
            load(2, u.at[pl.ds(pl.multiple_of(own0, BLOCK), half), :], u_own),
            load(3, tok.at[pl.ds(pl.multiple_of(own0, BLOCK), half), :], tok_own),
            load(4, cot, cot_all),
        ]
        weights = [load(5, wl, w_left), load(6, wr, w_right), load(7, wd, w_down)]
        for part in range(2):
            u_copy(part).start()
        sum_copy = over_x(2, sums_ref, sum_in)
        sum_copy.start()
        part_copy.wait()
        quarter = wo_peer.at[at(core * BLOCK), :]
        quarter_copy = remote(quarter, quarter, send.at[3], recv.at[3], sibling)
        quarter_copy.start()
        for copy in loads:
            copy.wait()

        def own_heads(part, carry):
            grad_hidden[chunk(part), :] = nn(u_own[chunk(part), :], wo_own[...])
            return carry

        lax.fori_loop(0, 2, own_heads, 0)

        def turn(part, carry):
            put_turned(turned.at[1], cot_all[chunk(part), :], chunk(part))
            return carry

        lax.fori_loop(0, rows // BLOCK, turn, 0)
        quarter_copy.wait()
        sum_copy.wait()
        scale_rows[...] = lax.rsqrt((sums_ref[...] + sum_in[...]) / full_inner + eps)

        def scale_of(block):
            return to_column(
                jnp.concatenate(
                    [
                        scale_rows[pl.ds(block * (BLOCK // 128) + i, 1), :]
                        for i in range(BLOCK // 128)
                    ],
                    axis=0,
                )
            )

        def open_chunk(part, carry):
            u_copy(part).wait()
            scale = scale_of(side * (half // BLOCK) + part)
            from_peer = u_in[chunk(part), :]
            attn = grad_hidden[chunk(part), :] + nn(from_peer, wo_peer[...])
            state = tok_own[chunk(part), :].astype(F32) + scale * attn
            hidden[chunk(part), :] = state
            lifted[at(own0 + part * BLOCK), :] = (state * rms_scale(state)).astype(BF16)
            lifted_copy(part).start()
            mixed[chunk(part), :width] = (u_own[chunk(part), :].astype(F32) * scale).astype(BF16)
            mixed[chunk(part), width:] = (from_peer.astype(F32) * scale).astype(BF16)
            return carry

        lax.fori_loop(0, 2, open_chunk, 0)
        for copy in weights:
            copy.wait()

        def gated(step, carry):
            part = lax.rem(step, 2)
            place = at((side + lax.div(step, 2) * (1 - 2 * side)) * half + part * BLOCK)

            @pl.when(step >= 2)
            def _():
                lifted_copy(part).wait()

            rows_in = lifted[place, :]
            rows_cot = cot_all[place, :]
            for start, size in tiles(units):
                cut = slice(start, start + size)
                left = nn(rows_in, w_left[:, cut])
                right = nn(rows_in, w_right[:, cut])
                grad = nt(rows_cot, w_down[cut, :])
                hidden_units[2, place, cut] = (left * right).astype(BF16)
                hidden_units[0, place, cut] = (grad * right).astype(BF16)
                hidden_units[1, place, cut] = (grad * left).astype(BF16)
            back = nt(hidden_units[0, place, :], w_left[...]) + nt(
                hidden_units[1, place, :], w_right[...]
            )

            @pl.when(step < 2)
            def _():
                grad_hidden[chunk(part), :] = back

            @pl.when(step >= 2)
            def _():
                back_out[chunk(part), :] = back.astype(BF16)
                back_copy(back_out, part).start()

            put_turned(turned.at[0], rows_in, place)
            return carry

        lax.fori_loop(0, 4, gated, 0)

        def down_other(part, carry):
            down_out[chunk(part), :] = nn(
                hidden_units[2, at(other0 + part * BLOCK), :], w_down[...]
            ).astype(BF16)
            return carry

        lax.fori_loop(0, 2, down_other, 0)

        def block_step(block, carry):
            lhs, rhs = turned.at[lax.div(block, 2)], hidden_units.at[block]
            first = core_copy(0, block, ffn_c, units)
            stage_send(lhs, rhs, units, first)

            @pl.when(block < 2)
            def _():
                part = block
                back_copy(back_out, part).wait()
                state = hidden[chunk(part), :]
                pulled = grad_hidden[chunk(part), :] + back_in[chunk(part), :].astype(F32)
                grad = cot_all[at(own0 + part * BLOCK), :].astype(F32) + rms_back(
                    state, rms_scale(state), pulled
                )
                grad_hidden[chunk(part), :] = grad
                low = grad.astype(BF16)
                for_own = nt(low, wo_own[...])
                for_peer = nt(low, wo_peer[...])
                mixed_out[chunk(part), :] = for_peer.astype(BF16)
                mixed_grad[at(own0 + part * BLOCK), :] = for_own.astype(BF16)
                mixed_copy(part).start()
                both = jnp.sum(
                    u_own[chunk(part), :].astype(F32) * for_own
                    + u_in[chunk(part), :].astype(F32) * for_peer,
                    axis=1,
                    keepdims=True,
                )
                lanes = to_rows(both)
                for i in range(BLOCK // 128):
                    cross[side, pl.ds(part * (BLOCK // 128) + i, 1), :] = lanes[i : i + 1, :]
                put_turned(low_turned, low, chunk(part))

                @pl.when(part == 1)
                def _():
                    over_x(10, cross.at[side], cross.at[side]).start()

                down_copy(part).start()

            stage_core(
                lhs, rhs, units, first, ffn_c.at[block], second_copy(0, block, ffn_c, ffn_y)
            )
            return carry

        lax.fori_loop(0, 3, block_step, 0)

        def down_own(part, carry):
            hidden[chunk(part), :] += nn(
                hidden_units[2, at(own0 + part * BLOCK), :], w_down[...]
            )
            return carry

        lax.fori_loop(0, 2, down_own, 0)
        columns = 2 * width
        first = core_copy(3, 0, att_c, columns)
        stage_send(low_turned, mixed, columns, first)
        stage_core(low_turned, mixed, columns, first, att_c.at[0], second_copy(3, 0, att_c, att_y))

    pl.run_scoped(
        middle,
        pltpu.VMEM((half, features), BF16),
        pltpu.VMEM((rows, features), BF16),
        pltpu.VMEM((2, features, rows), BF16),
        pltpu.VMEM((features, units), BF16),
        pltpu.VMEM((features, units), BF16),
        pltpu.VMEM((units, features), BF16),
        pltpu.VMEM((3, rows, units), BF16),
        pltpu.VMEM((half, features), BF16),
        pltpu.VMEM((features, half), BF16),
        pltpu.VMEM((half, 2 * width), BF16),
    )

    def last(q_all, grads, k_all, v_all, slope_q, slope_k, heads_all, gate_all, pulls, weights, norm_out, norm_own, results, turned, tok_all):
        columns = 2 * width
        loads = [
            load(0, v, v_all.at[pl.ds(BAND, rows), :]),
            load(1, k, k_all.at[pl.ds(BAND, rows), :]),
            load(2, q, q_all.at[pl.ds(0, rows), :]),
            load(3, gate, gate_all),
            load(4, heads, heads_all),
            load(5, sq, slope_q),
            load(6, sk, slope_k),
        ]
        later = [load(7, tok, tok_all)] + [
            load(8 + i, source, weights.at[:, pl.ds(i * width, width)])
            for i, source in enumerate((wq, wk, wv, wg))
        ]
        for padded in (k_all, v_all):
            padded[:BAND, :] = jnp.zeros((BAND, width), BF16)
        for padded in (q_all, grads):
            padded[rows:, :] = jnp.zeros((BAND, width), BF16)
        gain_sum[0] = jnp.zeros(gain_sum.shape[1:], F32)
        for copy in loads:
            copy.wait()
        for part in range(2):
            mixed_copy(part).wait()
        over_x(10, cross.at[side], cross.at[side]).wait()

        def lane_rows(source, block):
            return to_column(
                jnp.concatenate(
                    [source(block * (BLOCK // 128) + i) for i in range(BLOCK // 128)], axis=0
                )
            )

        def prepare(block, carry):
            place = chunk(block)
            scale = lane_rows(lambda i: scale_rows[pl.ds(i, 1), :], block)
            per_half = half // 128
            joint = lane_rows(
                lambda i: cross[lax.div(i, per_half), pl.ds(lax.rem(i, per_half), 1), :], block
            )
            grad = mixed_grad[place, :].astype(F32)
            head_rows = heads_all[place, :].astype(F32)
            gain = gain_ref[0:1, :]
            scaled = grad * gate_all[place, :].astype(F32)
            unit = head_rows * scale
            gain_sum[0, 0:1, :] += jnp.sum(scaled * unit, axis=0, keepdims=True)
            pulls[1, place, width:] = (grad * (unit * gain)).astype(BF16)
            grads[place, :] = (
                scale * (scaled * gain)
                - head_rows * (scale * scale * scale) * (joint / full_inner)
            ).astype(BF16)
            return carry

        lax.fori_loop(0, rows // BLOCK, prepare, 0)
        gain_copy(0, 0, sibling).start()

        def seg_lanes(start, size):
            return seg_ref[0:1, pl.ds(pl.multiple_of(start, 128), size)]

        def seg_column(start):
            return to_column(
                jnp.concatenate([seg_lanes(start + i, 128) for i in range(0, BLOCK, 128)], axis=0)
            )

        def by_query(block, carry):
            place, span = chunk(block), pl.ds(pl.multiple_of(block * BLOCK, BLOCK), SPAN)
            row_at = iota_f32((BLOCK, 1), 0)
            key_at = iota_f32((1, SPAN), 1) - float(BAND)
            allowed = (seg_column(BAND + block * BLOCK) == seg_lanes(block * BLOCK, SPAN)) & (
                row_at >= key_at
            )
            for head in range(width // 128):
                lanes = slice(head * 128, head * 128 + 128)
                decay = decay_ref[head]
                falloff = jnp.exp(-decay * row_at) * jnp.exp(decay * key_at)
                grad = nt(grads[place, lanes], v_all[span, lanes])
                grad = jnp.where(allowed, grad * falloff, 0.0).astype(BF16)
                pulls[0, place, lanes] = (
                    nn(grad, k_all[span, lanes]) * slope_q[place, lanes].astype(F32)
                ).astype(BF16)
            return carry

        lax.fori_loop(0, rows // BLOCK, by_query, 0)

        def by_key(block, carry):
            place, span = chunk(block), pl.ds(pl.multiple_of(block * BLOCK, BLOCK), SPAN)
            here = pl.ds(pl.multiple_of(BAND + block * BLOCK, 128), BLOCK)
            key_at = iota_f32((BLOCK, 1), 0)
            row_at = iota_f32((1, SPAN), 1)
            allowed = (
                seg_column(BAND + block * BLOCK) == seg_lanes(BAND + block * BLOCK, SPAN)
            ) & (row_at >= key_at)
            for head in range(width // 128):
                lanes = slice(head * 128, head * 128 + 128)
                turned_lanes = slice(width + head * 128, width + head * 128 + 128)
                decay = decay_ref[head]
                falloff = jnp.exp(decay * key_at) * jnp.exp(-decay * row_at)
                span_q, span_grad = q_all[span, lanes], grads[span, lanes]
                scores = nt(k_all[here, lanes], span_q)
                weighted = jnp.where(allowed, scores * falloff, 0.0).astype(BF16)
                pulls[1, place, lanes] = nn(weighted, span_grad).astype(BF16)
                grad = nt(v_all[here, lanes], span_grad)
                grad = jnp.where(allowed, grad * falloff, 0.0).astype(BF16)
                pulls[0, place, turned_lanes] = (
                    nn(grad, span_q) * slope_k[place, lanes].astype(F32)
                ).astype(BF16)
            return carry

        lax.fori_loop(0, rows // BLOCK, by_key, 0)
        for copy in later:
            copy.wait()

        def normed_part(step, carry):
            part = lax.rem(step, 2)
            place = at((1 - side + lax.div(step, 2) * (2 * side - 1)) * half + part * BLOCK)
            back = nt(pulls[0, place, :], weights[:, :columns]) + nt(
                pulls[1, place, :], weights[:, columns:]
            )

            @pl.when(step < 2)
            def _():
                norm_out[chunk(part), :] = back.astype(BF16)
                norm_copy(norm_out, part).start()

            @pl.when(step >= 2)
            def _():
                norm_own[chunk(part), :] = back

            return carry

        lax.fori_loop(0, 4, normed_part, 0)

        def turn(block, carry):
            source = tok_all[chunk(block), :].astype(F32)
            put_turned(turned, (source * rms_scale(source)).astype(BF16), chunk(block))
            return carry

        lax.fori_loop(0, rows // BLOCK, turn, 0)

        gain_copy(0, 0, sibling).wait()
        gain_sum[1] = gain_sum[0] + gain_in[0]
        gain_copy(1, 1, beside).start()

        def block_step(step, carry):
            block = step + 1
            rhs = pulls.at[step]
            first = core_copy(3, block, att_c, columns)
            stage_send(turned, rhs, columns, first)
            stage_core(
                turned, rhs, columns, first, att_c.at[block], second_copy(3, block, att_c, att_y)
            )
            return carry

        lax.fori_loop(0, 2, block_step, 0)

        def seconds(block, carry):
            stage_second(0, block, ffn_c, ffn_y, ffn_z)
            return carry

        lax.fori_loop(0, 3, seconds, 0)

        def finish_out(part, carry):
            down_copy(part).wait()
            results[0, chunk(part), :] = (
                hidden[chunk(part), :] + down_in[chunk(part), :].astype(F32)
            ).astype(BF16)
            out_copy(results.at[0], part).start()
            pltpu.make_async_copy(
                results.at[0, chunk(part), :], out_ref.at[at(own0 + part * BLOCK), :], local.at[part]
            ).start()
            return carry

        lax.fori_loop(0, 2, finish_out, 0)
        gain_copy(1, 1, beside).wait()
        gain_sum[2] = gain_sum[1] + gain_in[1]
        for hop in range(1, thirds):
            gain_copy(2, 1 + hop, far(hop)).start()

        def finish_tokens(part, carry):
            norm_copy(norm_out, part).wait()
            pulled = norm_own[chunk(part), :] + norm_in[chunk(part), :].astype(F32)
            source = tok_all[at(own0 + part * BLOCK), :].astype(F32)
            results[1, chunk(part), :] = (
                grad_hidden[chunk(part), :] + rms_back(source, rms_scale(source), pulled)
            ).astype(BF16)
            tg_copy(results.at[1], part).start()
            pltpu.make_async_copy(
                results.at[1, chunk(part), :], tg_ref.at[at(own0 + part * BLOCK), :], local.at[2 + part]
            ).start()
            return carry

        lax.fori_loop(0, 2, finish_tokens, 0)

        def seconds_last(block, carry):
            stage_second(3, block, att_c, att_y, att_z)
            return carry

        lax.fori_loop(0, 3, seconds_last, 0)

        def ffn_total(block, carry):
            ffn_ref[block] = stage_third(0, block, ffn_y, ffn_z)
            return carry

        lax.fori_loop(0, 3, ffn_total, 0)

        def attn_total(block, carry):
            attn_ref[block] = stage_third(3, block, att_y, att_z)
            return carry

        lax.fori_loop(0, 1, attn_total, 0)
        turn_out[...] = attn_ref[0, :, width:]
        turn_copy = over_x(19, turn_out, turn_in)
        turn_copy.start()
        lax.fori_loop(1, 3, attn_total, 0)
        total = gain_sum[2]
        for hop in range(1, thirds):
            gain_copy(2, 1 + hop, far(hop)).wait()
            total = total + gain_in[1 + hop]
        gain_out[...] = total
        turn_copy.wait()
        attn_ref[0, :, :width] += turn_in[...]

        def close(part, carry):
            out_copy(results.at[0], part).wait()
            tg_copy(results.at[1], part).wait()
            for index, target in ((0, out_ref), (1, tg_ref)):
                pltpu.make_async_copy(
                    results.at[index, chunk(part), :],
                    target.at[at(own0 + part * BLOCK), :],
                    local.at[2 * index + part],
                ).wait()
            return carry

        lax.fori_loop(0, 2, close, 0)

    pl.run_scoped(
        last,
        pltpu.VMEM((rows + BAND, width), BF16),
        pltpu.VMEM((rows + BAND, width), BF16),
        pltpu.VMEM((rows + BAND, width), BF16),
        pltpu.VMEM((rows + BAND, width), BF16),
        pltpu.VMEM((rows, width), BF16),
        pltpu.VMEM((rows, width), BF16),
        pltpu.VMEM((rows, width), BF16),
        pltpu.VMEM((rows, width), BF16),
        pltpu.VMEM((2, rows, 2 * width), BF16),
        pltpu.VMEM((features, 4 * width), BF16),
        pltpu.VMEM((half, features), BF16),
        pltpu.VMEM((half, features), F32),
        pltpu.VMEM((2, half, features), BF16),
        pltpu.VMEM((features, rows), BF16),
        pltpu.VMEM((rows, features), BF16),
    )


def run_rest(ways, *args):
    (seg, decays, sums, gain, tok, cot, u, wo, wo_part, wl) = args[:10]
    rows, features = tok.shape
    width, units = u.shape[1], wl.shape[1]
    half, thirds, share = rows // 2, ways // 4, features // ways
    quarter = features // 4
    vmem = pl.BlockSpec(memory_space=pltpu.VMEM)
    hbm = pl.BlockSpec(memory_space=pl.ANY)
    shape = jax.ShapeDtypeStruct
    scratch = [
        ((rows, features), BF16), ((half, width), BF16), ((width, features), BF16),
        (sums.shape, F32), ((half, features), BF16), ((half, features), BF16),
        ((rows, width), BF16), ((2, 8, 128), F32), ((half, features), BF16), ((share, width), F32),
        ((3, 2 * quarter, units), BF16), ((3, quarter, units), BF16),
        ((3, thirds - 1, share, units), BF16),
        ((3, 2 * quarter, 2 * width), BF16), ((3, quarter, 2 * width), BF16),
        ((3, thirds - 1, share, 2 * width), BF16), ((thirds + 1, 8, width), F32),
        ((half, width), BF16), ((width, features), BF16), ((half, width), BF16),
        ((half, features), BF16), ((half, features), F32), ((half, features), F32),
        (sums.shape, F32), ((2 * quarter, max(units, 2 * width)), BF16), ((3, 8, width), F32),
        ((share, width), F32),
    ]
    return pl.pallas_call(
        functools.partial(rest, ways),
        in_specs=[vmem, pl.BlockSpec(memory_space=pltpu.SMEM), vmem, vmem] + [hbm] * (len(args) - 4),
        out_specs=[hbm, hbm, vmem, vmem, vmem],
        out_shape=[
            shape((rows, features), BF16), shape((rows, features), BF16),
            shape((3, share, units), F32), shape((3, share, 2 * width), F32), shape((8, width), F32),
        ],
        scratch_shapes=[pltpu.VMEM(size, dtype) for size, dtype in scratch]
        + [
            pltpu.SemaphoreType.DMA((20,)), pltpu.SemaphoreType.DMA((20,)),
            pltpu.SemaphoreType.DMA((2, 6)), pltpu.SemaphoreType.DMA((2, 6)),
            pltpu.SemaphoreType.DMA((7, thirds + 1)), pltpu.SemaphoreType.DMA((7, thirds + 1)),
            pltpu.SemaphoreType.DMA((12,)),
        ],
        compiler_params=pltpu.CompilerParams(
            collective_id=1, has_side_effects=True, vmem_limit_bytes=VMEM_LIMIT
        ),
        cost_estimate=pl.CostEstimate(flops=5 * 10**10, bytes_accessed=60 * 2**20, transcendentals=10**6),
        name="rest",
    )(*args)


def local(
    ways, tokens, segment_ids, decay_rate, query_weight, key_weight, value_weight, gate_weight,
    output_weight, norm_gain, left_weight, right_weight, down_weight, cotangent,
):
    heads_here, head_size = norm_gain.shape
    width = heads_here * head_size
    gain = norm_gain.astype(F32).reshape(1, width)
    segments = jnp.pad(
        segment_ids.astype(F32).reshape(1, -1), ((0, 0), (BAND, BAND)), constant_values=-1.0
    )
    core = lax.rem(lax.axis_index("dp"), 2)
    part = lax.dynamic_slice_in_dim(output_weight, core * (width // 2), width // 2, 0)
    part = lax.ppermute(part, "tensor", [(0, 1), (1, 0)])
    u, heads, gate, q, k, v, sq, sk, sums = run_attend(
        segments, decay_rate, tokens, query_weight, key_weight, value_weight, gate_weight, gain
    )
    block_out, tokens_grad, ffn, attn, gain_total = run_rest(
        ways, segments, decay_rate, sums, gain, tokens, cotangent, u, output_weight, part,
        left_weight, right_weight, down_weight, query_weight, key_weight, value_weight, gate_weight,
        heads, gate, q, k, v, sq, sk,
    )
    each = head_size // ways
    gain_grad = lax.dynamic_slice_in_dim(
        gain_total[0].reshape(heads_here, head_size), lax.axis_index("dp") * each, each, 1
    )
    return (
        block_out,
        tokens_grad.astype(F32),
        attn[1, :, :width],
        attn[1, :, width:],
        attn[2, :, :width],
        attn[2, :, width:],
        attn[0, :, :width].T,
        gain_grad,
        ffn[0],
        ffn[1],
        ffn[2].T,
    )


def solution(mesh):
    dp, tensor = "dp", "tensor"
    in_specs = (
        P(dp, None), P(dp, None), P(tensor), P(None, tensor), P(None, tensor), P(None, tensor),
        P(None, tensor), P(tensor, None), P(tensor, None), P(None, tensor), P(None, tensor),
        P(tensor, None), P(dp, None),
    )
    out_specs = (
        P(dp, None), P(dp, None), P(dp, tensor), P(dp, tensor), P(dp, tensor), P(dp, tensor),
        P(tensor, dp), P(tensor, dp), P(dp, tensor), P(dp, tensor), P(tensor, dp),
    )
    return jax.shard_map(
        functools.partial(local, mesh.shape[dp]),
        mesh=mesh, in_specs=in_specs, out_specs=out_specs, check_vma=False,
    )
```

```python
import functools

import jax
import jax.numpy as jnp
from jax import lax
from jax.experimental import pallas as pl
from jax.experimental.pallas import tpu as pltpu
from jax.sharding import PartitionSpec as P

MESH = pl.DeviceIdType.MESH
eps = 1e-06
BAND = 384
BLOCK = 256
SPAN = BAND + BLOCK
F32 = jnp.float32
BF16 = jnp.bfloat16
VMEM_LIMIT = 62 * 1024 * 1024


def nn(left_op, right_op):
    return jnp.dot(left_op, right_op, preferred_element_type=F32)


def nt(left_op, right_op):
    return lax.dot_general(
        left_op, right_op, (((1,), (1,)), ((), ())), preferred_element_type=F32
    )


def at(start):
    return pl.ds(pl.multiple_of(start, BLOCK), BLOCK)


def rms_scale(values):
    return lax.rsqrt(jnp.mean(values * values, axis=1, keepdims=True) + eps)


def rms_back(values, scale, grads):
    return scale * grads - values * (scale * scale * scale) * jnp.mean(
        values * grads, axis=1, keepdims=True
    )


def eye():
    shape = (128, 128)
    return lax.broadcasted_iota(jnp.int32, shape, 0) == lax.broadcasted_iota(jnp.int32, shape, 1)


def to_column(rows):
    parts = [
        jnp.sum(jnp.where(eye(), rows[i : i + 1, :], 0.0), axis=1, keepdims=True)
        for i in range(rows.shape[0])
    ]
    return jnp.concatenate(parts, axis=0)


def to_rows(column):
    parts = [
        jnp.sum(jnp.where(eye(), column[i : i + 128, :], 0.0), axis=0, keepdims=True)
        for i in range(0, column.shape[0], 128)
    ]
    return jnp.concatenate(parts, axis=0)


def iota_f32(shape, axis):
    return lax.broadcasted_iota(jnp.int32, shape, axis).astype(F32)


def tiles(extent, most=512):
    return [(start, min(most, extent - start)) for start in range(0, extent, most)]


def layer(
    ways,
    ids_ref, decay_ref, gain_ref, tok, cot, wo, wl, wr, wd, wq, wk, wv, wg,
    out_ref, tg_ref, ffn_ref, attn_ref, gain_out,
    q, k, v, gate, heads, sq, sk,
    u_in, wo_peer, sum_in, back_in, down_in, mixed_grad, cross, norm_in, turn_in,
    ffn_c, ffn_y, ffn_z, att_c, att_y, att_z, gain_in,
    seg_ref, sums_ref, u_all, wo_own, mixed_out, down_out, hidden, grad_hidden, scale_rows, core_out, gain_sum, turn_out,
    send, recv, dp_send, dp_recv, z_send, z_recv, local, kept,
):
    dp, side = lax.axis_index("dp"), lax.axis_index("tensor")
    core, second, third = lax.rem(dp, 2), lax.rem(lax.div(dp, 2), 2), lax.div(dp, 4)
    rows, features = tok.shape
    width = wq.shape[1]
    units = wl.shape[1]
    half = rows // 2
    thirds = ways // 4
    share = features // ways
    full_inner = float(2 * width)
    own0, other0 = side * half, (1 - side) * half
    across = (dp, 1 - side)
    sibling = (dp + 1 - 2 * core, side)
    beside = (dp + 2 - 4 * second, side)

    def far(hop):
        return (lax.rem(third + hop, thirds) * 4 + second * 2 + core, side)

    def remote(source, target, send_sem, recv_sem, device):
        return pltpu.make_async_remote_copy(
            src_ref=source, dst_ref=target, send_sem=send_sem, recv_sem=recv_sem,
            device_id=device, device_id_type=MESH,
        )

    def over_x(index, source, target):
        return remote(source, target, send.at[index], recv.at[index], across)

    def load(index, source, target):
        copy = pltpu.make_async_copy(source, target, local.at[index])
        copy.start()
        return copy

    def put_turned(target, block, column):
        turned = jnp.transpose(block)
        for owner in range(ways):
            place = (owner % 2) * (ways // 2) + (owner // 2 % 2) * (ways // 4) + owner // 4
            target[place * share : (place + 1) * share, column] = turned[
                owner * share : (owner + 1) * share, :
            ]

    def chunk(part):
        return at(part * BLOCK)

    def u_copy(block):
        return over_x(block, u_all.at[chunk(block), :], u_in.at[chunk(block), :])

    def sum_copy(block):
        return over_x(4 + block, sums_ref.at[block], sum_in.at[block])

    def back_copy(source, part):
        return over_x(11 + part, source.at[chunk(part), :], back_in.at[chunk(part), :])

    def mixed_copy(part):
        return over_x(
            13 + part, mixed_out.at[chunk(part), :], mixed_grad.at[at(own0 + part * BLOCK), :]
        )

    def cross_copy(part):
        mine = cross.at[side * 2 + part]
        return over_x(15 + part, mine, mine)

    def down_copy(part):
        return over_x(17 + part, down_out.at[chunk(part), :], down_in.at[chunk(part), :])

    def norm_copy(source, part):
        return over_x(19 + part, source.at[chunk(part), :], norm_in.at[chunk(part), :])

    def out_copy(source, part):
        return over_x(21 + part, source.at[chunk(part), :], out_ref.at[at(own0 + part * BLOCK), :])

    def tg_copy(source, part):
        return over_x(23 + part, source.at[chunk(part), :], tg_ref.at[at(own0 + part * BLOCK), :])

    slice_rows = width // 4
    wo_start = core * (2 * slice_rows) + second * slice_rows
    wo_piece = pl.ds(pl.multiple_of(wo_start, slice_rows), slice_rows)

    def wo_across():
        return over_x(8, wo.at[wo_piece, :], wo_peer.at[wo_piece, :])

    def wo_beside():
        piece = wo_peer.at[wo_piece, :]
        return remote(piece, piece, send.at[9], recv.at[9], beside)

    def wo_sibling():
        piece = wo_peer.at[pl.ds(pl.multiple_of(core * (2 * slice_rows), 2 * slice_rows), 2 * slice_rows), :]
        return remote(piece, piece, send.at[10], recv.at[10], sibling)

    def core_copy(first, block, landing, columns):
        return remote(
            core_out.at[:, pl.ds(0, columns)], landing.at[block],
            dp_send.at[0, first + block], dp_recv.at[0, first + block], sibling,
        )

    def second_copy(first, block, summed, landing):
        return remote(
            summed.at[block, at((1 - second) * BLOCK), :], landing.at[block],
            dp_send.at[1, first + block], dp_recv.at[1, first + block], beside,
        )

    def third_copy(first, block, hop, summed, landing):
        piece = pl.ds(pl.multiple_of(lax.rem(third + hop, thirds) * share, share), share)
        return remote(
            summed.at[block, piece, :], landing.at[block, hop - 1],
            z_send.at[first + block, hop - 1], z_recv.at[first + block, hop - 1], far(hop),
        )

    def stage_send(turned, grads, columns, copy):
        def one(part, carry):
            left_op = turned[at((1 - core) * 2 * BLOCK + part * BLOCK), :]
            for start, size in tiles(columns):
                core_out[chunk(part), start : start + size] = nn(
                    left_op, grads[:, start : start + size]
                ).astype(BF16)
            return carry

        lax.fori_loop(0, 2, one, 0)
        copy.start()

    def stage_core(turned, grads, columns, copy, landing, onward):
        copy.wait()

        def one(part, carry):
            left_op = turned[at(core * 2 * BLOCK + part * BLOCK), :]
            for start, size in tiles(columns):
                cut = slice(start, start + size)
                total = nn(left_op, grads[:, cut]) + landing[chunk(part), cut].astype(F32)
                landing[chunk(part), cut] = total.astype(BF16)
            return carry

        lax.fori_loop(0, 2, one, 0)
        onward.start()

    def stage_second(first, block, summed, landing, group_out):
        copy = second_copy(first, block, summed, landing)
        copy.wait()
        for start, size in tiles(landing.shape[2]):
            cut = slice(start, start + size)
            total = (
                summed[block, at(second * BLOCK), cut].astype(F32)
                + landing[block, :, cut].astype(F32)
            )
            landing[block, :, cut] = total.astype(BF16)
        for hop in range(1, thirds):
            third_copy(first, block, hop, landing, group_out).start()

    def stage_third(first, block, summed, landing):
        mine = pl.ds(pl.multiple_of(third * share, share), share)
        total = summed[block, mine, :].astype(F32)
        for hop in range(1, thirds):
            third_copy(first, block, hop, summed, landing).wait()
            total = total + landing[block, hop - 1].astype(F32)
        return total

    def gain_copy(stage, slot, device):
        return remote(
            gain_sum.at[stage], gain_in.at[slot], z_send.at[6, slot], z_recv.at[6, slot], device
        )

    barrier = pltpu.get_barrier_semaphore()
    partners = [across, sibling, beside] + [far(hop) for hop in range(1, thirds)]
    for device in partners:
        pl.semaphore_signal(barrier, inc=1, device_id=device, device_id_type=MESH)

    def seg_lanes(start, size):
        return seg_ref[0:1, pl.ds(pl.multiple_of(start, 128), size)]

    def seg_column(start):
        return to_column(
            jnp.concatenate([seg_lanes(start + i, 128) for i in range(0, BLOCK, 128)], axis=0)
        )

    def gain_lanes(head):
        return gain_ref[head : head + 1, :].astype(F32)

    blocks = rows // BLOCK
    lanes_in = BLOCK // 128

    def lane_column(source, block):
        return to_column(
            jnp.concatenate([source[block, i : i + 1, :] for i in range(lanes_in)], axis=0)
        )

    def middle(lifted, cot_all, turned, w_left, w_right, w_down, hidden_units, back_out, low_turned):
        tok_all = hidden_units.at[2, :, pl.ds(0, features)]
        halves = (pl.ds(0, width), pl.ds(width, width))
        w_query, w_key = (hidden_units.at[0, :, cut] for cut in halves)
        w_value, w_gate = (hidden_units.at[1, :, cut] for cut in halves)
        q_all, gate_all = (turned.at[0, :, cut] for cut in halves)
        slope_q, slope_k = (turned.at[1, :, cut] for cut in halves)
        heads_all = low_turned
        k_all, v_all = (w_down.at[:, cut] for cut in halves)
        k_rows, v_rows = (whole.at[pl.ds(BAND, rows), :] for whole in (k_all, v_all))

        first = [load(0, tok, tok_all), load(1, wk, w_key), load(2, wv, w_value), load(3, wq, w_query), load(4, wg, w_gate)]
        pl.semaphore_wait(barrier, len(partners))
        wo_across().start()
        pad = jnp.full((1, BAND), -1.0, F32)
        seg_ref[0:1, :BAND] = pad
        seg_ref[0:1, BAND + rows :] = pad
        seg_ref[0:1, BAND : BAND + rows] = ids_ref[...].astype(F32)
        for padded in (k_all, v_all):
            padded[:BAND, :] = jnp.zeros((BAND, width), BF16)
        for copy in first:
            copy.wait()
        later = [load(5, wo, wo_own), load(6, cot, cot_all), load(7, wl, w_left), load(8, wr, w_right)]
        keeps = [(q_all, q), (k_rows, k), (v_rows, v), (gate_all, gate), (slope_q, sq), (slope_k, sk), (heads_all, heads)]

        def forward_block(block, carry):
            place = chunk(block)
            here = pl.ds(pl.multiple_of(BAND + block * BLOCK, 128), BLOCK)
            span = pl.ds(pl.multiple_of(block * BLOCK, BLOCK), SPAN)
            source = tok_all[place, :].astype(F32)
            normed = (source * rms_scale(source)).astype(BF16)
            for weight, slope, target, rows_at in ((w_key, slope_k, k_all, here), (w_query, slope_q, q_all, place)):
                pre = nn(normed, weight[...])
                sigma = jax.nn.sigmoid(pre)
                target[rows_at, :] = (pre * sigma).astype(BF16)
                slope[place, :] = (sigma * (1.0 + pre * (1.0 - sigma))).astype(BF16)
            v_all[here, :] = nn(normed, w_value[...]).astype(BF16)
            gate_all[place, :] = nn(normed, w_gate[...]).astype(BF16)
            row_at = iota_f32((BLOCK, 1), 0)
            key_at = iota_f32((1, SPAN), 1) - float(BAND)
            allowed = (seg_column(BAND + block * BLOCK) == seg_lanes(block * BLOCK, SPAN)) & (
                row_at >= key_at
            )
            total = jnp.zeros((BLOCK, 1), F32)
            for head in range(width // 128):
                lanes = slice(head * 128, head * 128 + 128)
                decay = decay_ref[head]
                falloff = jnp.exp(-decay * row_at) * jnp.exp(decay * key_at)
                scores = nt(q_all[place, lanes], k_all[span, lanes])
                weighted = jnp.where(allowed, scores * falloff, 0.0).astype(BF16)
                found = nn(weighted, v_all[span, lanes])
                total = total + jnp.sum(found * found, axis=1, keepdims=True)
                heads_all[place, lanes] = found.astype(BF16)
                u_all[place, lanes] = (
                    found * gain_lanes(head) * gate_all[place, lanes].astype(F32)
                ).astype(BF16)
            lane_rows = to_rows(total)
            for i in range(lanes_in):
                sums_ref[block, i : i + 1, :] = lane_rows[i : i + 1, :]
            u_copy(block).start()
            sum_copy(block).start()
            for index, (source, target) in enumerate(keeps):
                pltpu.make_async_copy(
                    source.at[place, :], target.at[place, :], kept.at[index]
                ).start()

            @pl.when(block == 1)
            def _():
                wo_across().wait()
                wo_beside().start()

            @pl.when(block == blocks - 1)
            def _():
                wo_beside().wait()
                wo_sibling().start()

            return carry

        lax.fori_loop(0, blocks, forward_block, 0)
        for index, (source, target) in enumerate(keeps):
            pltpu.make_async_copy(source, target, kept.at[index]).wait()
        later.append(load(9, wd, w_down))
        for copy in later:
            copy.wait()
        wo_sibling().wait()

        def gated(step, carry):
            block = lax.rem(step + 1 - side, blocks)
            part = lax.rem(block, 2)
            owned = lax.div(block, 2) == side
            place = chunk(block)
            u_copy(block).wait()
            sum_copy(block).wait()
            for i in range(lanes_in):
                scale_rows[block, i : i + 1, :] = lax.rsqrt(
                    (sums_ref[block, i : i + 1, :] + sum_in[block, i : i + 1, :]) / full_inner + eps
                )
            attn = nn(u_all[place, :], wo_own[...]) + nn(u_in[place, :], wo_peer[...])
            state = tok_all[place, :].astype(F32) + lane_column(scale_rows, block) * attn
            rows_in = (state * rms_scale(state)).astype(BF16)
            lifted[...] = rows_in

            @pl.when(owned)
            def _():
                hidden[chunk(part), :] = state

            rows_cot = cot_all[place, :]
            for start, size in tiles(units):
                cut = slice(start, start + size)
                left = nn(lifted[...], w_left[:, cut])
                right = nn(lifted[...], w_right[:, cut])
                grad = nt(rows_cot, w_down[cut, :])
                hidden_units[2, place, cut] = (left * right).astype(BF16)
                hidden_units[0, place, cut] = (grad * right).astype(BF16)
                hidden_units[1, place, cut] = (grad * left).astype(BF16)
            back = nt(hidden_units[0, place, :], w_left[...]) + nt(
                hidden_units[1, place, :], w_right[...]
            )

            @pl.when(owned)
            def _():
                grad_hidden[chunk(part), :] = back

            @pl.when(jnp.logical_not(owned))
            def _():
                back_out[chunk(part), :] = back.astype(BF16)
                back_copy(back_out, part).start()

            put_turned(turned.at[0], rows_in, place)
            put_turned(turned.at[1], rows_cot, place)
            return carry

        lax.fori_loop(0, blocks, gated, 0)

        def down_other(part, carry):
            down_out[chunk(part), :] = nn(
                hidden_units[2, at(other0 + part * BLOCK), :], w_down[...]
            ).astype(BF16)
            return carry

        lax.fori_loop(0, 2, down_other, 0)

        def block_step(block, carry):
            lhs, rhs = turned.at[lax.div(block, 2)], hidden_units.at[block]
            first = core_copy(0, block, ffn_c, units)
            stage_send(lhs, rhs, units, first)

            @pl.when(block < 2)
            def _():
                part = block
                back_copy(back_out, part).wait()
                state = hidden[chunk(part), :]
                pulled = grad_hidden[chunk(part), :] + back_in[chunk(part), :].astype(F32)
                grad = cot_all[at(own0 + part * BLOCK), :].astype(F32) + rms_back(
                    state, rms_scale(state), pulled
                )
                grad_hidden[chunk(part), :] = grad
                low = grad.astype(BF16)
                for_own = nt(low, wo_own[...])
                for_peer = nt(low, wo_peer[...])
                mixed_out[chunk(part), :] = for_peer.astype(BF16)
                mixed_grad[at(own0 + part * BLOCK), :] = for_own.astype(BF16)
                mixed_copy(part).start()
                place = at(own0 + part * BLOCK)
                both = jnp.sum(
                    u_all[place, :].astype(F32) * for_own + u_in[place, :].astype(F32) * for_peer,
                    axis=1,
                    keepdims=True,
                )
                lanes = to_rows(both)
                for i in range(lanes_in):
                    cross[side * 2 + part, i : i + 1, :] = lanes[i : i + 1, :]
                cross_copy(part).start()
                put_turned(low_turned, low, chunk(part))
                scale = lane_column(scale_rows, side * 2 + part)
                back_out[chunk(part), :width] = (u_all[place, :].astype(F32) * scale).astype(BF16)
                back_out[chunk(part), width:] = (u_in[place, :].astype(F32) * scale).astype(BF16)

                @pl.when(part == 1)
                def _():
                    down_copy(0).start()
                    down_copy(1).start()

            stage_core(
                lhs, rhs, units, first, ffn_c.at[block], second_copy(0, block, ffn_c, ffn_y)
            )
            return carry

        lax.fori_loop(0, 3, block_step, 0)

        def down_own(part, carry):
            hidden[chunk(part), :] += nn(
                hidden_units[2, at(own0 + part * BLOCK), :], w_down[...]
            )
            return carry

        lax.fori_loop(0, 2, down_own, 0)
        columns = 2 * width
        first = core_copy(3, 0, att_c, columns)
        stage_send(low_turned, back_out, columns, first)
        stage_core(low_turned, back_out, columns, first, att_c.at[0], second_copy(3, 0, att_c, att_y))
        stage_second(0, 0, ffn_c, ffn_y, ffn_z)

    pl.run_scoped(
        middle,
        pltpu.VMEM((BLOCK, features), BF16),
        pltpu.VMEM((rows, features), BF16),
        pltpu.VMEM((2, features, rows), BF16),
        pltpu.VMEM((features, units), BF16),
        pltpu.VMEM((features, units), BF16),
        pltpu.VMEM((units, features), BF16),
        pltpu.VMEM((3, rows, units), BF16),
        pltpu.VMEM((half, features), BF16),
        pltpu.VMEM((features, half), BF16),
    )

    def last(q_all, grads, k_all, v_all, slope_q, slope_k, heads_all, gate_all, pulls, weights, norm_out, norm_own, results, turned, tok_all):
        columns = 2 * width
        loads = [
            load(0, v, v_all.at[pl.ds(BAND, rows), :]),
            load(1, k, k_all.at[pl.ds(BAND, rows), :]),
            load(2, q, q_all.at[pl.ds(0, rows), :]),
            load(3, gate, gate_all),
            load(4, heads, heads_all),
            load(5, sq, slope_q),
            load(6, sk, slope_k),
        ]
        later = [load(7, tok, tok_all)] + [
            load(8 + i, source, weights.at[:, pl.ds(i * width, width)])
            for i, source in enumerate((wq, wk, wv, wg))
        ]
        for padded in (k_all, v_all):
            padded[:BAND, :] = jnp.zeros((BAND, width), BF16)
        for padded in (q_all, grads):
            padded[rows:, :] = jnp.zeros((BAND, width), BF16)
        gain_sum[0] = jnp.zeros(gain_sum.shape[1:], F32)
        for copy in loads:
            copy.wait()
        for part in range(2):
            mixed_copy(part).wait()
            cross_copy(part).wait()

        gain_row = jnp.concatenate([gain_lanes(i) for i in range(width // 128)], axis=1)

        def prepare(block, carry):
            place = chunk(block)
            scale = lane_column(scale_rows, block)
            joint = lane_column(cross, block)
            grad = mixed_grad[place, :].astype(F32)
            head_rows = heads_all[place, :].astype(F32)
            gain = gain_row
            scaled = grad * gate_all[place, :].astype(F32)
            unit = head_rows * scale
            gain_sum[0, 0:1, :] += jnp.sum(scaled * unit, axis=0, keepdims=True)
            pulls[1, place, width:] = (grad * (unit * gain)).astype(BF16)
            grads[place, :] = (
                scale * (scaled * gain)
                - head_rows * (scale * scale * scale) * (joint / full_inner)
            ).astype(BF16)
            return carry

        lax.fori_loop(0, rows // BLOCK, prepare, 0)
        gain_copy(0, 0, sibling).start()
        stage_second(0, 1, ffn_c, ffn_y, ffn_z)

        def by_query(block, carry):
            place, span = chunk(block), pl.ds(pl.multiple_of(block * BLOCK, BLOCK), SPAN)
            row_at = iota_f32((BLOCK, 1), 0)
            key_at = iota_f32((1, SPAN), 1) - float(BAND)
            allowed = (seg_column(BAND + block * BLOCK) == seg_lanes(block * BLOCK, SPAN)) & (
                row_at >= key_at
            )
            for head in range(width // 128):
                lanes = slice(head * 128, head * 128 + 128)
                decay = decay_ref[head]
                falloff = jnp.exp(-decay * row_at) * jnp.exp(decay * key_at)
                grad = nt(grads[place, lanes], v_all[span, lanes])
                grad = jnp.where(allowed, grad * falloff, 0.0).astype(BF16)
                pulls[0, place, lanes] = (
                    nn(grad, k_all[span, lanes]) * slope_q[place, lanes].astype(F32)
                ).astype(BF16)
            return carry

        lax.fori_loop(0, rows // BLOCK, by_query, 0)

        def by_key(block, carry):
            place, span = chunk(block), pl.ds(pl.multiple_of(block * BLOCK, BLOCK), SPAN)
            here = pl.ds(pl.multiple_of(BAND + block * BLOCK, 128), BLOCK)
            key_at = iota_f32((BLOCK, 1), 0)
            row_at = iota_f32((1, SPAN), 1)
            allowed = (
                seg_column(BAND + block * BLOCK) == seg_lanes(BAND + block * BLOCK, SPAN)
            ) & (row_at >= key_at)
            for head in range(width // 128):
                lanes = slice(head * 128, head * 128 + 128)
                turned_lanes = slice(width + head * 128, width + head * 128 + 128)
                decay = decay_ref[head]
                falloff = jnp.exp(decay * key_at) * jnp.exp(-decay * row_at)
                span_q, span_grad = q_all[span, lanes], grads[span, lanes]
                scores = nt(k_all[here, lanes], span_q)
                weighted = jnp.where(allowed, scores * falloff, 0.0).astype(BF16)
                pulls[1, place, lanes] = nn(weighted, span_grad).astype(BF16)
                grad = nt(v_all[here, lanes], span_grad)
                grad = jnp.where(allowed, grad * falloff, 0.0).astype(BF16)
                pulls[0, place, turned_lanes] = (
                    nn(grad, span_q) * slope_k[place, lanes].astype(F32)
                ).astype(BF16)
            return carry

        lax.fori_loop(0, rows // BLOCK, by_key, 0)
        for copy in later:
            copy.wait()

        def normed_part(step, carry):
            part = lax.rem(step, 2)
            place = at((1 - side + lax.div(step, 2) * (2 * side - 1)) * half + part * BLOCK)
            back = nt(pulls[0, place, :], weights[:, :columns]) + nt(
                pulls[1, place, :], weights[:, columns:]
            )

            @pl.when(step < 2)
            def _():
                norm_out[chunk(part), :] = back.astype(BF16)
                norm_copy(norm_out, part).start()

            @pl.when(step >= 2)
            def _():
                norm_own[chunk(part), :] = back

            return carry

        lax.fori_loop(0, 4, normed_part, 0)

        def finish_out(part, carry):
            down_copy(part).wait()
            results[0, chunk(part), :] = (
                hidden[chunk(part), :] + down_in[chunk(part), :].astype(F32)
            ).astype(BF16)
            out_copy(results.at[0], part).start()
            pltpu.make_async_copy(
                results.at[0, chunk(part), :], out_ref.at[at(own0 + part * BLOCK), :], local.at[part]
            ).start()
            return carry

        lax.fori_loop(0, 2, finish_out, 0)
        stage_second(0, 2, ffn_c, ffn_y, ffn_z)

        def turn(block, carry):
            source = tok_all[chunk(block), :].astype(F32)
            put_turned(turned, (source * rms_scale(source)).astype(BF16), chunk(block))
            return carry

        lax.fori_loop(0, rows // BLOCK, turn, 0)

        gain_copy(0, 0, sibling).wait()
        gain_sum[1] = gain_sum[0] + gain_in[0]
        gain_copy(1, 1, beside).start()

        def block_step(step, carry):
            block = step + 1
            rhs = pulls.at[step]
            first = core_copy(3, block, att_c, columns)
            stage_send(turned, rhs, columns, first)
            stage_core(
                turned, rhs, columns, first, att_c.at[block], second_copy(3, block, att_c, att_y)
            )
            return carry

        lax.fori_loop(0, 2, block_step, 0)

        gain_copy(1, 1, beside).wait()
        gain_sum[2] = gain_sum[1] + gain_in[1]
        for hop in range(1, thirds):
            gain_copy(2, 1 + hop, far(hop)).start()

        def finish_tokens(part, carry):
            norm_copy(norm_out, part).wait()
            pulled = norm_own[chunk(part), :] + norm_in[chunk(part), :].astype(F32)
            source = tok_all[at(own0 + part * BLOCK), :].astype(F32)
            results[1, chunk(part), :] = (
                grad_hidden[chunk(part), :] + rms_back(source, rms_scale(source), pulled)
            ).astype(BF16)
            tg_copy(results.at[1], part).start()
            pltpu.make_async_copy(
                results.at[1, chunk(part), :], tg_ref.at[at(own0 + part * BLOCK), :], local.at[2 + part]
            ).start()
            return carry

        lax.fori_loop(0, 2, finish_tokens, 0)

        stage_second(3, 0, att_c, att_y, att_z)

        def seconds_last(block, carry):
            stage_second(3, block, att_c, att_y, att_z)
            return carry

        lax.fori_loop(1, 3, seconds_last, 0)

        def ffn_total(block, carry):
            ffn_ref[block] = stage_third(0, block, ffn_y, ffn_z)
            return carry

        lax.fori_loop(0, 3, ffn_total, 0)

        def attn_total(block, carry):
            attn_ref[block] = stage_third(3, block, att_y, att_z)
            return carry

        lax.fori_loop(0, 1, attn_total, 0)
        turn_out[...] = attn_ref[0, :, width:]
        turn_copy = over_x(25, turn_out, turn_in)
        turn_copy.start()
        lax.fori_loop(1, 3, attn_total, 0)
        total = gain_sum[2]
        for hop in range(1, thirds):
            gain_copy(2, 1 + hop, far(hop)).wait()
            total = total + gain_in[1 + hop]
        gain_out[...] = total
        turn_copy.wait()
        attn_ref[0, :, :width] += turn_in[...]

        def close(part, carry):
            out_copy(results.at[0], part).wait()
            tg_copy(results.at[1], part).wait()
            for index, target in ((0, out_ref), (1, tg_ref)):
                pltpu.make_async_copy(
                    results.at[index, chunk(part), :],
                    target.at[at(own0 + part * BLOCK), :],
                    local.at[2 * index + part],
                ).wait()
            return carry

        lax.fori_loop(0, 2, close, 0)

    pl.run_scoped(
        last,
        pltpu.VMEM((rows + BAND, width), BF16),
        pltpu.VMEM((rows + BAND, width), BF16),
        pltpu.VMEM((rows + BAND, width), BF16),
        pltpu.VMEM((rows + BAND, width), BF16),
        pltpu.VMEM((rows, width), BF16),
        pltpu.VMEM((rows, width), BF16),
        pltpu.VMEM((rows, width), BF16),
        pltpu.VMEM((rows, width), BF16),
        pltpu.VMEM((2, rows, 2 * width), BF16),
        pltpu.VMEM((features, 4 * width), BF16),
        pltpu.VMEM((half, features), BF16),
        pltpu.VMEM((half, features), F32),
        pltpu.VMEM((2, half, features), BF16),
        pltpu.VMEM((features, rows), BF16),
        pltpu.VMEM((rows, features), BF16),
    )


def run_layer(ways, *args):
    (ids, decays, gain, tok, cot, wo, wl, wr, wd, wq) = args[:10]
    rows, features = tok.shape
    width, units = wq.shape[1], wl.shape[1]
    half, thirds, share = rows // 2, ways // 4, features // ways
    quarter = features // 4
    lane_rows = (rows // BLOCK, 8, 128)
    vmem = pl.BlockSpec(memory_space=pltpu.VMEM)
    hbm = pl.BlockSpec(memory_space=pl.ANY)
    shape = jax.ShapeDtypeStruct
    scratch = [
        ((rows, width), BF16), ((width, features), BF16), (lane_rows, F32),
        ((half, features), BF16), ((half, features), BF16),
        ((rows, width), BF16), (lane_rows, F32), ((half, features), BF16), ((share, width), F32),
        ((3, 2 * quarter, units), BF16), ((3, quarter, units), BF16),
        ((3, thirds - 1, share, units), BF16),
        ((3, 2 * quarter, 2 * width), BF16), ((3, quarter, 2 * width), BF16),
        ((3, thirds - 1, share, 2 * width), BF16), ((thirds + 1, 8, width), F32),
        ((1, rows + 2 * BAND), F32), (lane_rows, F32), ((rows, width), BF16),
        ((width, features), BF16), ((half, width), BF16),
        ((half, features), BF16), ((half, features), F32), ((half, features), F32),
        (lane_rows, F32), ((2 * quarter, max(units, 2 * width)), BF16), ((3, 8, width), F32),
        ((share, width), F32),
    ]
    return pl.pallas_call(
        functools.partial(layer, ways),
        in_specs=[vmem, pl.BlockSpec(memory_space=pltpu.SMEM), vmem] + [hbm] * (len(args) - 3),
        out_specs=[hbm, hbm, vmem, vmem, vmem] + [hbm] * 7,
        out_shape=[
            shape((rows, features), BF16), shape((rows, features), BF16),
            shape((3, share, units), F32), shape((3, share, 2 * width), F32), shape((8, width), F32),
        ]
        + [shape((rows, width), BF16)] * 7,
        scratch_shapes=[pltpu.VMEM(size, dtype) for size, dtype in scratch]
        + [
            pltpu.SemaphoreType.DMA((26,)), pltpu.SemaphoreType.DMA((26,)),
            pltpu.SemaphoreType.DMA((2, 6)), pltpu.SemaphoreType.DMA((2, 6)),
            pltpu.SemaphoreType.DMA((7, thirds + 1)), pltpu.SemaphoreType.DMA((7, thirds + 1)),
            pltpu.SemaphoreType.DMA((12,)), pltpu.SemaphoreType.DMA((7,)),
        ],
        compiler_params=pltpu.CompilerParams(
            collective_id=1, has_side_effects=True, vmem_limit_bytes=VMEM_LIMIT
        ),
        cost_estimate=pl.CostEstimate(flops=5 * 10**10, bytes_accessed=60 * 2**20, transcendentals=10**6),
        name="layer",
    )(*args)


def local(
    ways, tokens, segment_ids, decay_rate, query_weight, key_weight, value_weight, gate_weight,
    output_weight, norm_gain, left_weight, right_weight, down_weight, cotangent,
):
    heads_here, head_size = norm_gain.shape
    width = heads_here * head_size
    block_out, tokens_grad, ffn, attn, gain_total = run_layer(
        ways, segment_ids, decay_rate, norm_gain, tokens, cotangent, output_weight,
        left_weight, right_weight, down_weight, query_weight, key_weight, value_weight, gate_weight,
    )[:5]
    each = head_size // ways
    gain_grad = lax.dynamic_slice_in_dim(
        gain_total[0].reshape(heads_here, head_size), lax.axis_index("dp") * each, each, 1
    )
    return (
        block_out,
        tokens_grad.astype(F32),
        attn[1, :, :width],
        attn[1, :, width:],
        attn[2, :, :width],
        attn[2, :, width:],
        attn[0, :, :width].T,
        gain_grad,
        ffn[0],
        ffn[1],
        ffn[2].T,
    )


def solution(mesh):
    dp, tensor = "dp", "tensor"
    in_specs = (
        P(dp, None), P(dp, None), P(tensor), P(None, tensor), P(None, tensor), P(None, tensor),
        P(None, tensor), P(tensor, None), P(tensor, None), P(None, tensor), P(None, tensor),
        P(tensor, None), P(dp, None),
    )
    out_specs = (
        P(dp, None), P(dp, None), P(dp, tensor), P(dp, tensor), P(dp, tensor), P(dp, tensor),
        P(tensor, dp), P(tensor, dp), P(dp, tensor), P(dp, tensor), P(tensor, dp),
    )
    return jax.shard_map(
        functools.partial(local, mesh.shape[dp]),
        mesh=mesh, in_specs=in_specs, out_specs=out_specs, check_vma=False,
    )
```

```python
import functools

import jax
import jax.numpy as jnp
from jax import lax
from jax.experimental import pallas as pl
from jax.experimental.pallas import tpu as pltpu
from jax.sharding import PartitionSpec as P

MESH = pl.DeviceIdType.MESH
eps = 1e-06
BAND = 384
BLOCK = 256
SPAN = BAND + BLOCK
F32 = jnp.float32
BF16 = jnp.bfloat16
VMEM_LIMIT = 62 * 1024 * 1024


def nn(left_op, right_op):
    return jnp.dot(left_op, right_op, preferred_element_type=F32)


def nt(left_op, right_op):
    return lax.dot_general(
        left_op, right_op, (((1,), (1,)), ((), ())), preferred_element_type=F32
    )


def at(start):
    return pl.ds(pl.multiple_of(start, BLOCK), BLOCK)


def rms_scale(values):
    return lax.rsqrt(jnp.mean(values * values, axis=1, keepdims=True) + eps)


def rms_back(values, scale, grads):
    return scale * grads - values * (scale * scale * scale) * jnp.mean(
        values * grads, axis=1, keepdims=True
    )


def eye():
    shape = (128, 128)
    return lax.broadcasted_iota(jnp.int32, shape, 0) == lax.broadcasted_iota(jnp.int32, shape, 1)


def to_column(rows):
    parts = [
        jnp.sum(jnp.where(eye(), rows[i : i + 1, :], 0.0), axis=1, keepdims=True)
        for i in range(rows.shape[0])
    ]
    return jnp.concatenate(parts, axis=0)


def to_rows(column):
    parts = [
        jnp.sum(jnp.where(eye(), column[i : i + 128, :], 0.0), axis=0, keepdims=True)
        for i in range(0, column.shape[0], 128)
    ]
    return jnp.concatenate(parts, axis=0)


def iota_f32(shape, axis):
    return lax.broadcasted_iota(jnp.int32, shape, axis).astype(F32)


def tiles(extent, most=512):
    return [(start, min(most, extent - start)) for start in range(0, extent, most)]


def layer(
    ways,
    ids_ref, decay_ref, gain_ref, tok, cot, wo, wl, wr, wd, wq, wk, wv, wg,
    out_ref, tg_ref, ffn_ref, attn_ref, gain_out,
    q, k, v, gate, heads, sq, sk,
    u_in, wo_peer, sum_in, back_in, down_in, mixed_grad, cross, norm_in, turn_in,
    ffn_c, ffn_y, ffn_z, att_c, att_y, att_z, gain_in,
    seg_ref, sums_ref, u_all, wo_own, mixed_out, down_out, hidden, grad_hidden, scale_rows, core_out, gain_sum, turn_out,
    send, recv, dp_send, dp_recv, z_send, z_recv, local, kept,
):
    dp, side = lax.axis_index("dp"), lax.axis_index("tensor")
    core, second, third = lax.rem(dp, 2), lax.rem(lax.div(dp, 2), 2), lax.div(dp, 4)
    rows, features = tok.shape
    width = wq.shape[1]
    units = wl.shape[1]
    half = rows // 2
    thirds = ways // 4
    share = features // ways
    full_inner = float(2 * width)
    own0, other0 = side * half, (1 - side) * half
    across = (dp, 1 - side)
    sibling = (dp + 1 - 2 * core, side)
    beside = (dp + 2 - 4 * second, side)

    def far(hop):
        return (lax.rem(third + hop, thirds) * 4 + second * 2 + core, side)

    def remote(source, target, send_sem, recv_sem, device):
        return pltpu.make_async_remote_copy(
            src_ref=source, dst_ref=target, send_sem=send_sem, recv_sem=recv_sem,
            device_id=device, device_id_type=MESH,
        )

    def over_x(index, source, target):
        return remote(source, target, send.at[index], recv.at[index], across)

    def load(index, source, target):
        copy = pltpu.make_async_copy(source, target, local.at[index])
        copy.start()
        return copy

    def put_turned(target, block, column):
        turned = jnp.transpose(block)
        for owner in range(ways):
            place = (owner % 2) * (ways // 2) + (owner // 2 % 2) * (ways // 4) + owner // 4
            target[place * share : (place + 1) * share, column] = turned[
                owner * share : (owner + 1) * share, :
            ]

    def chunk(part):
        return at(part * BLOCK)

    def u_copy(block):
        return over_x(block, u_all.at[chunk(block), :], u_in.at[chunk(block), :])

    def sum_copy(block):
        return over_x(4 + block, sums_ref.at[block], sum_in.at[block])

    def back_copy(source, part):
        return over_x(11 + part, source.at[chunk(part), :], back_in.at[chunk(part), :])

    def mixed_copy(part):
        return over_x(
            13 + part, mixed_out.at[chunk(part), :], mixed_grad.at[at(own0 + part * BLOCK), :]
        )

    def cross_copy(part):
        mine = cross.at[side * 2 + part]
        return over_x(15 + part, mine, mine)

    def down_copy(part):
        return over_x(17 + part, down_out.at[chunk(part), :], down_in.at[chunk(part), :])

    def norm_copy(source, part):
        return over_x(19 + part, source.at[chunk(part), :], norm_in.at[chunk(part), :])

    def out_copy(source, part):
        return over_x(21 + part, source.at[chunk(part), :], out_ref.at[at(own0 + part * BLOCK), :])

    def tg_copy(source, part):
        return over_x(23 + part, source.at[chunk(part), :], tg_ref.at[at(own0 + part * BLOCK), :])

    slice_rows = width // 4
    wo_start = core * (2 * slice_rows) + second * slice_rows
    wo_piece = pl.ds(pl.multiple_of(wo_start, slice_rows), slice_rows)

    def wo_across():
        return over_x(8, wo.at[wo_piece, :], wo_peer.at[wo_piece, :])

    def wo_beside():
        piece = wo_peer.at[wo_piece, :]
        return remote(piece, piece, send.at[9], recv.at[9], beside)

    def wo_sibling():
        piece = wo_peer.at[pl.ds(pl.multiple_of(core * (2 * slice_rows), 2 * slice_rows), 2 * slice_rows), :]
        return remote(piece, piece, send.at[10], recv.at[10], sibling)

    def core_copy(first, block, landing, columns):
        return remote(
            core_out.at[:, pl.ds(0, columns)], landing.at[block],
            dp_send.at[0, first + block], dp_recv.at[0, first + block], sibling,
        )

    def second_copy(first, block, summed, landing):
        return remote(
            summed.at[block, at((1 - second) * BLOCK), :], landing.at[block],
            dp_send.at[1, first + block], dp_recv.at[1, first + block], beside,
        )

    def third_copy(first, block, hop, summed, landing):
        piece = pl.ds(pl.multiple_of(lax.rem(third + hop, thirds) * share, share), share)
        return remote(
            summed.at[block, piece, :], landing.at[block, hop - 1],
            z_send.at[first + block, hop - 1], z_recv.at[first + block, hop - 1], far(hop),
        )

    def stage_send(turned, grads, columns, copy):
        def one(part, carry):
            left_op = turned[at((1 - core) * 2 * BLOCK + part * BLOCK), :]
            for start, size in tiles(columns):
                core_out[chunk(part), start : start + size] = nn(
                    left_op, grads[:, start : start + size]
                ).astype(BF16)
            return carry

        lax.fori_loop(0, 2, one, 0)
        copy.start()

    def stage_core(turned, grads, columns, copy, landing, onward):
        copy.wait()

        def one(part, carry):
            left_op = turned[at(core * 2 * BLOCK + part * BLOCK), :]
            for start, size in tiles(columns):
                cut = slice(start, start + size)
                total = nn(left_op, grads[:, cut]) + landing[chunk(part), cut].astype(F32)
                landing[chunk(part), cut] = total.astype(BF16)
            return carry

        lax.fori_loop(0, 2, one, 0)
        onward.start()

    def stage_second(first, block, summed, landing, group_out):
        copy = second_copy(first, block, summed, landing)
        copy.wait()
        for start, size in tiles(landing.shape[2]):
            cut = slice(start, start + size)
            total = (
                summed[block, at(second * BLOCK), cut].astype(F32)
                + landing[block, :, cut].astype(F32)
            )
            landing[block, :, cut] = total.astype(BF16)
        for hop in range(1, thirds):
            third_copy(first, block, hop, landing, group_out).start()

    def stage_third(first, block, summed, landing):
        mine = pl.ds(pl.multiple_of(third * share, share), share)
        total = summed[block, mine, :].astype(F32)
        for hop in range(1, thirds):
            third_copy(first, block, hop, summed, landing).wait()
            total = total + landing[block, hop - 1].astype(F32)
        return total

    def gain_copy(stage, slot, device):
        return remote(
            gain_sum.at[stage], gain_in.at[slot], z_send.at[6, slot], z_recv.at[6, slot], device
        )

    barrier = pltpu.get_barrier_semaphore()
    partners = [across, sibling, beside] + [far(hop) for hop in range(1, thirds)]
    for device in partners:
        pl.semaphore_signal(barrier, inc=1, device_id=device, device_id_type=MESH)

    def seg_lanes(start, size):
        return seg_ref[0:1, pl.ds(pl.multiple_of(start, 128), size)]

    def seg_column(start):
        return to_column(
            jnp.concatenate([seg_lanes(start + i, 128) for i in range(0, BLOCK, 128)], axis=0)
        )

    def gain_lanes(head):
        return gain_ref[head : head + 1, :].astype(F32)

    blocks = rows // BLOCK
    lanes_in = BLOCK // 128

    def lane_column(source, block):
        return to_column(
            jnp.concatenate([source[block, i : i + 1, :] for i in range(lanes_in)], axis=0)
        )

    def middle(lifted, cot_all, turned, w_left, w_right, w_down, hidden_units, back_out, low_turned):
        tok_all = hidden_units.at[2, :, pl.ds(0, features)]
        halves = (pl.ds(0, width), pl.ds(width, width))
        w_query, w_key = (hidden_units.at[0, :, cut] for cut in halves)
        w_value, w_gate = (hidden_units.at[1, :, cut] for cut in halves)
        q_all, gate_all = (turned.at[0, :, cut] for cut in halves)
        slope_q, slope_k = (turned.at[1, :, cut] for cut in halves)
        heads_all = low_turned
        k_all, v_all = (w_down.at[:, cut] for cut in halves)
        k_rows, v_rows = (whole.at[pl.ds(BAND, rows), :] for whole in (k_all, v_all))

        first = [load(0, tok, tok_all), load(1, wk, w_key), load(2, wv, w_value), load(3, wq, w_query), load(4, wg, w_gate)]
        pl.semaphore_wait(barrier, len(partners))
        wo_across().start()
        pad = jnp.full((1, BAND), -1.0, F32)
        seg_ref[0:1, :BAND] = pad
        seg_ref[0:1, BAND + rows :] = pad
        seg_ref[0:1, BAND : BAND + rows] = ids_ref[...].astype(F32)
        for padded in (k_all, v_all):
            padded[:BAND, :] = jnp.zeros((BAND, width), BF16)
        for copy in first:
            copy.wait()
        later = [load(5, wo, wo_own), load(6, cot, cot_all), load(7, wl, w_left), load(8, wr, w_right)]
        keeps = [(q_all, q), (k_rows, k), (v_rows, v), (gate_all, gate), (slope_q, sq), (slope_k, sk), (heads_all, heads)]

        def forward_block(block, carry):
            place = chunk(block)
            here = pl.ds(pl.multiple_of(BAND + block * BLOCK, 128), BLOCK)
            span = pl.ds(pl.multiple_of(block * BLOCK, BLOCK), SPAN)
            source = tok_all[place, :].astype(F32)
            normed = (source * rms_scale(source)).astype(BF16)
            for weight, slope, target, rows_at in ((w_key, slope_k, k_all, here), (w_query, slope_q, q_all, place)):
                pre = nn(normed, weight[...])
                sigma = jax.nn.sigmoid(pre)
                target[rows_at, :] = (pre * sigma).astype(BF16)
                slope[place, :] = (sigma * (1.0 + pre * (1.0 - sigma))).astype(BF16)
            v_all[here, :] = nn(normed, w_value[...]).astype(BF16)
            gate_all[place, :] = nn(normed, w_gate[...]).astype(BF16)
            row_at = iota_f32((BLOCK, 1), 0)
            key_at = iota_f32((1, SPAN), 1) - float(BAND)
            allowed = (seg_column(BAND + block * BLOCK) == seg_lanes(block * BLOCK, SPAN)) & (
                row_at >= key_at
            )
            total = jnp.zeros((BLOCK, 1), F32)
            for head in range(width // 128):
                lanes = slice(head * 128, head * 128 + 128)
                decay = decay_ref[head]
                falloff = jnp.exp(-decay * row_at) * jnp.exp(decay * key_at)
                scores = nt(q_all[place, lanes], k_all[span, lanes])
                weighted = jnp.where(allowed, scores * falloff, 0.0).astype(BF16)
                found = nn(weighted, v_all[span, lanes])
                total = total + jnp.sum(found * found, axis=1, keepdims=True)
                heads_all[place, lanes] = found.astype(BF16)
                u_all[place, lanes] = (
                    found * gain_lanes(head) * gate_all[place, lanes].astype(F32)
                ).astype(BF16)
            lane_rows = to_rows(total)
            for i in range(lanes_in):
                sums_ref[block, i : i + 1, :] = lane_rows[i : i + 1, :]
            u_copy(block).start()
            sum_copy(block).start()
            for index, (source, target) in enumerate(keeps):
                pltpu.make_async_copy(
                    source.at[place, :], target.at[place, :], kept.at[index]
                ).start()

            @pl.when(block == 1)
            def _():
                wo_across().wait()
                wo_beside().start()

            @pl.when(block == blocks - 1)
            def _():
                wo_beside().wait()
                wo_sibling().start()

            return carry

        lax.fori_loop(0, blocks, forward_block, 0)
        for index, (source, target) in enumerate(keeps):
            pltpu.make_async_copy(source, target, kept.at[index]).wait()
        later.append(load(9, wd, w_down))
        for copy in later:
            copy.wait()
        wo_sibling().wait()

        def gated(step, carry):
            block = lax.rem(step + 1 - side, blocks)
            part = lax.rem(block, 2)
            owned = lax.div(block, 2) == side
            place = chunk(block)
            u_copy(block).wait()
            sum_copy(block).wait()
            for i in range(lanes_in):
                scale_rows[block, i : i + 1, :] = lax.rsqrt(
                    (sums_ref[block, i : i + 1, :] + sum_in[block, i : i + 1, :]) / full_inner + eps
                )
            attn = nn(u_all[place, :], wo_own[...]) + nn(u_in[place, :], wo_peer[...])
            state = tok_all[place, :].astype(F32) + lane_column(scale_rows, block) * attn
            rows_in = (state * rms_scale(state)).astype(BF16)
            lifted[...] = rows_in

            @pl.when(owned)
            def _():
                hidden[chunk(part), :] = state

            rows_cot = cot_all[place, :]
            for start, size in tiles(units):
                cut = slice(start, start + size)
                left = nn(lifted[...], w_left[:, cut])
                right = nn(lifted[...], w_right[:, cut])
                grad = nt(rows_cot, w_down[cut, :])
                hidden_units[2, place, cut] = (left * right).astype(BF16)
                hidden_units[0, place, cut] = (grad * right).astype(BF16)
                hidden_units[1, place, cut] = (grad * left).astype(BF16)
            back = nt(hidden_units[0, place, :], w_left[...]) + nt(
                hidden_units[1, place, :], w_right[...]
            )

            @pl.when(owned)
            def _():
                grad_hidden[chunk(part), :] = back

            @pl.when(jnp.logical_not(owned))
            def _():
                back_out[chunk(part), :] = back.astype(BF16)
                back_copy(back_out, part).start()

            put_turned(turned.at[0], rows_in, place)
            put_turned(turned.at[1], rows_cot, place)
            return carry

        lax.fori_loop(0, blocks, gated, 0)

        def down_other(part, carry):
            down_out[chunk(part), :] = nn(
                hidden_units[2, at(other0 + part * BLOCK), :], w_down[...]
            ).astype(BF16)
            return carry

        lax.fori_loop(0, 2, down_other, 0)

        def block_step(block, carry):
            lhs, rhs = turned.at[lax.div(block, 2)], hidden_units.at[block]
            first = core_copy(0, block, ffn_c, units)
            stage_send(lhs, rhs, units, first)

            @pl.when(block < 2)
            def _():
                part = block
                back_copy(back_out, part).wait()
                state = hidden[chunk(part), :]
                pulled = grad_hidden[chunk(part), :] + back_in[chunk(part), :].astype(F32)
                grad = cot_all[at(own0 + part * BLOCK), :].astype(F32) + rms_back(
                    state, rms_scale(state), pulled
                )
                grad_hidden[chunk(part), :] = grad
                low = grad.astype(BF16)
                for_own = nt(low, wo_own[...])
                for_peer = nt(low, wo_peer[...])
                mixed_out[chunk(part), :] = for_peer.astype(BF16)
                mixed_grad[at(own0 + part * BLOCK), :] = for_own.astype(BF16)
                mixed_copy(part).start()
                place = at(own0 + part * BLOCK)
                both = jnp.sum(
                    u_all[place, :].astype(F32) * for_own + u_in[place, :].astype(F32) * for_peer,
                    axis=1,
                    keepdims=True,
                )
                lanes = to_rows(both)
                for i in range(lanes_in):
                    cross[side * 2 + part, i : i + 1, :] = lanes[i : i + 1, :]
                cross_copy(part).start()
                put_turned(low_turned, low, chunk(part))
                scale = lane_column(scale_rows, side * 2 + part)
                back_out[chunk(part), :width] = (u_all[place, :].astype(F32) * scale).astype(BF16)
                back_out[chunk(part), width:] = (u_in[place, :].astype(F32) * scale).astype(BF16)

                @pl.when(part == 1)
                def _():
                    down_copy(0).start()
                    down_copy(1).start()

            stage_core(
                lhs, rhs, units, first, ffn_c.at[block], second_copy(0, block, ffn_c, ffn_y)
            )
            return carry

        lax.fori_loop(0, 2, block_step, 0)
        columns = 2 * width
        first = core_copy(3, 0, att_c, columns)
        stage_send(low_turned, back_out, columns, first)
        stage_core(low_turned, back_out, columns, first, att_c.at[0], second_copy(3, 0, att_c, att_y))
        lax.fori_loop(2, 3, block_step, 0)

        def down_own(part, carry):
            hidden[chunk(part), :] += nn(
                hidden_units[2, at(own0 + part * BLOCK), :], w_down[...]
            )
            return carry

        lax.fori_loop(0, 2, down_own, 0)
        stage_second(0, 0, ffn_c, ffn_y, ffn_z)

    pl.run_scoped(
        middle,
        pltpu.VMEM((BLOCK, features), BF16),
        pltpu.VMEM((rows, features), BF16),
        pltpu.VMEM((2, features, rows), BF16),
        pltpu.VMEM((features, units), BF16),
        pltpu.VMEM((features, units), BF16),
        pltpu.VMEM((units, features), BF16),
        pltpu.VMEM((3, rows, units), BF16),
        pltpu.VMEM((half, features), BF16),
        pltpu.VMEM((features, half), BF16),
    )

    def last(q_all, grads, k_all, v_all, slope_q, slope_k, heads_all, gate_all, pulls, weights, norm_out, norm_own, results, turned, tok_all):
        columns = 2 * width
        loads = [
            load(0, v, v_all.at[pl.ds(BAND, rows), :]),
            load(1, k, k_all.at[pl.ds(BAND, rows), :]),
            load(2, q, q_all.at[pl.ds(0, rows), :]),
            load(3, gate, gate_all),
            load(4, heads, heads_all),
            load(5, sq, slope_q),
            load(6, sk, slope_k),
        ]
        later = [load(7, tok, tok_all)] + [
            load(8 + i, source, weights.at[:, pl.ds(i * width, width)])
            for i, source in enumerate((wq, wk, wv, wg))
        ]
        for padded in (k_all, v_all):
            padded[:BAND, :] = jnp.zeros((BAND, width), BF16)
        for padded in (q_all, grads):
            padded[rows:, :] = jnp.zeros((BAND, width), BF16)
        gain_sum[0] = jnp.zeros(gain_sum.shape[1:], F32)
        for copy in loads:
            copy.wait()
        for part in range(2):
            mixed_copy(part).wait()
            cross_copy(part).wait()

        gain_row = jnp.concatenate([gain_lanes(i) for i in range(width // 128)], axis=1)

        def prepare(block, carry):
            place = chunk(block)
            scale = lane_column(scale_rows, block)
            joint = lane_column(cross, block)
            grad = mixed_grad[place, :].astype(F32)
            head_rows = heads_all[place, :].astype(F32)
            gain = gain_row
            scaled = grad * gate_all[place, :].astype(F32)
            unit = head_rows * scale
            gain_sum[0, 0:1, :] += jnp.sum(scaled * unit, axis=0, keepdims=True)
            pulls[1, place, width:] = (grad * (unit * gain)).astype(BF16)
            grads[place, :] = (
                scale * (scaled * gain)
                - head_rows * (scale * scale * scale) * (joint / full_inner)
            ).astype(BF16)
            return carry

        lax.fori_loop(0, rows // BLOCK, prepare, 0)
        gain_copy(0, 0, sibling).start()
        stage_second(0, 1, ffn_c, ffn_y, ffn_z)

        def by_query(block, carry):
            place, span = chunk(block), pl.ds(pl.multiple_of(block * BLOCK, BLOCK), SPAN)
            row_at = iota_f32((BLOCK, 1), 0)
            key_at = iota_f32((1, SPAN), 1) - float(BAND)
            allowed = (seg_column(BAND + block * BLOCK) == seg_lanes(block * BLOCK, SPAN)) & (
                row_at >= key_at
            )
            for head in range(width // 128):
                lanes = slice(head * 128, head * 128 + 128)
                decay = decay_ref[head]
                falloff = jnp.exp(-decay * row_at) * jnp.exp(decay * key_at)
                grad = nt(grads[place, lanes], v_all[span, lanes])
                grad = jnp.where(allowed, grad * falloff, 0.0).astype(BF16)
                pulls[0, place, lanes] = (
                    nn(grad, k_all[span, lanes]) * slope_q[place, lanes].astype(F32)
                ).astype(BF16)
            return carry

        def finish_out(part, carry):
            down_copy(part).wait()
            results[0, chunk(part), :] = (
                hidden[chunk(part), :] + down_in[chunk(part), :].astype(F32)
            ).astype(BF16)
            out_copy(results.at[0], part).start()
            pltpu.make_async_copy(
                results.at[0, chunk(part), :], out_ref.at[at(own0 + part * BLOCK), :], local.at[part]
            ).start()
            return carry

        lax.fori_loop(0, rows // BLOCK, by_query, 0)
        lax.fori_loop(0, 1, finish_out, 0)

        def by_key(block, carry):
            place, span = chunk(block), pl.ds(pl.multiple_of(block * BLOCK, BLOCK), SPAN)
            here = pl.ds(pl.multiple_of(BAND + block * BLOCK, 128), BLOCK)
            key_at = iota_f32((BLOCK, 1), 0)
            row_at = iota_f32((1, SPAN), 1)
            allowed = (
                seg_column(BAND + block * BLOCK) == seg_lanes(BAND + block * BLOCK, SPAN)
            ) & (row_at >= key_at)
            for head in range(width // 128):
                lanes = slice(head * 128, head * 128 + 128)
                turned_lanes = slice(width + head * 128, width + head * 128 + 128)
                decay = decay_ref[head]
                falloff = jnp.exp(decay * key_at) * jnp.exp(-decay * row_at)
                span_q, span_grad = q_all[span, lanes], grads[span, lanes]
                scores = nt(k_all[here, lanes], span_q)
                weighted = jnp.where(allowed, scores * falloff, 0.0).astype(BF16)
                pulls[1, place, lanes] = nn(weighted, span_grad).astype(BF16)
                grad = nt(v_all[here, lanes], span_grad)
                grad = jnp.where(allowed, grad * falloff, 0.0).astype(BF16)
                pulls[0, place, turned_lanes] = (
                    nn(grad, span_q) * slope_k[place, lanes].astype(F32)
                ).astype(BF16)
            return carry

        lax.fori_loop(0, rows // BLOCK, by_key, 0)
        lax.fori_loop(1, 2, finish_out, 0)
        stage_second(3, 0, att_c, att_y, att_z)
        for copy in later:
            copy.wait()

        def normed_part(step, carry):
            part = lax.rem(step, 2)
            place = at((1 - side + lax.div(step, 2) * (2 * side - 1)) * half + part * BLOCK)
            back = nt(pulls[0, place, :], weights[:, :columns]) + nt(
                pulls[1, place, :], weights[:, columns:]
            )

            @pl.when(step < 2)
            def _():
                norm_out[chunk(part), :] = back.astype(BF16)
                norm_copy(norm_out, part).start()

            @pl.when(step >= 2)
            def _():
                norm_own[chunk(part), :] = back

            return carry

        lax.fori_loop(0, 4, normed_part, 0)


        def turn(block, carry):
            source = tok_all[chunk(block), :].astype(F32)
            put_turned(turned, (source * rms_scale(source)).astype(BF16), chunk(block))
            return carry

        lax.fori_loop(0, rows // BLOCK, turn, 0)

        gain_copy(0, 0, sibling).wait()
        gain_sum[1] = gain_sum[0] + gain_in[0]
        gain_copy(1, 1, beside).start()

        def block_step(step, carry):
            block = step + 1
            rhs = pulls.at[step]
            first = core_copy(3, block, att_c, columns)
            stage_send(turned, rhs, columns, first)
            stage_core(
                turned, rhs, columns, first, att_c.at[block], second_copy(3, block, att_c, att_y)
            )

            @pl.when(step == 0)
            def _():
                stage_second(0, 2, ffn_c, ffn_y, ffn_z)

            return carry

        lax.fori_loop(0, 2, block_step, 0)
        gain_copy(1, 1, beside).wait()
        gain_sum[2] = gain_sum[1] + gain_in[1]
        for hop in range(1, thirds):
            gain_copy(2, 1 + hop, far(hop)).start()

        def attn_total(block, carry):
            attn_ref[block] = stage_third(3, block, att_y, att_z)
            return carry

        lax.fori_loop(0, 1, attn_total, 0)
        turn_out[...] = attn_ref[0, :, width:]
        turn_copy = over_x(25, turn_out, turn_in)
        turn_copy.start()

        def finish_tokens(part, carry):
            norm_copy(norm_out, part).wait()
            pulled = norm_own[chunk(part), :] + norm_in[chunk(part), :].astype(F32)
            source = tok_all[at(own0 + part * BLOCK), :].astype(F32)
            results[1, chunk(part), :] = (
                grad_hidden[chunk(part), :] + rms_back(source, rms_scale(source), pulled)
            ).astype(BF16)
            tg_copy(results.at[1], part).start()
            pltpu.make_async_copy(
                results.at[1, chunk(part), :], tg_ref.at[at(own0 + part * BLOCK), :], local.at[2 + part]
            ).start()
            return carry

        lax.fori_loop(0, 2, finish_tokens, 0)

        def seconds_last(block, carry):
            stage_second(3, block, att_c, att_y, att_z)
            return carry

        lax.fori_loop(1, 3, seconds_last, 0)

        def ffn_total(block, carry):
            ffn_ref[block] = stage_third(0, block, ffn_y, ffn_z)
            return carry

        lax.fori_loop(0, 3, ffn_total, 0)
        lax.fori_loop(1, 3, attn_total, 0)
        total = gain_sum[2]
        for hop in range(1, thirds):
            gain_copy(2, 1 + hop, far(hop)).wait()
            total = total + gain_in[1 + hop]
        gain_out[...] = total
        turn_copy.wait()
        attn_ref[0, :, :width] += turn_in[...]

        def close(part, carry):
            out_copy(results.at[0], part).wait()
            tg_copy(results.at[1], part).wait()
            for index, target in ((0, out_ref), (1, tg_ref)):
                pltpu.make_async_copy(
                    results.at[index, chunk(part), :],
                    target.at[at(own0 + part * BLOCK), :],
                    local.at[2 * index + part],
                ).wait()
            return carry

        lax.fori_loop(0, 2, close, 0)

    pl.run_scoped(
        last,
        pltpu.VMEM((rows + BAND, width), BF16),
        pltpu.VMEM((rows + BAND, width), BF16),
        pltpu.VMEM((rows + BAND, width), BF16),
        pltpu.VMEM((rows + BAND, width), BF16),
        pltpu.VMEM((rows, width), BF16),
        pltpu.VMEM((rows, width), BF16),
        pltpu.VMEM((rows, width), BF16),
        pltpu.VMEM((rows, width), BF16),
        pltpu.VMEM((2, rows, 2 * width), BF16),
        pltpu.VMEM((features, 4 * width), BF16),
        pltpu.VMEM((half, features), BF16),
        pltpu.VMEM((half, features), F32),
        pltpu.VMEM((2, half, features), BF16),
        pltpu.VMEM((features, rows), BF16),
        pltpu.VMEM((rows, features), BF16),
    )


def run_layer(ways, *args):
    (ids, decays, gain, tok, cot, wo, wl, wr, wd, wq) = args[:10]
    rows, features = tok.shape
    width, units = wq.shape[1], wl.shape[1]
    half, thirds, share = rows // 2, ways // 4, features // ways
    quarter = features // 4
    lane_rows = (rows // BLOCK, 8, 128)
    vmem = pl.BlockSpec(memory_space=pltpu.VMEM)
    hbm = pl.BlockSpec(memory_space=pl.ANY)
    shape = jax.ShapeDtypeStruct
    scratch = [
        ((rows, width), BF16), ((width, features), BF16), (lane_rows, F32),
        ((half, features), BF16), ((half, features), BF16),
        ((rows, width), BF16), (lane_rows, F32), ((half, features), BF16), ((share, width), F32),
        ((3, 2 * quarter, units), BF16), ((3, quarter, units), BF16),
        ((3, thirds - 1, share, units), BF16),
        ((3, 2 * quarter, 2 * width), BF16), ((3, quarter, 2 * width), BF16),
        ((3, thirds - 1, share, 2 * width), BF16), ((thirds + 1, 8, width), F32),
        ((1, rows + 2 * BAND), F32), (lane_rows, F32), ((rows, width), BF16),
        ((width, features), BF16), ((half, width), BF16),
        ((half, features), BF16), ((half, features), F32), ((half, features), F32),
        (lane_rows, F32), ((2 * quarter, max(units, 2 * width)), BF16), ((3, 8, width), F32),
        ((share, width), F32),
    ]
    return pl.pallas_call(
        functools.partial(layer, ways),
        in_specs=[vmem, pl.BlockSpec(memory_space=pltpu.SMEM), vmem] + [hbm] * (len(args) - 3),
        out_specs=[hbm, hbm, vmem, vmem, vmem] + [hbm] * 7,
        out_shape=[
            shape((rows, features), BF16), shape((rows, features), BF16),
            shape((3, share, units), F32), shape((3, share, 2 * width), F32), shape((8, width), F32),
        ]
        + [shape((rows, width), BF16)] * 7,
        scratch_shapes=[pltpu.VMEM(size, dtype) for size, dtype in scratch]
        + [
            pltpu.SemaphoreType.DMA((26,)), pltpu.SemaphoreType.DMA((26,)),
            pltpu.SemaphoreType.DMA((2, 6)), pltpu.SemaphoreType.DMA((2, 6)),
            pltpu.SemaphoreType.DMA((7, thirds + 1)), pltpu.SemaphoreType.DMA((7, thirds + 1)),
            pltpu.SemaphoreType.DMA((12,)), pltpu.SemaphoreType.DMA((7,)),
        ],
        compiler_params=pltpu.CompilerParams(
            collective_id=1, has_side_effects=True, vmem_limit_bytes=VMEM_LIMIT
        ),
        cost_estimate=pl.CostEstimate(flops=5 * 10**10, bytes_accessed=60 * 2**20, transcendentals=10**6),
        name="layer",
    )(*args)


def finish(
    ways, out_in, tg_in, ffn, attn, gain_in,
    out, tg, query, key, value, gate, output, gain, left, right, down,
    out_held, tg_low, tg_wide, ffn_held, attn_held, arrived, left_here,
):
    width = query.shape[1]
    blocks = tg.shape[0] // BLOCK
    pairs = []
    for i in range(blocks):
        place = at(i * BLOCK)
        pairs.append((tg_in.at[place, :], tg_low.at[place, :], tg_wide.at[place, :], tg.at[place, :]))
    for i, target in enumerate((left, right, down)):
        pairs.append((ffn.at[i], ffn_held.at[i], ffn_held.at[i], target))
    for i, j, target in ((1, 0, query), (1, 1, key), (2, 0, value), (2, 1, gate), (0, 0, output)):
        cut = pl.ds(j * width, width)
        held = attn_held.at[i, :, cut]
        pairs.append((attn.at[i, :, cut], held, held, target))
    for i in range(blocks):
        place = at(i * BLOCK)
        pairs.append((out_in.at[place, :], out_held.at[place, :], out_held.at[place, :], out.at[place, :]))
    loads = [
        pltpu.make_async_copy(source, held, arrived.at[i])
        for i, (source, held, _, _) in enumerate(pairs)
    ]
    stores = [
        pltpu.make_async_copy(held, target, left_here.at[i])
        for i, (_, _, held, target) in enumerate(pairs)
    ]
    for copy in loads:
        copy.start()
    heads, each = gain.shape
    rows_in = jnp.concatenate([gain_in[0:1, i * 128 : i * 128 + 128] for i in range(heads)], axis=0)
    lane = lax.broadcasted_iota(jnp.int32, rows_in.shape, 1)
    place = lax.broadcasted_iota(jnp.int32, gain.shape, 1)
    first = lax.axis_index("dp") * each
    found = jnp.zeros(gain.shape, F32)
    for i in range(each):
        column = jnp.sum(jnp.where(lane == first + i, rows_in, 0.0), axis=1, keepdims=True)
        found = jnp.where(place == i, column, found)
    gain[...] = found
    for i in range(len(pairs)):
        loads[i].wait()
        if i < blocks:
            tg_wide[at(i * BLOCK), :] = tg_low[at(i * BLOCK), :].astype(F32)
        stores[i].start()
    for copy in stores:
        copy.wait()


def run_finish(ways, heads, out_in, tg_in, ffn, attn, gain_in):
    rows, features = tg_in.shape
    share, units, width = ffn.shape[1], ffn.shape[2], attn.shape[2] // 2
    vmem = pl.BlockSpec(memory_space=pltpu.VMEM)
    hbm = pl.BlockSpec(memory_space=pl.ANY)
    shape = lambda *size: jax.ShapeDtypeStruct(size, F32)
    copies = 2 * (rows // BLOCK) + 8
    return pl.pallas_call(
        functools.partial(finish, ways),
        in_specs=[hbm] * 4 + [vmem],
        out_specs=[hbm] * 7 + [vmem] + [hbm] * 3,
        out_shape=[jax.ShapeDtypeStruct((rows, features), BF16), shape(rows, features)]
        + [shape(share, width)] * 5
        + [shape(heads, gain_in.shape[1] // heads // ways)]
        + [shape(share, units)] * 3,
        scratch_shapes=[
            pltpu.VMEM((rows, features), BF16), pltpu.VMEM((rows, features), BF16),
            pltpu.VMEM((rows, features), F32), pltpu.VMEM((3, share, units), F32),
            pltpu.VMEM((3, share, 2 * width), F32),
            pltpu.SemaphoreType.DMA((copies,)), pltpu.SemaphoreType.DMA((copies,)),
        ],
        compiler_params=pltpu.CompilerParams(vmem_limit_bytes=VMEM_LIMIT),
        name="finish",
    )(out_in, tg_in, ffn, attn, gain_in)


def local(
    ways, tokens, segment_ids, decay_rate, query_weight, key_weight, value_weight, gate_weight,
    output_weight, norm_gain, left_weight, right_weight, down_weight, cotangent,
):
    held = run_layer(
        ways, segment_ids, decay_rate, norm_gain, tokens, cotangent, output_weight,
        left_weight, right_weight, down_weight, query_weight, key_weight, value_weight, gate_weight,
    )[:5]
    results = list(run_finish(ways, norm_gain.shape[0], *held))
    for turned in (6, 10):
        results[turned] = results[turned].T
    return tuple(results)


def solution(mesh):
    dp, tensor = "dp", "tensor"
    in_specs = (
        P(dp, None), P(dp, None), P(tensor), P(None, tensor), P(None, tensor), P(None, tensor),
        P(None, tensor), P(tensor, None), P(tensor, None), P(None, tensor), P(None, tensor),
        P(tensor, None), P(dp, None),
    )
    out_specs = (
        P(dp, None), P(dp, None), P(dp, tensor), P(dp, tensor), P(dp, tensor), P(dp, tensor),
        P(tensor, dp), P(tensor, dp), P(dp, tensor), P(dp, tensor), P(tensor, dp),
    )
    return jax.shard_map(
        functools.partial(local, mesh.shape[dp]),
        mesh=mesh, in_specs=in_specs, out_specs=out_specs, check_vma=False,
    )
```

```python
import functools

import jax
import jax.numpy as jnp
from jax import lax
from jax.experimental import pallas as pl
from jax.experimental.pallas import tpu as pltpu
from jax.sharding import PartitionSpec as P

MESH = pl.DeviceIdType.MESH
eps = 1e-06
BAND = 384
BLOCK = 256
SPAN = BAND + BLOCK
F32 = jnp.float32
BF16 = jnp.bfloat16
VMEM_LIMIT = 62 * 1024 * 1024


def nn(left_op, right_op):
    return jnp.dot(left_op, right_op, preferred_element_type=F32)


def nt(left_op, right_op):
    return lax.dot_general(
        left_op, right_op, (((1,), (1,)), ((), ())), preferred_element_type=F32
    )


def at(start):
    return pl.ds(pl.multiple_of(start, BLOCK), BLOCK)


def rms_scale(values):
    return lax.rsqrt(jnp.mean(values * values, axis=1, keepdims=True) + eps)


def rms_back(values, scale, grads):
    return scale * grads - values * (scale * scale * scale) * jnp.mean(
        values * grads, axis=1, keepdims=True
    )


def eye():
    shape = (128, 128)
    return lax.broadcasted_iota(jnp.int32, shape, 0) == lax.broadcasted_iota(jnp.int32, shape, 1)


def to_column(rows):
    parts = [
        jnp.sum(jnp.where(eye(), rows[i : i + 1, :], 0.0), axis=1, keepdims=True)
        for i in range(rows.shape[0])
    ]
    return jnp.concatenate(parts, axis=0)


def to_rows(column):
    parts = [
        jnp.sum(jnp.where(eye(), column[i : i + 128, :], 0.0), axis=0, keepdims=True)
        for i in range(0, column.shape[0], 128)
    ]
    return jnp.concatenate(parts, axis=0)


def iota_f32(shape, axis):
    return lax.broadcasted_iota(jnp.int32, shape, axis).astype(F32)


def tiles(extent, most=512):
    return [(start, min(most, extent - start)) for start in range(0, extent, most)]


def layer(
    ways,
    ids_ref, decay_ref, gain_ref, tok, cot, wo, wl, wr, wd, wq, wk, wv, wg,
    out_ref, tg_ref, ffn_out, attn_out, gain_out,
    q, k, v, gate, heads, sq, sk,
    u_in, wo_peer, sum_in, back_in, down_in, mixed_grad, cross, norm_in, turn_in,
    ffn_c, ffn_y, ffn_z, att_c, att_y, att_z, gain_in,
    seg_ref, sums_ref, u_all, wo_own, mixed_out, down_out, hidden, grad_hidden, scale_rows, core_out, gain_sum, turn_out,
    send, recv, dp_send, dp_recv, z_send, z_recv, local, kept,
):
    dp, side = lax.axis_index("dp"), lax.axis_index("tensor")
    core, second, third = lax.rem(dp, 2), lax.rem(lax.div(dp, 2), 2), lax.div(dp, 4)
    rows, features = tok.shape
    width = wq.shape[1]
    units = wl.shape[1]
    half = rows // 2
    thirds = ways // 4
    share = features // ways
    full_inner = float(2 * width)
    own0, other0 = side * half, (1 - side) * half
    across = (dp, 1 - side)
    sibling = (dp + 1 - 2 * core, side)
    beside = (dp + 2 - 4 * second, side)

    def far(hop):
        return (lax.rem(third + hop, thirds) * 4 + second * 2 + core, side)

    def remote(source, target, send_sem, recv_sem, device):
        return pltpu.make_async_remote_copy(
            src_ref=source, dst_ref=target, send_sem=send_sem, recv_sem=recv_sem,
            device_id=device, device_id_type=MESH,
        )

    def over_x(index, source, target):
        return remote(source, target, send.at[index], recv.at[index], across)

    def load(index, source, target):
        copy = pltpu.make_async_copy(source, target, local.at[index])
        copy.start()
        return copy

    def put_turned(target, block, column):
        turned = jnp.transpose(block)
        for owner in range(ways):
            place = (owner % 2) * (ways // 2) + (owner // 2 % 2) * (ways // 4) + owner // 4
            target[place * share : (place + 1) * share, column] = turned[
                owner * share : (owner + 1) * share, :
            ]

    def chunk(part):
        return at(part * BLOCK)

    def u_copy(block):
        return over_x(block, u_all.at[chunk(block), :], u_in.at[chunk(block), :])

    def sum_copy(block):
        return over_x(4 + block, sums_ref.at[block], sum_in.at[block])

    def back_copy(source, part):
        return over_x(11 + part, source.at[chunk(part), :], back_in.at[chunk(part), :])

    def mixed_copy(part):
        return over_x(
            13 + part, mixed_out.at[chunk(part), :], mixed_grad.at[at(own0 + part * BLOCK), :]
        )

    def cross_copy(part):
        mine = cross.at[side * 2 + part]
        return over_x(15 + part, mine, mine)

    def down_copy(part):
        return over_x(17 + part, down_out.at[chunk(part), :], down_in.at[chunk(part), :])

    def norm_copy(source, part):
        return over_x(19 + part, source.at[chunk(part), :], norm_in.at[chunk(part), :])

    def out_copy(source, part):
        return over_x(21 + part, source.at[chunk(part), :], out_ref.at[at(own0 + part * BLOCK), :])

    def tg_copy(source, part):
        return over_x(23 + part, source.at[chunk(part), :], tg_ref.at[at(own0 + part * BLOCK), :])

    odd = lax.rem(third, 2)
    paired = ((third + 1 - 2 * odd) * 4 + second * 2 + core, side)

    def wo_rows(start, size):
        return pl.ds(pl.multiple_of(start, size), size)

    def wo_across():
        place = wo_rows(((core * 2 + second) * 2 + odd) * (width // 8), width // 8)
        return over_x(8, wo.at[place, :], wo_peer.at[place, :])

    def wo_pass(index, place, device):
        piece = wo_peer.at[place, :]
        return remote(piece, piece, send.at[index], recv.at[index], device)

    def wo_paired():
        place = wo_rows(((core * 2 + second) * 2 + odd) * (width // 8), width // 8)
        return wo_pass(26, place, paired)

    def wo_beside():
        return wo_pass(9, wo_rows((core * 2 + second) * (width // 4), width // 4), beside)

    def wo_sibling():
        return wo_pass(10, wo_rows(core * (width // 2), width // 2), sibling)

    def core_copy(first, block, landing, columns):
        return remote(
            core_out.at[:, pl.ds(0, columns)], landing.at[block],
            dp_send.at[0, first + block], dp_recv.at[0, first + block], sibling,
        )

    def second_copy(first, block, summed, landing):
        return remote(
            summed.at[block, at((1 - second) * BLOCK), :], landing.at[block],
            dp_send.at[1, first + block], dp_recv.at[1, first + block], beside,
        )

    def third_copy(first, block, hop, summed, landing):
        piece = pl.ds(pl.multiple_of(lax.rem(third + hop, thirds) * share, share), share)
        return remote(
            summed.at[block, piece, :], landing.at[block, hop - 1],
            z_send.at[first + block, hop - 1], z_recv.at[first + block, hop - 1], far(hop),
        )

    def stage_send(turned, grads, columns, copy):
        def one(part, carry):
            left_op = turned[at((1 - core) * 2 * BLOCK + part * BLOCK), :]
            for start, size in tiles(columns):
                core_out[chunk(part), start : start + size] = nn(
                    left_op, grads[:, start : start + size]
                ).astype(BF16)
            return carry

        lax.fori_loop(0, 2, one, 0)
        copy.start()

    def stage_core(turned, grads, columns, copy, landing, onward):
        copy.wait()

        def one(part, carry):
            left_op = turned[at(core * 2 * BLOCK + part * BLOCK), :]
            for start, size in tiles(columns):
                cut = slice(start, start + size)
                total = nn(left_op, grads[:, cut]) + landing[chunk(part), cut].astype(F32)
                landing[chunk(part), cut] = total.astype(BF16)
            return carry

        lax.fori_loop(0, 2, one, 0)
        onward.start()

    def stage_second(first, block, summed, landing, group_out):
        copy = second_copy(first, block, summed, landing)
        copy.wait()
        for start, size in tiles(landing.shape[2]):
            cut = slice(start, start + size)
            total = (
                summed[block, at(second * BLOCK), cut].astype(F32)
                + landing[block, :, cut].astype(F32)
            )
            landing[block, :, cut] = total.astype(BF16)
        for hop in range(1, thirds):
            third_copy(first, block, hop, landing, group_out).start()

    def stage_third(first, block, summed, landing):
        mine = pl.ds(pl.multiple_of(third * share, share), share)
        total = summed[block, mine, :].astype(F32)
        for hop in range(1, thirds):
            third_copy(first, block, hop, summed, landing).wait()
            total = total + landing[block, hop - 1].astype(F32)
        return total

    def gain_copy(stage, slot, device):
        return remote(
            gain_sum.at[stage], gain_in.at[slot], z_send.at[6, slot], z_recv.at[6, slot], device
        )

    barrier = pltpu.get_barrier_semaphore()
    partners = [across, sibling, beside] + [far(hop) for hop in range(1, thirds)]
    for device in partners:
        pl.semaphore_signal(barrier, inc=1, device_id=device, device_id_type=MESH)

    def seg_lanes(start, size):
        return seg_ref[0:1, pl.ds(pl.multiple_of(start, 128), size)]

    def seg_column(start):
        return to_column(
            jnp.concatenate([seg_lanes(start + i, 128) for i in range(0, BLOCK, 128)], axis=0)
        )

    def gain_lanes(head):
        return gain_ref[head : head + 1, :].astype(F32)

    blocks = rows // BLOCK
    lanes_in = BLOCK // 128

    def lane_column(source, block):
        return to_column(
            jnp.concatenate([source[block, i : i + 1, :] for i in range(lanes_in)], axis=0)
        )

    def middle(lifted, cot_all, turned, w_left, w_right, w_down, hidden_units, back_out, low_turned):
        tok_all = hidden_units.at[2, :, pl.ds(0, features)]
        halves = (pl.ds(0, width), pl.ds(width, width))
        w_query, w_key = (hidden_units.at[0, :, cut] for cut in halves)
        w_value, w_gate = (hidden_units.at[1, :, cut] for cut in halves)
        q_all, gate_all = (turned.at[0, :, cut] for cut in halves)
        slope_q, slope_k = (turned.at[1, :, cut] for cut in halves)
        heads_all = low_turned
        k_all, v_all = (w_down.at[:, cut] for cut in halves)
        k_rows, v_rows = (whole.at[pl.ds(BAND, rows), :] for whole in (k_all, v_all))

        first = [load(0, tok, tok_all), load(1, wk, w_key), load(2, wv, w_value), load(3, wq, w_query), load(4, wg, w_gate)]
        pl.semaphore_wait(barrier, len(partners))
        wo_across().start()
        pad = jnp.full((1, BAND), -1.0, F32)
        seg_ref[0:1, :BAND] = pad
        seg_ref[0:1, BAND + rows :] = pad
        seg_ref[0:1, BAND : BAND + rows] = ids_ref[...].astype(F32)
        for padded in (k_all, v_all):
            padded[:BAND, :] = jnp.zeros((BAND, width), BF16)
        for copy in first:
            copy.wait()
        later = [load(5, wo, wo_own), load(6, cot, cot_all), load(7, wl, w_left), load(8, wr, w_right)]
        keeps = [(q_all, q), (k_rows, k), (v_rows, v), (gate_all, gate), (slope_q, sq), (slope_k, sk), (heads_all, heads)]

        def forward_block(block, carry):
            place = chunk(block)
            here = pl.ds(pl.multiple_of(BAND + block * BLOCK, 128), BLOCK)
            span = pl.ds(pl.multiple_of(block * BLOCK, BLOCK), SPAN)
            source = tok_all[place, :].astype(F32)
            normed = (source * rms_scale(source)).astype(BF16)
            for weight, slope, target, rows_at in ((w_key, slope_k, k_all, here), (w_query, slope_q, q_all, place)):
                pre = nn(normed, weight[...])
                sigma = jax.nn.sigmoid(pre)
                target[rows_at, :] = (pre * sigma).astype(BF16)
                slope[place, :] = (sigma * (1.0 + pre * (1.0 - sigma))).astype(BF16)
            v_all[here, :] = nn(normed, w_value[...]).astype(BF16)
            gate_all[place, :] = nn(normed, w_gate[...]).astype(BF16)
            row_at = iota_f32((BLOCK, 1), 0)
            key_at = iota_f32((1, SPAN), 1) - float(BAND)
            allowed = (seg_column(BAND + block * BLOCK) == seg_lanes(block * BLOCK, SPAN)) & (
                row_at >= key_at
            )
            total = jnp.zeros((BLOCK, 1), F32)
            for head in range(width // 128):
                lanes = slice(head * 128, head * 128 + 128)
                decay = decay_ref[head]
                falloff = jnp.exp(-decay * row_at) * jnp.exp(decay * key_at)
                scores = nt(q_all[place, lanes], k_all[span, lanes])
                weighted = jnp.where(allowed, scores * falloff, 0.0).astype(BF16)
                found = nn(weighted, v_all[span, lanes])
                total = total + jnp.sum(found * found, axis=1, keepdims=True)
                heads_all[place, lanes] = found.astype(BF16)
                u_all[place, lanes] = (
                    found * gain_lanes(head) * gate_all[place, lanes].astype(F32)
                ).astype(BF16)
            lane_rows = to_rows(total)
            for i in range(lanes_in):
                sums_ref[block, i : i + 1, :] = lane_rows[i : i + 1, :]
            u_copy(block).start()
            sum_copy(block).start()
            for index, (source, target) in enumerate(keeps):
                pltpu.make_async_copy(
                    source.at[place, :], target.at[place, :], kept.at[index]
                ).start()

            @pl.when(block == 0)
            def _():
                wo_across().wait()
                wo_paired().start()

            @pl.when(block == 1)
            def _():
                wo_paired().wait()
                wo_beside().start()

            @pl.when(block == blocks - 1)
            def _():
                wo_beside().wait()
                wo_sibling().start()

            return carry

        lax.fori_loop(0, blocks, forward_block, 0)
        for index, (source, target) in enumerate(keeps):
            pltpu.make_async_copy(source, target, kept.at[index]).wait()
        later.append(load(9, wd, w_down))
        for copy in later:
            copy.wait()
        wo_sibling().wait()

        def gated(step, carry):
            block = lax.rem(step + 1 - side, blocks)
            part = lax.rem(block, 2)
            owned = lax.div(block, 2) == side
            place = chunk(block)
            u_copy(block).wait()
            sum_copy(block).wait()
            for i in range(lanes_in):
                scale_rows[block, i : i + 1, :] = lax.rsqrt(
                    (sums_ref[block, i : i + 1, :] + sum_in[block, i : i + 1, :]) / full_inner + eps
                )
            attn = nn(u_all[place, :], wo_own[...]) + nn(u_in[place, :], wo_peer[...])
            state = tok_all[place, :].astype(F32) + lane_column(scale_rows, block) * attn
            rows_in = (state * rms_scale(state)).astype(BF16)
            lifted[...] = rows_in

            @pl.when(owned)
            def _():
                hidden[chunk(part), :] = state

            rows_cot = cot_all[place, :]
            for start, size in tiles(units):
                cut = slice(start, start + size)
                left = nn(lifted[...], w_left[:, cut])
                right = nn(lifted[...], w_right[:, cut])
                grad = nt(rows_cot, w_down[cut, :])
                hidden_units[2, place, cut] = (left * right).astype(BF16)
                hidden_units[0, place, cut] = (grad * right).astype(BF16)
                hidden_units[1, place, cut] = (grad * left).astype(BF16)
            back = nt(hidden_units[0, place, :], w_left[...]) + nt(
                hidden_units[1, place, :], w_right[...]
            )

            @pl.when(owned)
            def _():
                grad_hidden[chunk(part), :] = back

            @pl.when(jnp.logical_not(owned))
            def _():
                back_out[chunk(part), :] = back.astype(BF16)
                back_copy(back_out, part).start()

            put_turned(turned.at[0], rows_in, place)
            put_turned(turned.at[1], rows_cot, place)
            return carry

        lax.fori_loop(0, blocks, gated, 0)

        def down_other(part, carry):
            down_out[chunk(part), :] = nn(
                hidden_units[2, at(other0 + part * BLOCK), :], w_down[...]
            ).astype(BF16)
            return carry

        lax.fori_loop(0, 2, down_other, 0)

        def block_step(block, carry):
            lhs, rhs = turned.at[lax.div(block, 2)], hidden_units.at[block]
            first = core_copy(0, block, ffn_c, units)
            stage_send(lhs, rhs, units, first)

            @pl.when(block < 2)
            def _():
                part = block
                back_copy(back_out, part).wait()
                state = hidden[chunk(part), :]
                pulled = grad_hidden[chunk(part), :] + back_in[chunk(part), :].astype(F32)
                grad = cot_all[at(own0 + part * BLOCK), :].astype(F32) + rms_back(
                    state, rms_scale(state), pulled
                )
                grad_hidden[chunk(part), :] = grad
                low = grad.astype(BF16)
                for_own = nt(low, wo_own[...])
                for_peer = nt(low, wo_peer[...])
                mixed_out[chunk(part), :] = for_peer.astype(BF16)
                mixed_grad[at(own0 + part * BLOCK), :] = for_own.astype(BF16)
                mixed_copy(part).start()
                place = at(own0 + part * BLOCK)
                both = jnp.sum(
                    u_all[place, :].astype(F32) * for_own + u_in[place, :].astype(F32) * for_peer,
                    axis=1,
                    keepdims=True,
                )
                lanes = to_rows(both)
                for i in range(lanes_in):
                    cross[side * 2 + part, i : i + 1, :] = lanes[i : i + 1, :]
                cross_copy(part).start()
                put_turned(low_turned, low, chunk(part))
                scale = lane_column(scale_rows, side * 2 + part)
                back_out[chunk(part), :width] = (u_all[place, :].astype(F32) * scale).astype(BF16)
                back_out[chunk(part), width:] = (u_in[place, :].astype(F32) * scale).astype(BF16)

                @pl.when(part == 1)
                def _():
                    down_copy(0).start()
                    down_copy(1).start()

            stage_core(
                lhs, rhs, units, first, ffn_c.at[block], second_copy(0, block, ffn_c, ffn_y)
            )
            return carry

        lax.fori_loop(0, 2, block_step, 0)
        columns = 2 * width
        first = core_copy(3, 0, att_c, columns)
        stage_send(low_turned, back_out, columns, first)
        stage_core(low_turned, back_out, columns, first, att_c.at[0], second_copy(3, 0, att_c, att_y))
        lax.fori_loop(2, 3, block_step, 0)

        def down_own(part, carry):
            hidden[chunk(part), :] += nn(
                hidden_units[2, at(own0 + part * BLOCK), :], w_down[...]
            )
            return carry

        lax.fori_loop(0, 2, down_own, 0)
        stage_second(0, 0, ffn_c, ffn_y, ffn_z)

    pl.run_scoped(
        middle,
        pltpu.VMEM((BLOCK, features), BF16),
        pltpu.VMEM((rows, features), BF16),
        pltpu.VMEM((2, features, rows), BF16),
        pltpu.VMEM((features, units), BF16),
        pltpu.VMEM((features, units), BF16),
        pltpu.VMEM((units, features), BF16),
        pltpu.VMEM((3, rows, units), BF16),
        pltpu.VMEM((half, features), BF16),
        pltpu.VMEM((features, half), BF16),
    )

    def last(q_all, grads, k_all, v_all, slope_q, slope_k, heads_all, gate_all, pulls, weights, norm_out, norm_own, results, turned, tok_all, ffn_ref, attn_ref):
        columns = 2 * width
        loads = [
            load(0, v, v_all.at[pl.ds(BAND, rows), :]),
            load(1, k, k_all.at[pl.ds(BAND, rows), :]),
            load(2, q, q_all.at[pl.ds(0, rows), :]),
            load(3, gate, gate_all),
            load(4, heads, heads_all),
            load(5, sq, slope_q),
            load(6, sk, slope_k),
        ]
        later = [load(7, tok, tok_all)] + [
            load(8 + i, source, weights.at[:, pl.ds(i * width, width)])
            for i, source in enumerate((wq, wk, wv, wg))
        ]
        for padded in (k_all, v_all):
            padded[:BAND, :] = jnp.zeros((BAND, width), BF16)
        for padded in (q_all, grads):
            padded[rows:, :] = jnp.zeros((BAND, width), BF16)
        gain_sum[0] = jnp.zeros(gain_sum.shape[1:], F32)
        for copy in loads:
            copy.wait()
        for part in range(2):
            mixed_copy(part).wait()
            cross_copy(part).wait()

        gain_row = jnp.concatenate([gain_lanes(i) for i in range(width // 128)], axis=1)

        def prepare(block, carry):
            place = chunk(block)
            scale = lane_column(scale_rows, block)
            joint = lane_column(cross, block)
            grad = mixed_grad[place, :].astype(F32)
            head_rows = heads_all[place, :].astype(F32)
            gain = gain_row
            scaled = grad * gate_all[place, :].astype(F32)
            unit = head_rows * scale
            gain_sum[0, 0:1, :] += jnp.sum(scaled * unit, axis=0, keepdims=True)
            pulls[1, place, width:] = (grad * (unit * gain)).astype(BF16)
            grads[place, :] = (
                scale * (scaled * gain)
                - head_rows * (scale * scale * scale) * (joint / full_inner)
            ).astype(BF16)
            return carry

        lax.fori_loop(0, rows // BLOCK, prepare, 0)
        gain_copy(0, 0, sibling).start()
        stage_second(0, 1, ffn_c, ffn_y, ffn_z)

        def by_query(block, carry):
            place, span = chunk(block), pl.ds(pl.multiple_of(block * BLOCK, BLOCK), SPAN)
            row_at = iota_f32((BLOCK, 1), 0)
            key_at = iota_f32((1, SPAN), 1) - float(BAND)
            allowed = (seg_column(BAND + block * BLOCK) == seg_lanes(block * BLOCK, SPAN)) & (
                row_at >= key_at
            )
            for head in range(width // 128):
                lanes = slice(head * 128, head * 128 + 128)
                decay = decay_ref[head]
                falloff = jnp.exp(-decay * row_at) * jnp.exp(decay * key_at)
                grad = nt(grads[place, lanes], v_all[span, lanes])
                grad = jnp.where(allowed, grad * falloff, 0.0).astype(BF16)
                pulls[0, place, lanes] = (
                    nn(grad, k_all[span, lanes]) * slope_q[place, lanes].astype(F32)
                ).astype(BF16)
            return carry

        def finish_out(part, carry):
            down_copy(part).wait()
            results[0, chunk(part), :] = (
                hidden[chunk(part), :] + down_in[chunk(part), :].astype(F32)
            ).astype(BF16)
            out_copy(results.at[0], part).start()
            pltpu.make_async_copy(
                results.at[0, chunk(part), :], out_ref.at[at(own0 + part * BLOCK), :], local.at[part]
            ).start()
            return carry

        lax.fori_loop(0, rows // BLOCK, by_query, 0)
        lax.fori_loop(0, 1, finish_out, 0)

        def by_key(block, carry):
            place, span = chunk(block), pl.ds(pl.multiple_of(block * BLOCK, BLOCK), SPAN)
            here = pl.ds(pl.multiple_of(BAND + block * BLOCK, 128), BLOCK)
            key_at = iota_f32((BLOCK, 1), 0)
            row_at = iota_f32((1, SPAN), 1)
            allowed = (
                seg_column(BAND + block * BLOCK) == seg_lanes(BAND + block * BLOCK, SPAN)
            ) & (row_at >= key_at)
            for head in range(width // 128):
                lanes = slice(head * 128, head * 128 + 128)
                turned_lanes = slice(width + head * 128, width + head * 128 + 128)
                decay = decay_ref[head]
                falloff = jnp.exp(decay * key_at) * jnp.exp(-decay * row_at)
                span_q, span_grad = q_all[span, lanes], grads[span, lanes]
                scores = nt(k_all[here, lanes], span_q)
                weighted = jnp.where(allowed, scores * falloff, 0.0).astype(BF16)
                pulls[1, place, lanes] = nn(weighted, span_grad).astype(BF16)
                grad = nt(v_all[here, lanes], span_grad)
                grad = jnp.where(allowed, grad * falloff, 0.0).astype(BF16)
                pulls[0, place, turned_lanes] = (
                    nn(grad, span_q) * slope_k[place, lanes].astype(F32)
                ).astype(BF16)
            return carry

        lax.fori_loop(0, rows // BLOCK, by_key, 0)
        lax.fori_loop(1, 2, finish_out, 0)
        stage_second(3, 0, att_c, att_y, att_z)
        for copy in later:
            copy.wait()

        def normed_part(step, carry):
            part = lax.rem(step, 2)
            place = at((1 - side + lax.div(step, 2) * (2 * side - 1)) * half + part * BLOCK)
            back = nt(pulls[0, place, :], weights[:, :columns]) + nt(
                pulls[1, place, :], weights[:, columns:]
            )

            @pl.when(step < 2)
            def _():
                norm_out[chunk(part), :] = back.astype(BF16)
                norm_copy(norm_out, part).start()

            @pl.when(step >= 2)
            def _():
                norm_own[chunk(part), :] = back

            return carry

        lax.fori_loop(0, 4, normed_part, 0)


        def turn(block, carry):
            source = tok_all[chunk(block), :].astype(F32)
            put_turned(turned, (source * rms_scale(source)).astype(BF16), chunk(block))
            return carry

        lax.fori_loop(0, rows // BLOCK, turn, 0)

        gain_copy(0, 0, sibling).wait()
        gain_sum[1] = gain_sum[0] + gain_in[0]
        gain_copy(1, 1, beside).start()

        def block_step(step, carry):
            block = step + 1
            rhs = pulls.at[step]
            first = core_copy(3, block, att_c, columns)
            stage_send(turned, rhs, columns, first)
            stage_core(
                turned, rhs, columns, first, att_c.at[block], second_copy(3, block, att_c, att_y)
            )

            @pl.when(step == 0)
            def _():
                stage_second(0, 2, ffn_c, ffn_y, ffn_z)

            return carry

        lax.fori_loop(0, 2, block_step, 0)
        gain_copy(1, 1, beside).wait()
        gain_sum[2] = gain_sum[1] + gain_in[1]
        for hop in range(1, thirds):
            gain_copy(2, 1 + hop, far(hop)).start()

        def attn_copy(block):
            return pltpu.make_async_copy(attn_ref.at[block], attn_out.at[block], local.at[7 + block])

        def attn_total(block, carry):
            attn_ref[block] = stage_third(3, block, att_y, att_z)

            @pl.when(block > 0)
            def _():
                attn_copy(block).start()

            return carry

        lax.fori_loop(0, 1, attn_total, 0)
        turn_out[...] = attn_ref[0, :, width:].astype(BF16)
        turn_copy = over_x(25, turn_out, turn_in)
        turn_copy.start()

        def finish_tokens(part, carry):
            norm_copy(norm_out, part).wait()
            pulled = norm_own[chunk(part), :] + norm_in[chunk(part), :].astype(F32)
            source = tok_all[at(own0 + part * BLOCK), :].astype(F32)
            results[1, chunk(part), :] = (
                grad_hidden[chunk(part), :] + rms_back(source, rms_scale(source), pulled)
            ).astype(BF16)
            tg_copy(results.at[1], part).start()
            pltpu.make_async_copy(
                results.at[1, chunk(part), :], tg_ref.at[at(own0 + part * BLOCK), :], local.at[2 + part]
            ).start()
            return carry

        lax.fori_loop(0, 2, finish_tokens, 0)

        def seconds_last(block, carry):
            stage_second(3, block, att_c, att_y, att_z)
            return carry

        lax.fori_loop(1, 3, seconds_last, 0)

        def ffn_total(block, carry):
            ffn_ref[block] = stage_third(0, block, ffn_y, ffn_z)
            pltpu.make_async_copy(ffn_ref.at[block], ffn_out.at[block], local.at[4 + block]).start()
            return carry

        lax.fori_loop(0, 3, ffn_total, 0)
        lax.fori_loop(1, 3, attn_total, 0)
        total = gain_sum[2]
        for hop in range(1, thirds):
            gain_copy(2, 1 + hop, far(hop)).wait()
            total = total + gain_in[1 + hop]
        gain_out[...] = total
        turn_copy.wait()
        attn_ref[0, :, :width] += turn_in[...].astype(F32)
        attn_copy(0).start()

        def close(part, carry):
            out_copy(results.at[0], part).wait()
            tg_copy(results.at[1], part).wait()
            for index, target in ((0, out_ref), (1, tg_ref)):
                pltpu.make_async_copy(
                    results.at[index, chunk(part), :],
                    target.at[at(own0 + part * BLOCK), :],
                    local.at[2 * index + part],
                ).wait()
            return carry

        lax.fori_loop(0, 2, close, 0)
        for block in range(3):
            pltpu.make_async_copy(ffn_ref.at[block], ffn_out.at[block], local.at[4 + block]).wait()
            attn_copy(block).wait()

    pl.run_scoped(
        last,
        pltpu.VMEM((rows + BAND, width), BF16),
        pltpu.VMEM((rows + BAND, width), BF16),
        pltpu.VMEM((rows + BAND, width), BF16),
        pltpu.VMEM((rows + BAND, width), BF16),
        pltpu.VMEM((rows, width), BF16),
        pltpu.VMEM((rows, width), BF16),
        pltpu.VMEM((rows, width), BF16),
        pltpu.VMEM((rows, width), BF16),
        pltpu.VMEM((2, rows, 2 * width), BF16),
        pltpu.VMEM((features, 4 * width), BF16),
        pltpu.VMEM((half, features), BF16),
        pltpu.VMEM((half, features), F32),
        pltpu.VMEM((2, half, features), BF16),
        pltpu.VMEM((features, rows), BF16),
        pltpu.VMEM((rows, features), BF16),
        pltpu.VMEM(ffn_out.shape, F32),
        pltpu.VMEM(attn_out.shape, F32),
    )


def run_layer(ways, *args):
    (ids, decays, gain, tok, cot, wo, wl, wr, wd, wq) = args[:10]
    rows, features = tok.shape
    width, units = wq.shape[1], wl.shape[1]
    half, thirds, share = rows // 2, ways // 4, features // ways
    quarter = features // 4
    lane_rows = (rows // BLOCK, 8, 128)
    vmem = pl.BlockSpec(memory_space=pltpu.VMEM)
    hbm = pl.BlockSpec(memory_space=pl.ANY)
    shape = jax.ShapeDtypeStruct
    scratch = [
        ((rows, width), BF16), ((width, features), BF16), (lane_rows, F32),
        ((half, features), BF16), ((half, features), BF16),
        ((rows, width), BF16), (lane_rows, F32), ((half, features), BF16), ((share, width), BF16),
        ((3, 2 * quarter, units), BF16), ((3, quarter, units), BF16),
        ((3, thirds - 1, share, units), BF16),
        ((3, 2 * quarter, 2 * width), BF16), ((3, quarter, 2 * width), BF16),
        ((3, thirds - 1, share, 2 * width), BF16), ((thirds + 1, 8, width), F32),
        ((1, rows + 2 * BAND), F32), (lane_rows, F32), ((rows, width), BF16),
        ((width, features), BF16), ((half, width), BF16),
        ((half, features), BF16), ((half, features), F32), ((half, features), F32),
        (lane_rows, F32), ((2 * quarter, max(units, 2 * width)), BF16), ((3, 8, width), F32),
        ((share, width), BF16),
    ]
    return pl.pallas_call(
        functools.partial(layer, ways),
        in_specs=[vmem, pl.BlockSpec(memory_space=pltpu.SMEM), vmem] + [hbm] * (len(args) - 3),
        out_specs=[hbm] * 4 + [vmem] + [hbm] * 7,
        out_shape=[
            shape((rows, features), BF16), shape((rows, features), BF16),
            shape((3, share, units), F32), shape((3, share, 2 * width), F32), shape((8, width), F32),
        ]
        + [shape((rows, width), BF16)] * 7,
        scratch_shapes=[pltpu.VMEM(size, dtype) for size, dtype in scratch]
        + [
            pltpu.SemaphoreType.DMA((27,)), pltpu.SemaphoreType.DMA((27,)),
            pltpu.SemaphoreType.DMA((2, 6)), pltpu.SemaphoreType.DMA((2, 6)),
            pltpu.SemaphoreType.DMA((7, thirds + 1)), pltpu.SemaphoreType.DMA((7, thirds + 1)),
            pltpu.SemaphoreType.DMA((12,)), pltpu.SemaphoreType.DMA((7,)),
        ],
        compiler_params=pltpu.CompilerParams(
            collective_id=1, has_side_effects=True, vmem_limit_bytes=VMEM_LIMIT
        ),
        cost_estimate=pl.CostEstimate(flops=5 * 10**10, bytes_accessed=60 * 2**20, transcendentals=10**6),
        name="layer",
    )(*args)


def finish(
    ways, out_in, tg_in, ffn, attn, gain_in,
    out, tg, query, key, value, gate, output, gain, left, right, down,
    out_held, tg_low, tg_wide, ffn_held, attn_held, arrived, left_here,
):
    width = query.shape[1]
    blocks = 2
    size = tg.shape[0] // blocks
    places = [pl.ds(i * size, size) for i in range(blocks)]
    pairs = [(tg_in.at[i, :], tg_low.at[i, :], tg_wide.at[i, :], tg.at[i, :]) for i in places]
    pairs += [(out_in.at[i, :], out_held.at[i, :], out_held.at[i, :], out.at[i, :]) for i in places]
    for i, target in enumerate((left, right, down)):
        pairs.append((ffn.at[i], ffn_held.at[i], ffn_held.at[i], target))
    for i, j, target in ((1, 0, query), (1, 1, key), (2, 0, value), (2, 1, gate), (0, 0, output)):
        cut = pl.ds(j * width, width)
        held = attn_held.at[i, :, cut]
        pairs.append((attn.at[i, :, cut], held, held, target))
    loads = [
        pltpu.make_async_copy(source, held, arrived.at[i])
        for i, (source, held, _, _) in enumerate(pairs)
    ]
    stores = [
        pltpu.make_async_copy(held, target, left_here.at[i])
        for i, (_, _, held, target) in enumerate(pairs)
    ]
    for copy in loads:
        copy.start()
    heads, each = gain.shape
    rows_in = jnp.concatenate([gain_in[0:1, i * 128 : i * 128 + 128] for i in range(heads)], axis=0)
    lane = lax.broadcasted_iota(jnp.int32, rows_in.shape, 1)
    place = lax.broadcasted_iota(jnp.int32, gain.shape, 1)
    first = lax.axis_index("dp") * each
    found = jnp.zeros(gain.shape, F32)
    for i in range(each):
        column = jnp.sum(jnp.where(lane == first + i, rows_in, 0.0), axis=1, keepdims=True)
        found = jnp.where(place == i, column, found)
    gain[...] = found
    for i in range(len(pairs)):
        loads[i].wait()
        if i < blocks:
            tg_wide[places[i], :] = tg_low[places[i], :].astype(F32)
        stores[i].start()
    for copy in stores:
        copy.wait()


def run_finish(ways, heads, out_in, tg_in, ffn, attn, gain_in):
    rows, features = tg_in.shape
    share, units, width = ffn.shape[1], ffn.shape[2], attn.shape[2] // 2
    vmem = pl.BlockSpec(memory_space=pltpu.VMEM)
    hbm = pl.BlockSpec(memory_space=pl.ANY)
    shape = lambda *size: jax.ShapeDtypeStruct(size, F32)
    copies = 12
    return pl.pallas_call(
        functools.partial(finish, ways),
        in_specs=[hbm] * 4 + [vmem],
        out_specs=[hbm] * 7 + [vmem] + [hbm] * 3,
        out_shape=[jax.ShapeDtypeStruct((rows, features), BF16), shape(rows, features)]
        + [shape(share, width)] * 5
        + [shape(heads, gain_in.shape[1] // heads // ways)]
        + [shape(share, units)] * 3,
        scratch_shapes=[
            pltpu.VMEM((rows, features), BF16), pltpu.VMEM((rows, features), BF16),
            pltpu.VMEM((rows, features), F32), pltpu.VMEM((3, share, units), F32),
            pltpu.VMEM((3, share, 2 * width), F32),
            pltpu.SemaphoreType.DMA((copies,)), pltpu.SemaphoreType.DMA((copies,)),
        ],
        compiler_params=pltpu.CompilerParams(vmem_limit_bytes=VMEM_LIMIT),
        name="finish",
    )(out_in, tg_in, ffn, attn, gain_in)


def local(
    ways, tokens, segment_ids, decay_rate, query_weight, key_weight, value_weight, gate_weight,
    output_weight, norm_gain, left_weight, right_weight, down_weight, cotangent,
):
    held = run_layer(
        ways, segment_ids, decay_rate, norm_gain, tokens, cotangent, output_weight,
        left_weight, right_weight, down_weight, query_weight, key_weight, value_weight, gate_weight,
    )[:5]
    results = list(run_finish(ways, norm_gain.shape[0], *held))
    for turned in (6, 10):
        results[turned] = results[turned].T
    return tuple(results)


def solution(mesh):
    dp, tensor = "dp", "tensor"
    in_specs = (
        P(dp, None), P(dp, None), P(tensor), P(None, tensor), P(None, tensor), P(None, tensor),
        P(None, tensor), P(tensor, None), P(tensor, None), P(None, tensor), P(None, tensor),
        P(tensor, None), P(dp, None),
    )
    out_specs = (
        P(dp, None), P(dp, None), P(dp, tensor), P(dp, tensor), P(dp, tensor), P(dp, tensor),
        P(tensor, dp), P(tensor, dp), P(dp, tensor), P(dp, tensor), P(tensor, dp),
    )
    return jax.shard_map(
        functools.partial(local, mesh.shape[dp]),
        mesh=mesh, in_specs=in_specs, out_specs=out_specs, check_vma=False,
    )
```

```python
import functools

import jax
import jax.numpy as jnp
from jax import lax
from jax.experimental import pallas as pl
from jax.experimental.pallas import tpu as pltpu
from jax.sharding import PartitionSpec as P

MESH = pl.DeviceIdType.MESH
eps = 1e-06
BAND = 384
BLOCK = 256
SPAN = BAND + BLOCK
F32 = jnp.float32
BF16 = jnp.bfloat16
VMEM_LIMIT = 62 * 1024 * 1024


def nn(left_op, right_op):
    return jnp.dot(left_op, right_op, preferred_element_type=F32)


def nt(left_op, right_op):
    return lax.dot_general(
        left_op, right_op, (((1,), (1,)), ((), ())), preferred_element_type=F32
    )


def at(start):
    return pl.ds(pl.multiple_of(start, BLOCK), BLOCK)


def rms_scale(values):
    return lax.rsqrt(jnp.mean(values * values, axis=1, keepdims=True) + eps)


def rms_back(values, scale, grads):
    return scale * grads - values * (scale * scale * scale) * jnp.mean(
        values * grads, axis=1, keepdims=True
    )


def eye():
    shape = (128, 128)
    return lax.broadcasted_iota(jnp.int32, shape, 0) == lax.broadcasted_iota(jnp.int32, shape, 1)


def to_column(rows):
    parts = [
        jnp.sum(jnp.where(eye(), rows[i : i + 1, :], 0.0), axis=1, keepdims=True)
        for i in range(rows.shape[0])
    ]
    return jnp.concatenate(parts, axis=0)


def to_rows(column):
    parts = [
        jnp.sum(jnp.where(eye(), column[i : i + 128, :], 0.0), axis=0, keepdims=True)
        for i in range(0, column.shape[0], 128)
    ]
    return jnp.concatenate(parts, axis=0)


def iota_f32(shape, axis):
    return lax.broadcasted_iota(jnp.int32, shape, axis).astype(F32)


def tiles(extent, most=512):
    return [(start, min(most, extent - start)) for start in range(0, extent, most)]


def layer(
    ways,
    ids_ref, decay_ref, gain_ref, tok, cot, wo, wl, wr, wd, wq, wk, wv, wg,
    out_ref, tg_ref, ffn_out, attn_out, gain_out,
    q, k, v, gate, heads, sq, sk,
    u_in, wo_peer, sum_in, back_in, down_in, mixed_grad, cross, norm_in, turn_in,
    ffn_c, ffn_y, ffn_z, att_c, att_y, att_z, gain_in,
    seg_ref, sums_ref, u_all, wo_own, mixed_out, down_out, hidden, grad_hidden, scale_rows, core_out, gain_sum, turn_out,
    send, recv, dp_send, dp_recv, z_send, z_recv, local, kept,
):
    dp, side = lax.axis_index("dp"), lax.axis_index("tensor")
    core, second, third = lax.rem(dp, 2), lax.rem(lax.div(dp, 2), 2), lax.div(dp, 4)
    rows, features = tok.shape
    width = wq.shape[1]
    units = wl.shape[1]
    half = rows // 2
    thirds = ways // 4
    share = features // ways
    full_inner = float(2 * width)
    own0, other0 = side * half, (1 - side) * half
    across = (dp, 1 - side)
    sibling = (dp + 1 - 2 * core, side)
    beside = (dp + 2 - 4 * second, side)

    def far(hop):
        return (lax.rem(third + hop, thirds) * 4 + second * 2 + core, side)

    def remote(source, target, send_sem, recv_sem, device):
        return pltpu.make_async_remote_copy(
            src_ref=source, dst_ref=target, send_sem=send_sem, recv_sem=recv_sem,
            device_id=device, device_id_type=MESH,
        )

    def over_x(index, source, target):
        return remote(source, target, send.at[index], recv.at[index], across)

    def load(index, source, target):
        copy = pltpu.make_async_copy(source, target, local.at[index])
        copy.start()
        return copy

    def put_turned(target, block, column):
        turned = jnp.transpose(block)
        for owner in range(ways):
            place, left = 0, owner
            for _ in range(ways.bit_length() - 1):
                place, left = place * 2 + left % 2, left // 2
            target[place * share : (place + 1) * share, column] = turned[
                owner * share : (owner + 1) * share, :
            ]

    def chunk(part):
        return at(part * BLOCK)

    def u_copy(block):
        return over_x(block, u_all.at[chunk(block), :], u_in.at[chunk(block), :])

    def sum_copy(block):
        return over_x(4 + block, sums_ref.at[block], sum_in.at[block])

    def back_copy(source, part):
        return over_x(11 + part, source.at[chunk(part), :], back_in.at[chunk(part), :])

    def mixed_copy(part):
        return over_x(
            13 + part, mixed_out.at[chunk(part), :], mixed_grad.at[at(own0 + part * BLOCK), :]
        )

    def cross_copy(part):
        mine = cross.at[side * 2 + part]
        return over_x(15 + part, mine, mine)

    def down_copy(part):
        return over_x(17 + part, down_out.at[chunk(part), :], down_in.at[chunk(part), :])

    def norm_copy(source, part):
        return over_x(19 + part, source.at[chunk(part), :], norm_in.at[chunk(part), :])

    def out_copy(source, part):
        return over_x(21 + part, source.at[chunk(part), :], out_ref.at[at(own0 + part * BLOCK), :])

    def tg_copy(source, part):
        return over_x(23 + part, source.at[chunk(part), :], tg_ref.at[at(own0 + part * BLOCK), :])

    odd = lax.rem(third, 2)
    paired = ((third + 1 - 2 * odd) * 4 + second * 2 + core, side)

    def wo_rows(start, size):
        return pl.ds(pl.multiple_of(start, size), size)

    def wo_across():
        place = wo_rows(((core * 2 + second) * 2 + odd) * (width // 8), width // 8)
        return over_x(8, wo.at[place, :], wo_peer.at[place, :])

    def wo_pass(index, place, device):
        piece = wo_peer.at[place, :]
        return remote(piece, piece, send.at[index], recv.at[index], device)

    def wo_paired():
        place = wo_rows(((core * 2 + second) * 2 + odd) * (width // 8), width // 8)
        return wo_pass(26, place, paired)

    def wo_beside():
        return wo_pass(9, wo_rows((core * 2 + second) * (width // 4), width // 4), beside)

    def wo_sibling():
        return wo_pass(10, wo_rows(core * (width // 2), width // 2), sibling)

    def section(part):
        return chunk(1 - second + part * (2 * second - 1))

    def core_copy(first, block, landing, columns, part):
        return remote(
            core_out.at[section(part), pl.ds(0, columns)], landing.at[block, section(part), :],
            dp_send.at[part, first + block], dp_recv.at[part, first + block], sibling,
        )

    def second_copy(first, block, summed, landing):
        return remote(
            summed.at[block, at((1 - second) * BLOCK), :], landing.at[block],
            dp_send.at[2, first + block], dp_recv.at[2, first + block], beside,
        )

    levels = thirds.bit_length() - 1

    def third_bit(level):
        return lax.rem(lax.div(third, 2**level), 2)

    def third_start(level):
        return BLOCK - (BLOCK >> level)

    def third_rows(level, bit):
        size = BLOCK >> (level + 1)
        start = bit * size + (third_start(level - 1) if level else 0)
        return pl.ds(pl.multiple_of(start, size), size)

    def third_source(level, summed, landing):
        return landing if level else summed

    def third_copy(first, block, level, summed, landing):
        bit = third_bit(level)
        other = third + (1 - 2 * bit) * 2**level
        return remote(
            third_source(level, summed, landing).at[block, third_rows(level, 1 - bit), :],
            landing.at[block, pl.ds(third_start(level), BLOCK >> (level + 1)), :],
            z_send.at[first + block, level], z_recv.at[first + block, level],
            (other * 4 + second * 2 + core, side),
        )

    def stage_send(turned, grads, first, block, landing, columns):
        def one(part, carry):
            place = section(part)
            left_op = turned[pl.ds(pl.multiple_of((1 - core) * 2 * BLOCK + place.start, BLOCK), BLOCK), :]
            for start, size in tiles(columns):
                core_out[place, start : start + size] = nn(
                    left_op, grads[:, start : start + size]
                ).astype(BF16)
            core_copy(first, block, landing, columns, part).start()
            return carry

        lax.fori_loop(0, 2, one, 0)

    def stage_core(turned, grads, first, block, landing, columns, onward):
        def one(part, carry):
            place = section(part)
            left_op = turned[pl.ds(pl.multiple_of(core * 2 * BLOCK + place.start, BLOCK), BLOCK), :]
            core_copy(first, block, landing, columns, part).wait()
            for start, size in tiles(columns):
                cut = slice(start, start + size)
                total = nn(left_op, grads[:, cut]) + landing[block, place, cut].astype(F32)
                landing[block, place, cut] = total.astype(BF16)

            @pl.when(part == 0)
            def _():
                onward.start()

            return carry

        lax.fori_loop(0, 2, one, 0)

    def stage_second(first, block, summed, landing, group_out):
        copy = second_copy(first, block, summed, landing)
        copy.wait()
        for start, size in tiles(landing.shape[2]):
            cut = slice(start, start + size)
            total = (
                summed[block, at(second * BLOCK), cut].astype(F32)
                + landing[block, :, cut].astype(F32)
            )
            landing[block, :, cut] = total.astype(BF16)
        third_copy(first, block, 0, landing, group_out).start()

    def third_total(first, block, level, summed, landing):
        third_copy(first, block, level, summed, landing).wait()
        kept_rows = third_source(level, summed, landing)[
            block, third_rows(level, third_bit(level)), :
        ]
        here = pl.ds(third_start(level), BLOCK >> (level + 1))
        return kept_rows.astype(F32) + landing[block, here, :].astype(F32)

    def stage_pass(first, block, summed, landing):
        for level in range(levels - 1):
            here = pl.ds(third_start(level), BLOCK >> (level + 1))
            landing[block, here, :] = third_total(first, block, level, summed, landing).astype(BF16)
            third_copy(first, block, level + 1, summed, landing).start()

    def stage_third(first, block, summed, landing):
        return third_total(first, block, levels - 1, summed, landing)

    def gain_copy(stage, slot, device):
        return remote(
            gain_sum.at[stage], gain_in.at[slot], z_send.at[6, slot], z_recv.at[6, slot], device
        )

    barrier = pltpu.get_barrier_semaphore()
    partners = [across, sibling, beside] + [far(hop) for hop in range(1, thirds)]
    for device in partners:
        pl.semaphore_signal(barrier, inc=1, device_id=device, device_id_type=MESH)

    def seg_lanes(start, size):
        return seg_ref[0:1, pl.ds(pl.multiple_of(start, 128), size)]

    def seg_column(start):
        return to_column(
            jnp.concatenate([seg_lanes(start + i, 128) for i in range(0, BLOCK, 128)], axis=0)
        )

    def gain_lanes(head):
        return gain_ref[head : head + 1, :].astype(F32)

    blocks = rows // BLOCK
    lanes_in = BLOCK // 128

    def lane_column(source, block):
        return to_column(
            jnp.concatenate([source[block, i : i + 1, :] for i in range(lanes_in)], axis=0)
        )

    def middle(lifted, cot_all, turned, w_left, w_right, w_down, hidden_units, back_out, low_turned):
        tok_all = hidden_units.at[2, :, pl.ds(0, features)]
        halves = (pl.ds(0, width), pl.ds(width, width))
        w_query, w_key = (hidden_units.at[0, :, cut] for cut in halves)
        w_value, w_gate = (hidden_units.at[1, :, cut] for cut in halves)
        q_all, gate_all = (turned.at[0, :, cut] for cut in halves)
        slope_q, slope_k = (turned.at[1, :, cut] for cut in halves)
        heads_all = low_turned
        k_all, v_all = (w_down.at[:, cut] for cut in halves)
        k_rows, v_rows = (whole.at[pl.ds(BAND, rows), :] for whole in (k_all, v_all))

        first = [load(0, tok, tok_all), load(1, wk, w_key), load(2, wv, w_value), load(3, wq, w_query), load(4, wg, w_gate)]
        pl.semaphore_wait(barrier, len(partners))
        wo_across().start()
        pad = jnp.full((1, BAND), -1.0, F32)
        seg_ref[0:1, :BAND] = pad
        seg_ref[0:1, BAND + rows :] = pad
        seg_ref[0:1, BAND : BAND + rows] = ids_ref[...].astype(F32)
        for padded in (k_all, v_all):
            padded[:BAND, :] = jnp.zeros((BAND, width), BF16)
        for copy in first:
            copy.wait()
        later = [load(5, wo, wo_own), load(6, cot, cot_all), load(7, wl, w_left), load(8, wr, w_right)]
        keeps = [(q_all, q), (k_rows, k), (v_rows, v), (gate_all, gate), (slope_q, sq), (slope_k, sk), (heads_all, heads)]

        def forward_block(block, carry):
            place = chunk(block)
            here = pl.ds(pl.multiple_of(BAND + block * BLOCK, 128), BLOCK)
            span = pl.ds(pl.multiple_of(block * BLOCK, BLOCK), SPAN)
            source = tok_all[place, :].astype(F32)
            normed = (source * rms_scale(source)).astype(BF16)
            for weight, slope, target, rows_at in ((w_key, slope_k, k_all, here), (w_query, slope_q, q_all, place)):
                pre = nn(normed, weight[...])
                sigma = jax.nn.sigmoid(pre)
                target[rows_at, :] = (pre * sigma).astype(BF16)
                slope[place, :] = (sigma * (1.0 + pre * (1.0 - sigma))).astype(BF16)
            v_all[here, :] = nn(normed, w_value[...]).astype(BF16)
            gate_all[place, :] = nn(normed, w_gate[...]).astype(BF16)
            row_at = iota_f32((BLOCK, 1), 0)
            key_at = iota_f32((1, SPAN), 1) - float(BAND)
            allowed = (seg_column(BAND + block * BLOCK) == seg_lanes(block * BLOCK, SPAN)) & (
                row_at >= key_at
            )
            total = jnp.zeros((BLOCK, 1), F32)
            for head in range(width // 128):
                lanes = slice(head * 128, head * 128 + 128)
                decay = decay_ref[head]
                falloff = jnp.exp(-decay * row_at) * jnp.exp(decay * key_at)
                scores = nt(q_all[place, lanes], k_all[span, lanes])
                weighted = jnp.where(allowed, scores * falloff, 0.0).astype(BF16)
                found = nn(weighted, v_all[span, lanes])
                total = total + jnp.sum(found * found, axis=1, keepdims=True)
                heads_all[place, lanes] = found.astype(BF16)
                u_all[place, lanes] = (
                    found * gain_lanes(head) * gate_all[place, lanes].astype(F32)
                ).astype(BF16)
            lane_rows = to_rows(total)
            for i in range(lanes_in):
                sums_ref[block, i : i + 1, :] = lane_rows[i : i + 1, :]
            u_copy(block).start()
            sum_copy(block).start()
            for index, (source, target) in enumerate(keeps):
                pltpu.make_async_copy(
                    source.at[place, :], target.at[place, :], kept.at[index]
                ).start()

            @pl.when(block == 0)
            def _():
                wo_across().wait()
                wo_paired().start()

            @pl.when(block == 1)
            def _():
                wo_paired().wait()
                wo_beside().start()

            @pl.when(block == blocks - 1)
            def _():
                wo_beside().wait()
                wo_sibling().start()

            return carry

        lax.fori_loop(0, blocks, forward_block, 0)
        for index, (source, target) in enumerate(keeps):
            pltpu.make_async_copy(source, target, kept.at[index]).wait()
        later.append(load(9, wd, w_down))
        for copy in later:
            copy.wait()
        wo_sibling().wait()

        def gated(step, carry):
            block = lax.rem(step + 1 - side, blocks)
            part = lax.rem(block, 2)
            owned = lax.div(block, 2) == side
            place = chunk(block)
            u_copy(block).wait()
            sum_copy(block).wait()
            for i in range(lanes_in):
                scale_rows[block, i : i + 1, :] = lax.rsqrt(
                    (sums_ref[block, i : i + 1, :] + sum_in[block, i : i + 1, :]) / full_inner + eps
                )
            attn = nn(u_all[place, :], wo_own[...]) + nn(u_in[place, :], wo_peer[...])
            state = tok_all[place, :].astype(F32) + lane_column(scale_rows, block) * attn
            rows_in = (state * rms_scale(state)).astype(BF16)
            lifted[...] = rows_in

            @pl.when(owned)
            def _():
                hidden[chunk(part), :] = state

            rows_cot = cot_all[place, :]
            for start, size in tiles(units):
                cut = slice(start, start + size)
                left = nn(lifted[...], w_left[:, cut])
                right = nn(lifted[...], w_right[:, cut])
                grad = nt(rows_cot, w_down[cut, :])
                hidden_units[2, place, cut] = (left * right).astype(BF16)
                hidden_units[0, place, cut] = (grad * right).astype(BF16)
                hidden_units[1, place, cut] = (grad * left).astype(BF16)
            back = nt(hidden_units[0, place, :], w_left[...]) + nt(
                hidden_units[1, place, :], w_right[...]
            )

            @pl.when(owned)
            def _():
                grad_hidden[chunk(part), :] = back

            @pl.when(jnp.logical_not(owned))
            def _():
                back_out[chunk(part), :] = back.astype(BF16)
                back_copy(back_out, part).start()

            put_turned(turned.at[0], rows_in, place)
            put_turned(turned.at[1], rows_cot, place)
            return carry

        lax.fori_loop(0, blocks, gated, 0)

        def down_other(part, carry):
            down_out[chunk(part), :] = nn(
                hidden_units[2, at(other0 + part * BLOCK), :], w_down[...]
            ).astype(BF16)
            return carry

        lax.fori_loop(0, 2, down_other, 0)

        def block_step(block, carry):
            lhs, rhs = turned.at[lax.div(block, 2)], hidden_units.at[block]
            stage_send(lhs, rhs, 0, block, ffn_c, units)

            @pl.when(block < 2)
            def _():
                part = block
                back_copy(back_out, part).wait()
                state = hidden[chunk(part), :]
                pulled = grad_hidden[chunk(part), :] + back_in[chunk(part), :].astype(F32)
                grad = cot_all[at(own0 + part * BLOCK), :].astype(F32) + rms_back(
                    state, rms_scale(state), pulled
                )
                grad_hidden[chunk(part), :] = grad
                low = grad.astype(BF16)
                for_own = nt(low, wo_own[...])
                for_peer = nt(low, wo_peer[...])
                mixed_out[chunk(part), :] = for_peer.astype(BF16)
                mixed_grad[at(own0 + part * BLOCK), :] = for_own.astype(BF16)
                mixed_copy(part).start()
                place = at(own0 + part * BLOCK)
                both = jnp.sum(
                    u_all[place, :].astype(F32) * for_own + u_in[place, :].astype(F32) * for_peer,
                    axis=1,
                    keepdims=True,
                )
                lanes = to_rows(both)
                for i in range(lanes_in):
                    cross[side * 2 + part, i : i + 1, :] = lanes[i : i + 1, :]
                cross_copy(part).start()
                put_turned(low_turned, low, chunk(part))
                scale = lane_column(scale_rows, side * 2 + part)
                back_out[chunk(part), :width] = (u_all[place, :].astype(F32) * scale).astype(BF16)
                back_out[chunk(part), width:] = (u_in[place, :].astype(F32) * scale).astype(BF16)

                @pl.when(part == 1)
                def _():
                    down_copy(0).start()
                    down_copy(1).start()

            stage_core(
                lhs, rhs, 0, block, ffn_c, units, second_copy(0, block, ffn_c, ffn_y)
            )
            return carry

        lax.fori_loop(0, 2, block_step, 0)
        columns = 2 * width
        stage_send(low_turned, back_out, 3, 0, att_c, columns)
        stage_core(low_turned, back_out, 3, 0, att_c, columns, second_copy(3, 0, att_c, att_y))
        lax.fori_loop(2, 3, block_step, 0)

        def down_own(part, carry):
            hidden[chunk(part), :] += nn(
                hidden_units[2, at(own0 + part * BLOCK), :], w_down[...]
            )
            return carry

        lax.fori_loop(0, 2, down_own, 0)
        stage_second(0, 0, ffn_c, ffn_y, ffn_z)

    pl.run_scoped(
        middle,
        pltpu.VMEM((BLOCK, features), BF16),
        pltpu.VMEM((rows, features), BF16),
        pltpu.VMEM((2, features, rows), BF16),
        pltpu.VMEM((features, units), BF16),
        pltpu.VMEM((features, units), BF16),
        pltpu.VMEM((units, features), BF16),
        pltpu.VMEM((3, rows, units), BF16),
        pltpu.VMEM((half, features), BF16),
        pltpu.VMEM((features, half), BF16),
    )

    def last(q_all, grads, k_all, v_all, slope_q, slope_k, heads_all, gate_all, pulls, weights, norm_out, norm_own, results, turned, tok_all, ffn_ref, attn_ref):
        columns = 2 * width
        loads = [
            load(0, v, v_all.at[pl.ds(BAND, rows), :]),
            load(1, k, k_all.at[pl.ds(BAND, rows), :]),
            load(2, q, q_all.at[pl.ds(0, rows), :]),
            load(3, gate, gate_all),
            load(4, heads, heads_all),
            load(5, sq, slope_q),
            load(6, sk, slope_k),
        ]
        later = [load(7, tok, tok_all)] + [
            load(8 + i, source, weights.at[:, pl.ds(i * width, width)])
            for i, source in enumerate((wq, wk, wv, wg))
        ]
        for padded in (k_all, v_all):
            padded[:BAND, :] = jnp.zeros((BAND, width), BF16)
        for padded in (q_all, grads):
            padded[rows:, :] = jnp.zeros((BAND, width), BF16)
        gain_sum[0] = jnp.zeros(gain_sum.shape[1:], F32)
        for copy in loads:
            copy.wait()
        for part in range(2):
            mixed_copy(part).wait()
            cross_copy(part).wait()

        gain_row = jnp.concatenate([gain_lanes(i) for i in range(width // 128)], axis=1)

        def prepare(block, carry):
            place = chunk(block)
            scale = lane_column(scale_rows, block)
            joint = lane_column(cross, block)
            grad = mixed_grad[place, :].astype(F32)
            head_rows = heads_all[place, :].astype(F32)
            gain = gain_row
            scaled = grad * gate_all[place, :].astype(F32)
            unit = head_rows * scale
            gain_sum[0, 0:1, :] += jnp.sum(scaled * unit, axis=0, keepdims=True)
            pulls[1, place, width:] = (grad * (unit * gain)).astype(BF16)
            grads[place, :] = (
                scale * (scaled * gain)
                - head_rows * (scale * scale * scale) * (joint / full_inner)
            ).astype(BF16)
            return carry

        lax.fori_loop(0, rows // BLOCK, prepare, 0)
        gain_copy(0, 0, sibling).start()
        stage_second(0, 1, ffn_c, ffn_y, ffn_z)
        stage_pass(0, 0, ffn_y, ffn_z)

        def by_query(block, carry):
            place, span = chunk(block), pl.ds(pl.multiple_of(block * BLOCK, BLOCK), SPAN)
            row_at = iota_f32((BLOCK, 1), 0)
            key_at = iota_f32((1, SPAN), 1) - float(BAND)
            allowed = (seg_column(BAND + block * BLOCK) == seg_lanes(block * BLOCK, SPAN)) & (
                row_at >= key_at
            )
            for head in range(width // 128):
                lanes = slice(head * 128, head * 128 + 128)
                decay = decay_ref[head]
                falloff = jnp.exp(-decay * row_at) * jnp.exp(decay * key_at)
                grad = nt(grads[place, lanes], v_all[span, lanes])
                grad = jnp.where(allowed, grad * falloff, 0.0).astype(BF16)
                pulls[0, place, lanes] = (
                    nn(grad, k_all[span, lanes]) * slope_q[place, lanes].astype(F32)
                ).astype(BF16)
            return carry

        def finish_out(part, carry):
            down_copy(part).wait()
            results[0, chunk(part), :] = (
                hidden[chunk(part), :] + down_in[chunk(part), :].astype(F32)
            ).astype(BF16)
            out_copy(results.at[0], part).start()
            pltpu.make_async_copy(
                results.at[0, chunk(part), :], out_ref.at[at(own0 + part * BLOCK), :], local.at[part]
            ).start()
            return carry

        lax.fori_loop(0, rows // BLOCK, by_query, 0)
        lax.fori_loop(0, 1, finish_out, 0)

        def by_key(block, carry):
            place, span = chunk(block), pl.ds(pl.multiple_of(block * BLOCK, BLOCK), SPAN)
            here = pl.ds(pl.multiple_of(BAND + block * BLOCK, 128), BLOCK)
            key_at = iota_f32((BLOCK, 1), 0)
            row_at = iota_f32((1, SPAN), 1)
            allowed = (
                seg_column(BAND + block * BLOCK) == seg_lanes(BAND + block * BLOCK, SPAN)
            ) & (row_at >= key_at)
            for head in range(width // 128):
                lanes = slice(head * 128, head * 128 + 128)
                turned_lanes = slice(width + head * 128, width + head * 128 + 128)
                decay = decay_ref[head]
                falloff = jnp.exp(decay * key_at) * jnp.exp(-decay * row_at)
                span_q, span_grad = q_all[span, lanes], grads[span, lanes]
                scores = nt(k_all[here, lanes], span_q)
                weighted = jnp.where(allowed, scores * falloff, 0.0).astype(BF16)
                pulls[1, place, lanes] = nn(weighted, span_grad).astype(BF16)
                grad = nt(v_all[here, lanes], span_grad)
                grad = jnp.where(allowed, grad * falloff, 0.0).astype(BF16)
                pulls[0, place, turned_lanes] = (
                    nn(grad, span_q) * slope_k[place, lanes].astype(F32)
                ).astype(BF16)
            return carry

        lax.fori_loop(0, rows // BLOCK, by_key, 0)
        lax.fori_loop(1, 2, finish_out, 0)
        stage_second(3, 0, att_c, att_y, att_z)
        stage_pass(0, 1, ffn_y, ffn_z)
        for copy in later:
            copy.wait()

        def normed_part(step, carry):
            part = lax.rem(step, 2)
            place = at((1 - side + lax.div(step, 2) * (2 * side - 1)) * half + part * BLOCK)
            back = nt(pulls[0, place, :], weights[:, :columns]) + nt(
                pulls[1, place, :], weights[:, columns:]
            )

            @pl.when(step < 2)
            def _():
                norm_out[chunk(part), :] = back.astype(BF16)
                norm_copy(norm_out, part).start()

            @pl.when(step >= 2)
            def _():
                norm_own[chunk(part), :] = back

            return carry

        lax.fori_loop(0, 4, normed_part, 0)


        def turn(block, carry):
            source = tok_all[chunk(block), :].astype(F32)
            put_turned(turned, (source * rms_scale(source)).astype(BF16), chunk(block))
            return carry

        lax.fori_loop(0, rows // BLOCK, turn, 0)

        gain_copy(0, 0, sibling).wait()
        gain_sum[1] = gain_sum[0] + gain_in[0]
        gain_copy(1, 1, beside).start()

        def block_step(step, carry):
            block = step + 1
            rhs = pulls.at[step]
            stage_send(turned, rhs, 3, block, att_c, columns)
            stage_core(
                turned, rhs, 3, block, att_c, columns, second_copy(3, block, att_c, att_y)
            )

            @pl.when(step == 0)
            def _():
                stage_second(0, 2, ffn_c, ffn_y, ffn_z)
                stage_pass(3, 0, att_y, att_z)

            return carry

        lax.fori_loop(0, 2, block_step, 0)
        gain_copy(1, 1, beside).wait()
        gain_sum[2] = gain_sum[1] + gain_in[1]
        for hop in range(1, thirds):
            gain_copy(2, 1 + hop, far(hop)).start()

        def attn_copy(block):
            return pltpu.make_async_copy(attn_ref.at[block], attn_out.at[block], local.at[7 + block])

        def attn_total(block, carry):
            attn_ref[block] = stage_third(3, block, att_y, att_z)

            @pl.when(block > 0)
            def _():
                attn_copy(block).start()

            return carry

        stage_pass(0, 2, ffn_y, ffn_z)
        lax.fori_loop(0, 1, attn_total, 0)
        turn_out[...] = attn_ref[0, :, width:].astype(BF16)
        turn_copy = over_x(25, turn_out, turn_in)
        turn_copy.start()

        def finish_tokens(part, carry):
            norm_copy(norm_out, part).wait()
            pulled = norm_own[chunk(part), :] + norm_in[chunk(part), :].astype(F32)
            source = tok_all[at(own0 + part * BLOCK), :].astype(F32)
            results[1, chunk(part), :] = (
                grad_hidden[chunk(part), :] + rms_back(source, rms_scale(source), pulled)
            ).astype(BF16)
            tg_copy(results.at[1], part).start()
            pltpu.make_async_copy(
                results.at[1, chunk(part), :], tg_ref.at[at(own0 + part * BLOCK), :], local.at[2 + part]
            ).start()
            return carry

        lax.fori_loop(0, 2, finish_tokens, 0)

        def seconds_last(block, carry):
            stage_second(3, block, att_c, att_y, att_z)

            @pl.when(block == 2)
            def _():
                stage_pass(3, 1, att_y, att_z)

            return carry

        lax.fori_loop(1, 3, seconds_last, 0)

        def ffn_total(block, carry):
            ffn_ref[block] = stage_third(0, block, ffn_y, ffn_z)
            pltpu.make_async_copy(ffn_ref.at[block], ffn_out.at[block], local.at[4 + block]).start()
            return carry

        lax.fori_loop(0, 3, ffn_total, 0)
        stage_pass(3, 2, att_y, att_z)
        lax.fori_loop(1, 3, attn_total, 0)
        total = gain_sum[2]
        for hop in range(1, thirds):
            gain_copy(2, 1 + hop, far(hop)).wait()
            total = total + gain_in[1 + hop]
        gain_out[...] = total
        turn_copy.wait()
        attn_ref[0, :, :width] += turn_in[...].astype(F32)
        attn_copy(0).start()

        def close(part, carry):
            out_copy(results.at[0], part).wait()
            tg_copy(results.at[1], part).wait()
            for index, target in ((0, out_ref), (1, tg_ref)):
                pltpu.make_async_copy(
                    results.at[index, chunk(part), :],
                    target.at[at(own0 + part * BLOCK), :],
                    local.at[2 * index + part],
                ).wait()
            return carry

        lax.fori_loop(0, 2, close, 0)
        for block in range(3):
            pltpu.make_async_copy(ffn_ref.at[block], ffn_out.at[block], local.at[4 + block]).wait()
            attn_copy(block).wait()

    pl.run_scoped(
        last,
        pltpu.VMEM((rows + BAND, width), BF16),
        pltpu.VMEM((rows + BAND, width), BF16),
        pltpu.VMEM((rows + BAND, width), BF16),
        pltpu.VMEM((rows + BAND, width), BF16),
        pltpu.VMEM((rows, width), BF16),
        pltpu.VMEM((rows, width), BF16),
        pltpu.VMEM((rows, width), BF16),
        pltpu.VMEM((rows, width), BF16),
        pltpu.VMEM((2, rows, 2 * width), BF16),
        pltpu.VMEM((features, 4 * width), BF16),
        pltpu.VMEM((half, features), BF16),
        pltpu.VMEM((half, features), F32),
        pltpu.VMEM((2, half, features), BF16),
        pltpu.VMEM((features, rows), BF16),
        pltpu.VMEM((rows, features), BF16),
        pltpu.VMEM(ffn_out.shape, F32),
        pltpu.VMEM(attn_out.shape, F32),
    )


def run_layer(ways, *args):
    (ids, decays, gain, tok, cot, wo, wl, wr, wd, wq) = args[:10]
    rows, features = tok.shape
    width, units = wq.shape[1], wl.shape[1]
    half, thirds, share = rows // 2, ways // 4, features // ways
    quarter = features // 4
    lane_rows = (rows // BLOCK, 8, 128)
    vmem = pl.BlockSpec(memory_space=pltpu.VMEM)
    hbm = pl.BlockSpec(memory_space=pl.ANY)
    shape = jax.ShapeDtypeStruct
    scratch = [
        ((rows, width), BF16), ((width, features), BF16), (lane_rows, F32),
        ((half, features), BF16), ((half, features), BF16),
        ((rows, width), BF16), (lane_rows, F32), ((half, features), BF16), ((share, width), BF16),
        ((3, 2 * quarter, units), BF16), ((3, quarter, units), BF16),
        ((3, quarter - share, units), BF16),
        ((3, 2 * quarter, 2 * width), BF16), ((3, quarter, 2 * width), BF16),
        ((3, quarter - share, 2 * width), BF16), ((thirds + 1, 8, width), F32),
        ((1, rows + 2 * BAND), F32), (lane_rows, F32), ((rows, width), BF16),
        ((width, features), BF16), ((half, width), BF16),
        ((half, features), BF16), ((half, features), F32), ((half, features), F32),
        (lane_rows, F32), ((2 * quarter, max(units, 2 * width)), BF16), ((3, 8, width), F32),
        ((share, width), BF16),
    ]
    return pl.pallas_call(
        functools.partial(layer, ways),
        in_specs=[vmem, pl.BlockSpec(memory_space=pltpu.SMEM), vmem] + [hbm] * (len(args) - 3),
        out_specs=[hbm] * 4 + [vmem] + [hbm] * 7,
        out_shape=[
            shape((rows, features), BF16), shape((rows, features), BF16),
            shape((3, share, units), F32), shape((3, share, 2 * width), F32), shape((8, width), F32),
        ]
        + [shape((rows, width), BF16)] * 7,
        scratch_shapes=[pltpu.VMEM(size, dtype) for size, dtype in scratch]
        + [
            pltpu.SemaphoreType.DMA((27,)), pltpu.SemaphoreType.DMA((27,)),
            pltpu.SemaphoreType.DMA((3, 6)), pltpu.SemaphoreType.DMA((3, 6)),
            pltpu.SemaphoreType.DMA((7, thirds + 1)), pltpu.SemaphoreType.DMA((7, thirds + 1)),
            pltpu.SemaphoreType.DMA((12,)), pltpu.SemaphoreType.DMA((7,)),
        ],
        compiler_params=pltpu.CompilerParams(
            collective_id=1, has_side_effects=True, vmem_limit_bytes=VMEM_LIMIT
        ),
        cost_estimate=pl.CostEstimate(flops=5 * 10**10, bytes_accessed=60 * 2**20, transcendentals=10**6),
        name="layer",
    )(*args)


def finish(
    ways, out_in, tg_in, ffn, attn, gain_in,
    out, tg, query, key, value, gate, output, gain, left, right, down,
    out_held, tg_low, tg_wide, ffn_held, attn_held, arrived, left_here,
):
    width = query.shape[1]
    blocks = 2
    size = tg.shape[0] // blocks
    places = [pl.ds(i * size, size) for i in range(blocks)]
    pairs = [(tg_in.at[i, :], tg_low.at[i, :], tg_wide.at[i, :], tg.at[i, :]) for i in places]
    pairs += [(out_in.at[i, :], out_held.at[i, :], out_held.at[i, :], out.at[i, :]) for i in places]
    for i, target in enumerate((left, right, down)):
        pairs.append((ffn.at[i], ffn_held.at[i], ffn_held.at[i], target))
    for i, j, target in ((1, 0, query), (1, 1, key), (2, 0, value), (2, 1, gate), (0, 0, output)):
        cut = pl.ds(j * width, width)
        held = attn_held.at[i, :, cut]
        pairs.append((attn.at[i, :, cut], held, held, target))
    loads = [
        pltpu.make_async_copy(source, held, arrived.at[i])
        for i, (source, held, _, _) in enumerate(pairs)
    ]
    stores = [
        pltpu.make_async_copy(held, target, left_here.at[i])
        for i, (_, _, held, target) in enumerate(pairs)
    ]
    for copy in loads:
        copy.start()
    heads, each = gain.shape
    rows_in = jnp.concatenate([gain_in[0:1, i * 128 : i * 128 + 128] for i in range(heads)], axis=0)
    lane = lax.broadcasted_iota(jnp.int32, rows_in.shape, 1)
    place = lax.broadcasted_iota(jnp.int32, gain.shape, 1)
    first = lax.axis_index("dp") * each
    found = jnp.zeros(gain.shape, F32)
    for i in range(each):
        column = jnp.sum(jnp.where(lane == first + i, rows_in, 0.0), axis=1, keepdims=True)
        found = jnp.where(place == i, column, found)
    gain[...] = found
    for i in range(len(pairs)):
        loads[i].wait()
        if i < blocks:
            tg_wide[places[i], :] = tg_low[places[i], :].astype(F32)
        stores[i].start()
    for copy in stores:
        copy.wait()


def run_finish(ways, heads, out_in, tg_in, ffn, attn, gain_in):
    rows, features = tg_in.shape
    share, units, width = ffn.shape[1], ffn.shape[2], attn.shape[2] // 2
    vmem = pl.BlockSpec(memory_space=pltpu.VMEM)
    hbm = pl.BlockSpec(memory_space=pl.ANY)
    shape = lambda *size: jax.ShapeDtypeStruct(size, F32)
    copies = 12
    return pl.pallas_call(
        functools.partial(finish, ways),
        in_specs=[hbm] * 4 + [vmem],
        out_specs=[hbm] * 7 + [vmem] + [hbm] * 3,
        out_shape=[jax.ShapeDtypeStruct((rows, features), BF16), shape(rows, features)]
        + [shape(share, width)] * 5
        + [shape(heads, gain_in.shape[1] // heads // ways)]
        + [shape(share, units)] * 3,
        scratch_shapes=[
            pltpu.VMEM((rows, features), BF16), pltpu.VMEM((rows, features), BF16),
            pltpu.VMEM((rows, features), F32), pltpu.VMEM((3, share, units), F32),
            pltpu.VMEM((3, share, 2 * width), F32),
            pltpu.SemaphoreType.DMA((copies,)), pltpu.SemaphoreType.DMA((copies,)),
        ],
        compiler_params=pltpu.CompilerParams(vmem_limit_bytes=VMEM_LIMIT),
        name="finish",
    )(out_in, tg_in, ffn, attn, gain_in)


def local(
    ways, tokens, segment_ids, decay_rate, query_weight, key_weight, value_weight, gate_weight,
    output_weight, norm_gain, left_weight, right_weight, down_weight, cotangent,
):
    held = run_layer(
        ways, segment_ids, decay_rate, norm_gain, tokens, cotangent, output_weight,
        left_weight, right_weight, down_weight, query_weight, key_weight, value_weight, gate_weight,
    )[:5]
    results = list(run_finish(ways, norm_gain.shape[0], *held))
    for turned in (6, 10):
        results[turned] = results[turned].T
    return tuple(results)


def solution(mesh):
    dp, tensor = "dp", "tensor"
    in_specs = (
        P(dp, None), P(dp, None), P(tensor), P(None, tensor), P(None, tensor), P(None, tensor),
        P(None, tensor), P(tensor, None), P(tensor, None), P(None, tensor), P(None, tensor),
        P(tensor, None), P(dp, None),
    )
    out_specs = (
        P(dp, None), P(dp, None), P(dp, tensor), P(dp, tensor), P(dp, tensor), P(dp, tensor),
        P(tensor, dp), P(tensor, dp), P(dp, tensor), P(dp, tensor), P(tensor, dp),
    )
    return jax.shard_map(
        functools.partial(local, mesh.shape[dp]),
        mesh=mesh, in_specs=in_specs, out_specs=out_specs, check_vma=False,
    )
```

```python
import functools

import jax
import jax.numpy as jnp
from jax import lax
from jax.experimental import pallas as pl
from jax.experimental.pallas import tpu as pltpu
from jax.sharding import PartitionSpec as P

MESH = pl.DeviceIdType.MESH
eps = 1e-06
BAND = 384
BLOCK = 256
SPAN = BAND + BLOCK
F32 = jnp.float32
BF16 = jnp.bfloat16
VMEM_LIMIT = 58 * 1024 * 1024


def nn(left_op, right_op):
    return jnp.dot(left_op, right_op, preferred_element_type=F32)


def nt(left_op, right_op):
    return lax.dot_general(
        left_op, right_op, (((1,), (1,)), ((), ())), preferred_element_type=F32
    )


def at(start):
    return pl.ds(pl.multiple_of(start, BLOCK), BLOCK)


def rms_scale(values):
    return lax.rsqrt(jnp.mean(values * values, axis=1, keepdims=True) + eps)


def rms_back(values, scale, grads):
    return scale * grads - values * (scale * scale * scale) * jnp.mean(
        values * grads, axis=1, keepdims=True
    )


def eye():
    shape = (128, 128)
    return lax.broadcasted_iota(jnp.int32, shape, 0) == lax.broadcasted_iota(jnp.int32, shape, 1)


def to_column(rows):
    parts = [
        jnp.sum(jnp.where(eye(), rows[i : i + 1, :], 0.0), axis=1, keepdims=True)
        for i in range(rows.shape[0])
    ]
    return jnp.concatenate(parts, axis=0)


def to_rows(column):
    parts = [
        jnp.sum(jnp.where(eye(), column[i : i + 128, :], 0.0), axis=0, keepdims=True)
        for i in range(0, column.shape[0], 128)
    ]
    return jnp.concatenate(parts, axis=0)


def iota_f32(shape, axis):
    return lax.broadcasted_iota(jnp.int32, shape, axis).astype(F32)


def tiles(extent, most=512):
    return [(start, min(most, extent - start)) for start in range(0, extent, most)]


def layer(
    ways,
    ids_ref, decay_ref, gain_ref, tok, cot, wo, wl, wr, wd, wq, wk, wv, wg,
    out_ref, tg_ref, ffn_ref, attn_ref, gain_out,
    q, k, v, gate, heads, sq, sk,
    u_in, wo_peer, sum_in, back_in, down_in, mixed_grad, cross, turn_in,
    ffn_c, ffn_y, ffn_z, att_c, att_y, att_z, gain_in,
    seg_ref, sums_ref, u_all, wo_own, down_out, hidden, grad_hidden, scale_rows, core_out, gain_sum, turn_out,
    send, recv, dp_send, dp_recv, z_send, z_recv, local, kept,
):
    dp, side = lax.axis_index("dp"), lax.axis_index("tensor")
    core, second, third = lax.rem(dp, 2), lax.rem(lax.div(dp, 2), 2), lax.div(dp, 4)
    rows, features = tok.shape
    width = wq.shape[1]
    units = wl.shape[1]
    half = rows // 2
    thirds = ways // 4
    share = features // ways
    full_inner = float(2 * width)
    own0, other0 = side * half, (1 - side) * half
    across = (dp, 1 - side)
    sibling = (dp + 1 - 2 * core, side)
    beside = (dp + 2 - 4 * second, side)

    def far(hop):
        return (lax.rem(third + hop, thirds) * 4 + second * 2 + core, side)

    def remote(source, target, send_sem, recv_sem, device):
        return pltpu.make_async_remote_copy(
            src_ref=source, dst_ref=target, send_sem=send_sem, recv_sem=recv_sem,
            device_id=device, device_id_type=MESH,
        )

    def over_x(index, source, target):
        return remote(source, target, send.at[index], recv.at[index], across)

    def load(index, source, target):
        copy = pltpu.make_async_copy(source, target, local.at[index])
        copy.start()
        return copy

    def put_turned(target, block, column):
        turned = jnp.transpose(block)
        for owner in range(ways):
            place, left = 0, owner
            for _ in range(ways.bit_length() - 1):
                place, left = place * 2 + left % 2, left // 2
            target[place * share : (place + 1) * share, column] = turned[
                owner * share : (owner + 1) * share, :
            ]

    def chunk(part):
        return at(part * BLOCK)

    def u_copy(block):
        return over_x(block, u_all.at[chunk(block), :], u_in.at[chunk(block), :])

    def sum_copy(block):
        return over_x(4 + block, sums_ref.at[block], sum_in.at[block])

    def back_copy(source, part):
        return over_x(11 + part, source.at[chunk(part), :], back_in.at[chunk(part), :])

    def mixed_copy(part):
        place = at(own0 + part * BLOCK)
        return over_x(13 + part, u_all.at[place, :], mixed_grad.at[place, :])

    def cross_copy(part):
        mine = cross.at[side * 2 + part]
        return over_x(15 + part, mine, mine)

    def down_copy(part):
        return over_x(17 + part, down_out.at[chunk(part), :], down_in.at[chunk(part), :])

    def norm_copy(source, part):
        return over_x(19 + part, source.at[chunk(part), :], back_in.at[chunk(part), :])

    def out_copy(part):
        place = out_ref.at[at(own0 + part * BLOCK), :]
        return over_x(21 + part, place, place)

    def tg_copy(part):
        place = tg_ref.at[at(own0 + part * BLOCK), :]
        return over_x(23 + part, place, place)

    odd = lax.rem(third, 2)
    paired = ((third + 1 - 2 * odd) * 4 + second * 2 + core, side)

    def wo_rows(start, size):
        return pl.ds(pl.multiple_of(start, size), size)

    def wo_across():
        place = wo_rows(((core * 2 + second) * 2 + odd) * (width // 8), width // 8)
        return over_x(8, wo.at[place, :], wo_peer.at[place, :])

    def wo_pass(index, place, device):
        piece = wo_peer.at[place, :]
        return remote(piece, piece, send.at[index], recv.at[index], device)

    def wo_paired():
        place = wo_rows(((core * 2 + second) * 2 + odd) * (width // 8), width // 8)
        return wo_pass(26, place, paired)

    def wo_beside():
        return wo_pass(9, wo_rows((core * 2 + second) * (width // 4), width // 4), beside)

    def wo_sibling():
        return wo_pass(10, wo_rows(core * (width // 2), width // 2), sibling)

    def section(part):
        return chunk(1 - second + part * (2 * second - 1))

    def core_copy(first, block, landing, columns, part):
        return remote(
            core_out.at[section(part), pl.ds(0, columns)], landing.at[block, section(part), :],
            dp_send.at[part, first + block], dp_recv.at[part, first + block], sibling,
        )

    def second_copy(first, block, summed, landing):
        return remote(
            summed.at[block, at((1 - second) * BLOCK), :], landing.at[block],
            dp_send.at[2, first + block], dp_recv.at[2, first + block], beside,
        )

    levels = thirds.bit_length() - 1

    def third_bit(level):
        return lax.rem(lax.div(third, 2**level), 2)

    def third_start(level):
        return BLOCK - (BLOCK >> level)

    def third_rows(level, bit):
        size = BLOCK >> (level + 1)
        start = bit * size + (third_start(level - 1) if level else 0)
        return pl.ds(pl.multiple_of(start, size), size)

    def third_source(level, summed, landing):
        return landing if level else summed

    def third_copy(first, block, level, summed, landing):
        bit = third_bit(level)
        other = third + (1 - 2 * bit) * 2**level
        return remote(
            third_source(level, summed, landing).at[block, third_rows(level, 1 - bit), :],
            landing.at[block, pl.ds(third_start(level), BLOCK >> (level + 1)), :],
            z_send.at[first + block, level], z_recv.at[first + block, level],
            (other * 4 + second * 2 + core, side),
        )

    def stage_send(turned, grads, first, block, landing, columns):
        def one(part, carry):
            place = section(part)
            left_op = turned[pl.ds(pl.multiple_of((1 - core) * 2 * BLOCK + place.start, BLOCK), BLOCK), :]
            for start, size in tiles(columns):
                core_out[place, start : start + size] = nn(
                    left_op, grads[:, start : start + size]
                ).astype(BF16)
            core_copy(first, block, landing, columns, part).start()
            return carry

        lax.fori_loop(0, 2, one, 0)

    def stage_core(turned, grads, first, block, landing, columns, onward):
        def one(part, carry):
            place = section(part)
            left_op = turned[pl.ds(pl.multiple_of(core * 2 * BLOCK + place.start, BLOCK), BLOCK), :]
            core_copy(first, block, landing, columns, part).wait()
            for start, size in tiles(columns):
                cut = slice(start, start + size)
                total = nn(left_op, grads[:, cut]) + landing[block, place, cut].astype(F32)
                landing[block, place, cut] = total.astype(BF16)

            @pl.when(part == 0)
            def _():
                onward.start()

            return carry

        lax.fori_loop(0, 2, one, 0)

    def stage_second(first, block, summed, landing, group_out):
        copy = second_copy(first, block, summed, landing)
        copy.wait()
        for start, size in tiles(landing.shape[2]):
            cut = slice(start, start + size)
            total = (
                summed[block, at(second * BLOCK), cut].astype(F32)
                + landing[block, :, cut].astype(F32)
            )
            landing[block, :, cut] = total.astype(BF16)
        third_copy(first, block, 0, landing, group_out).start()

    def third_total(first, block, level, summed, landing):
        third_copy(first, block, level, summed, landing).wait()
        kept_rows = third_source(level, summed, landing)[
            block, third_rows(level, third_bit(level)), :
        ]
        here = pl.ds(third_start(level), BLOCK >> (level + 1))
        return kept_rows.astype(F32) + landing[block, here, :].astype(F32)

    def stage_pass(first, block, summed, landing):
        for level in range(levels - 1):
            here = pl.ds(third_start(level), BLOCK >> (level + 1))
            landing[block, here, :] = third_total(first, block, level, summed, landing).astype(BF16)
            third_copy(first, block, level + 1, summed, landing).start()

    def stage_third(first, block, summed, landing):
        return third_total(first, block, levels - 1, summed, landing)

    def gain_copy(stage, slot, device):
        return remote(
            gain_sum.at[stage], gain_in.at[slot], z_send.at[6, slot], z_recv.at[6, slot], device
        )

    barrier = pltpu.get_barrier_semaphore()
    partners = [across, sibling, beside] + [far(hop) for hop in range(1, thirds)]
    for device in partners:
        pl.semaphore_signal(barrier, inc=1, device_id=device, device_id_type=MESH)

    def seg_lanes(start, size):
        return seg_ref[0:1, pl.ds(pl.multiple_of(start, 128), size)]

    def seg_column(start):
        return to_column(
            jnp.concatenate([seg_lanes(start + i, 128) for i in range(0, BLOCK, 128)], axis=0)
        )

    def gain_lanes(head):
        return gain_ref[head : head + 1, :].astype(F32)

    blocks = rows // BLOCK
    lanes_in = BLOCK // 128

    def lane_column(source, block):
        return to_column(
            jnp.concatenate([source[block, i : i + 1, :] for i in range(lanes_in)], axis=0)
        )

    def middle(lifted, cot_all, turned, w_left, w_right, w_down, hidden_units, back_out, low_turned):
        tok_all = hidden_units.at[2, :, pl.ds(0, features)]
        halves = (pl.ds(0, width), pl.ds(width, width))
        w_query, w_key = (hidden_units.at[0, :, cut] for cut in halves)
        w_value, w_gate = (hidden_units.at[1, :, cut] for cut in halves)
        q_all, gate_all = (turned.at[0, :, cut] for cut in halves)
        slope_q, slope_k = (turned.at[1, :, cut] for cut in halves)
        heads_all = low_turned
        k_all, v_all = (w_down.at[:, cut] for cut in halves)
        k_rows, v_rows = (whole.at[pl.ds(BAND, rows), :] for whole in (k_all, v_all))

        first = [load(0, tok, tok_all), load(1, wk, w_key), load(2, wv, w_value), load(3, wq, w_query), load(4, wg, w_gate)]
        pl.semaphore_wait(barrier, len(partners))
        wo_across().start()
        pad = jnp.full((1, BAND), -1.0, F32)
        seg_ref[0:1, :BAND] = pad
        seg_ref[0:1, BAND + rows :] = pad
        seg_ref[0:1, BAND : BAND + rows] = ids_ref[...].astype(F32)
        for padded in (k_all, v_all):
            padded[:BAND, :] = jnp.zeros((BAND, width), BF16)
        for copy in first:
            copy.wait()
        later = [load(5, wo, wo_own), load(6, cot, cot_all), load(7, wl, w_left), load(8, wr, w_right)]
        keeps = [(q_all, q), (k_rows, k), (v_rows, v), (gate_all, gate), (slope_q, sq), (slope_k, sk), (heads_all, heads)]

        def forward_block(block, carry):
            place = chunk(block)
            here = pl.ds(pl.multiple_of(BAND + block * BLOCK, 128), BLOCK)
            span = pl.ds(pl.multiple_of(block * BLOCK, BLOCK), SPAN)
            source = tok_all[place, :].astype(F32)
            normed = (source * rms_scale(source)).astype(BF16)
            for weight, slope, target, rows_at in ((w_key, slope_k, k_all, here), (w_query, slope_q, q_all, place)):
                pre = nn(normed, weight[...])
                sigma = jax.nn.sigmoid(pre)
                target[rows_at, :] = (pre * sigma).astype(BF16)
                slope[place, :] = (sigma * (1.0 + pre * (1.0 - sigma))).astype(BF16)
            v_all[here, :] = nn(normed, w_value[...]).astype(BF16)
            gate_all[place, :] = nn(normed, w_gate[...]).astype(BF16)
            row_at = iota_f32((BLOCK, 1), 0)
            key_at = iota_f32((1, SPAN), 1) - float(BAND)
            allowed = (seg_column(BAND + block * BLOCK) == seg_lanes(block * BLOCK, SPAN)) & (
                row_at >= key_at
            )
            total = jnp.zeros((BLOCK, 1), F32)
            for head in range(width // 128):
                lanes = slice(head * 128, head * 128 + 128)
                decay = decay_ref[head]
                falloff = jnp.exp(-decay * row_at) * jnp.exp(decay * key_at)
                scores = nt(q_all[place, lanes], k_all[span, lanes])
                weighted = jnp.where(allowed, scores * falloff, 0.0).astype(BF16)
                found = nn(weighted, v_all[span, lanes])
                total = total + jnp.sum(found * found, axis=1, keepdims=True)
                heads_all[place, lanes] = found.astype(BF16)
                u_all[place, lanes] = (
                    found * gain_lanes(head) * gate_all[place, lanes].astype(F32)
                ).astype(BF16)
            lane_rows = to_rows(total)
            for i in range(lanes_in):
                sums_ref[block, i : i + 1, :] = lane_rows[i : i + 1, :]
            u_copy(block).start()
            sum_copy(block).start()
            for index, (source, target) in enumerate(keeps):
                pltpu.make_async_copy(
                    source.at[place, :], target.at[place, :], kept.at[index]
                ).start()

            @pl.when(block == 0)
            def _():
                wo_across().wait()
                wo_paired().start()

            @pl.when(block == 1)
            def _():
                wo_paired().wait()
                wo_beside().start()

            @pl.when(block == blocks - 1)
            def _():
                wo_beside().wait()
                wo_sibling().start()

            return carry

        lax.fori_loop(0, blocks, forward_block, 0)
        for index, (source, target) in enumerate(keeps):
            pltpu.make_async_copy(source, target, kept.at[index]).wait()
        later.append(load(9, wd, w_down))
        for copy in later:
            copy.wait()
        wo_sibling().wait()

        def gated(step, carry):
            block = lax.rem(step + 1 - side, blocks)
            part = lax.rem(block, 2)
            owned = lax.div(block, 2) == side
            place = chunk(block)
            u_copy(block).wait()
            sum_copy(block).wait()
            for i in range(lanes_in):
                scale_rows[block, i : i + 1, :] = lax.rsqrt(
                    (sums_ref[block, i : i + 1, :] + sum_in[block, i : i + 1, :]) / full_inner + eps
                )
            attn = nn(u_all[place, :], wo_own[...]) + nn(u_in[place, :], wo_peer[...])
            state = tok_all[place, :].astype(F32) + lane_column(scale_rows, block) * attn
            rows_in = (state * rms_scale(state)).astype(BF16)
            lifted[...] = rows_in

            @pl.when(owned)
            def _():
                hidden[chunk(part), :] = state

            rows_cot = cot_all[place, :]
            for start, size in tiles(units):
                cut = slice(start, start + size)
                left = nn(lifted[...], w_left[:, cut])
                right = nn(lifted[...], w_right[:, cut])
                grad = nt(rows_cot, w_down[cut, :])
                hidden_units[2, place, cut] = (left * right).astype(BF16)
                hidden_units[0, place, cut] = (grad * right).astype(BF16)
                hidden_units[1, place, cut] = (grad * left).astype(BF16)
            back = nt(hidden_units[0, place, :], w_left[...]) + nt(
                hidden_units[1, place, :], w_right[...]
            )

            @pl.when(owned)
            def _():
                grad_hidden[chunk(part), :] = back

            @pl.when(jnp.logical_not(owned))
            def _():
                back_out[chunk(part), :] = back.astype(BF16)
                back_copy(back_out, part).start()

            put_turned(turned.at[0], rows_in, place)
            put_turned(turned.at[1], rows_cot, place)
            return carry

        lax.fori_loop(0, blocks, gated, 0)

        def down_other(part, carry):
            down_out[chunk(part), :] = nn(
                hidden_units[2, at(other0 + part * BLOCK), :], w_down[...]
            ).astype(BF16)
            return carry

        lax.fori_loop(0, 2, down_other, 0)

        def block_step(block, carry):
            lhs, rhs = turned.at[lax.div(block, 2)], hidden_units.at[block]
            stage_send(lhs, rhs, 0, block, ffn_c, units)

            @pl.when(block < 2)
            def _():
                part = block
                back_copy(back_out, part).wait()
                state = hidden[chunk(part), :]
                pulled = grad_hidden[chunk(part), :] + back_in[chunk(part), :].astype(F32)
                grad = cot_all[at(own0 + part * BLOCK), :].astype(F32) + rms_back(
                    state, rms_scale(state), pulled
                )
                grad_hidden[chunk(part), :] = grad
                low = grad.astype(BF16)
                for_own = nt(low, wo_own[...])
                for_peer = nt(low, wo_peer[...])
                mixed_grad[at(own0 + part * BLOCK), :] = for_own.astype(BF16)
                place = at(own0 + part * BLOCK)
                both = jnp.sum(
                    u_all[place, :].astype(F32) * for_own + u_in[place, :].astype(F32) * for_peer,
                    axis=1,
                    keepdims=True,
                )
                lanes = to_rows(both)
                for i in range(lanes_in):
                    cross[side * 2 + part, i : i + 1, :] = lanes[i : i + 1, :]
                scale = lane_column(scale_rows, side * 2 + part)
                back_out[chunk(part), :width] = (u_all[place, :].astype(F32) * scale).astype(BF16)
                back_out[chunk(part), width:] = (u_in[place, :].astype(F32) * scale).astype(BF16)
                u_all[place, :] = for_peer.astype(BF16)
                mixed_copy(part).start()
                cross_copy(part).start()
                put_turned(low_turned, low, chunk(part))

                @pl.when(part == 1)
                def _():
                    down_copy(0).start()
                    down_copy(1).start()

            stage_core(
                lhs, rhs, 0, block, ffn_c, units, second_copy(0, block, ffn_c, ffn_y)
            )
            return carry

        lax.fori_loop(0, 2, block_step, 0)
        columns = 2 * width
        stage_send(low_turned, back_out, 3, 0, att_c, columns)
        stage_core(low_turned, back_out, 3, 0, att_c, columns, second_copy(3, 0, att_c, att_y))
        lax.fori_loop(2, 3, block_step, 0)

        def down_own(part, carry):
            hidden[chunk(part), :] += nn(
                hidden_units[2, at(own0 + part * BLOCK), :], w_down[...]
            )
            return carry

        lax.fori_loop(0, 2, down_own, 0)
        stage_second(0, 0, ffn_c, ffn_y, ffn_z)

    pl.run_scoped(
        middle,
        pltpu.VMEM((BLOCK, features), BF16),
        pltpu.VMEM((rows, features), BF16),
        pltpu.VMEM((2, features, rows), BF16),
        pltpu.VMEM((features, units), BF16),
        pltpu.VMEM((features, units), BF16),
        pltpu.VMEM((units, features), BF16),
        pltpu.VMEM((3, rows, units), BF16),
        pltpu.VMEM((half, features), BF16),
        pltpu.VMEM((features, half), BF16),
    )

    def last(q_all, grads, k_all, v_all, slope_q, slope_k, heads_all, gate_all, pulls, weights, norm_out, norm_own, turned, tok_all):
        columns = 2 * width
        loads = [
            load(0, v, v_all.at[pl.ds(BAND, rows), :]),
            load(1, k, k_all.at[pl.ds(BAND, rows), :]),
            load(2, q, q_all.at[pl.ds(0, rows), :]),
            load(3, gate, gate_all),
            load(4, heads, heads_all),
            load(5, sq, slope_q),
            load(6, sk, slope_k),
        ]
        later = [load(7, tok, tok_all)] + [
            load(8 + i, source, weights.at[:, pl.ds(i * width, width)])
            for i, source in enumerate((wq, wk, wv, wg))
        ]
        for padded in (k_all, v_all):
            padded[:BAND, :] = jnp.zeros((BAND, width), BF16)
        for padded in (q_all, grads):
            padded[rows:, :] = jnp.zeros((BAND, width), BF16)
        gain_sum[0] = jnp.zeros(gain_sum.shape[1:], F32)
        for copy in loads:
            copy.wait()
        for part in range(2):
            mixed_copy(part).wait()
            cross_copy(part).wait()

        gain_row = jnp.concatenate([gain_lanes(i) for i in range(width // 128)], axis=1)

        def prepare(block, carry):
            place = chunk(block)
            scale = lane_column(scale_rows, block)
            joint = lane_column(cross, block)
            grad = mixed_grad[place, :].astype(F32)
            head_rows = heads_all[place, :].astype(F32)
            gain = gain_row
            scaled = grad * gate_all[place, :].astype(F32)
            unit = head_rows * scale
            gain_sum[0, 0:1, :] += jnp.sum(scaled * unit, axis=0, keepdims=True)
            pulls[1, place, width:] = (grad * (unit * gain)).astype(BF16)
            grads[place, :] = (
                scale * (scaled * gain)
                - head_rows * (scale * scale * scale) * (joint / full_inner)
            ).astype(BF16)
            return carry

        lax.fori_loop(0, rows // BLOCK, prepare, 0)
        gain_copy(0, 0, sibling).start()
        stage_second(0, 1, ffn_c, ffn_y, ffn_z)
        stage_pass(0, 0, ffn_y, ffn_z)

        def by_query(block, carry):
            place, span = chunk(block), pl.ds(pl.multiple_of(block * BLOCK, BLOCK), SPAN)
            row_at = iota_f32((BLOCK, 1), 0)
            key_at = iota_f32((1, SPAN), 1) - float(BAND)
            allowed = (seg_column(BAND + block * BLOCK) == seg_lanes(block * BLOCK, SPAN)) & (
                row_at >= key_at
            )
            for head in range(width // 128):
                lanes = slice(head * 128, head * 128 + 128)
                decay = decay_ref[head]
                falloff = jnp.exp(-decay * row_at) * jnp.exp(decay * key_at)
                grad = nt(grads[place, lanes], v_all[span, lanes])
                grad = jnp.where(allowed, grad * falloff, 0.0).astype(BF16)
                pulls[0, place, lanes] = (
                    nn(grad, k_all[span, lanes]) * slope_q[place, lanes].astype(F32)
                ).astype(BF16)
            return carry

        def finish_out(part, carry):
            down_copy(part).wait()
            out_ref[at(own0 + part * BLOCK), :] = (
                hidden[chunk(part), :] + down_in[chunk(part), :].astype(F32)
            ).astype(BF16)
            out_copy(part).start()
            return carry

        lax.fori_loop(0, rows // BLOCK, by_query, 0)
        lax.fori_loop(0, 1, finish_out, 0)

        def by_key(block, carry):
            place, span = chunk(block), pl.ds(pl.multiple_of(block * BLOCK, BLOCK), SPAN)
            here = pl.ds(pl.multiple_of(BAND + block * BLOCK, 128), BLOCK)
            key_at = iota_f32((BLOCK, 1), 0)
            row_at = iota_f32((1, SPAN), 1)
            allowed = (
                seg_column(BAND + block * BLOCK) == seg_lanes(BAND + block * BLOCK, SPAN)
            ) & (row_at >= key_at)
            for head in range(width // 128):
                lanes = slice(head * 128, head * 128 + 128)
                turned_lanes = slice(width + head * 128, width + head * 128 + 128)
                decay = decay_ref[head]
                falloff = jnp.exp(decay * key_at) * jnp.exp(-decay * row_at)
                span_q, span_grad = q_all[span, lanes], grads[span, lanes]
                scores = nt(k_all[here, lanes], span_q)
                weighted = jnp.where(allowed, scores * falloff, 0.0).astype(BF16)
                pulls[1, place, lanes] = nn(weighted, span_grad).astype(BF16)
                grad = nt(v_all[here, lanes], span_grad)
                grad = jnp.where(allowed, grad * falloff, 0.0).astype(BF16)
                pulls[0, place, turned_lanes] = (
                    nn(grad, span_q) * slope_k[place, lanes].astype(F32)
                ).astype(BF16)
            return carry

        lax.fori_loop(0, rows // BLOCK, by_key, 0)
        lax.fori_loop(1, 2, finish_out, 0)
        stage_second(3, 0, att_c, att_y, att_z)
        stage_pass(0, 1, ffn_y, ffn_z)
        for copy in later:
            copy.wait()

        def normed_part(step, carry):
            part = lax.rem(step, 2)
            place = at((1 - side + lax.div(step, 2) * (2 * side - 1)) * half + part * BLOCK)
            back = nt(pulls[0, place, :], weights[:, :columns]) + nt(
                pulls[1, place, :], weights[:, columns:]
            )

            @pl.when(step < 2)
            def _():
                norm_out[chunk(part), :] = back.astype(BF16)
                norm_copy(norm_out, part).start()

            @pl.when(step >= 2)
            def _():
                norm_own[chunk(part), :] = back

            return carry

        lax.fori_loop(0, 4, normed_part, 0)


        def turn(block, carry):
            source = tok_all[chunk(block), :].astype(F32)
            put_turned(turned, (source * rms_scale(source)).astype(BF16), chunk(block))
            return carry

        lax.fori_loop(0, rows // BLOCK, turn, 0)

        gain_copy(0, 0, sibling).wait()
        gain_sum[1] = gain_sum[0] + gain_in[0]
        gain_copy(1, 1, beside).start()

        def block_step(step, carry):
            block = step + 1
            rhs = pulls.at[step]
            stage_send(turned, rhs, 3, block, att_c, columns)
            stage_core(
                turned, rhs, 3, block, att_c, columns, second_copy(3, block, att_c, att_y)
            )

            @pl.when(step == 0)
            def _():
                stage_second(0, 2, ffn_c, ffn_y, ffn_z)
                stage_pass(3, 0, att_y, att_z)

            return carry

        lax.fori_loop(0, 2, block_step, 0)
        gain_copy(1, 1, beside).wait()
        gain_sum[2] = gain_sum[1] + gain_in[1]
        for hop in range(1, thirds):
            gain_copy(2, 1 + hop, far(hop)).start()

        def attn_total(block, carry):
            attn_ref[block] = stage_third(3, block, att_y, att_z)
            return carry

        stage_pass(0, 2, ffn_y, ffn_z)
        lax.fori_loop(0, 1, attn_total, 0)
        turn_out[...] = attn_ref[0, :, width:].astype(BF16)
        turn_copy = over_x(25, turn_out, turn_in)
        turn_copy.start()

        def finish_tokens(part, carry):
            norm_copy(norm_out, part).wait()
            pulled = norm_own[chunk(part), :] + back_in[chunk(part), :].astype(F32)
            source = tok_all[at(own0 + part * BLOCK), :].astype(F32)
            tg_ref[at(own0 + part * BLOCK), :] = (
                grad_hidden[chunk(part), :] + rms_back(source, rms_scale(source), pulled)
            ).astype(BF16)
            tg_copy(part).start()
            return carry

        lax.fori_loop(0, 2, finish_tokens, 0)

        def seconds_last(block, carry):
            stage_second(3, block, att_c, att_y, att_z)

            @pl.when(block == 2)
            def _():
                stage_pass(3, 1, att_y, att_z)

            return carry

        lax.fori_loop(1, 3, seconds_last, 0)

        def ffn_total(block, carry):
            ffn_ref[block] = stage_third(0, block, ffn_y, ffn_z)
            return carry

        lax.fori_loop(0, 3, ffn_total, 0)
        stage_pass(3, 2, att_y, att_z)
        lax.fori_loop(1, 3, attn_total, 0)
        total = gain_sum[2]
        for hop in range(1, thirds):
            gain_copy(2, 1 + hop, far(hop)).wait()
            total = total + gain_in[1 + hop]
        gain_out[...] = total
        turn_copy.wait()
        attn_ref[0, :, :width] += turn_in[...].astype(F32)

        for part in range(2):
            out_copy(part).wait()
            tg_copy(part).wait()

    pl.run_scoped(
        last,
        pltpu.VMEM((rows + BAND, width), BF16),
        pltpu.VMEM((rows + BAND, width), BF16),
        pltpu.VMEM((rows + BAND, width), BF16),
        pltpu.VMEM((rows + BAND, width), BF16),
        pltpu.VMEM((rows, width), BF16),
        pltpu.VMEM((rows, width), BF16),
        pltpu.VMEM((rows, width), BF16),
        pltpu.VMEM((rows, width), BF16),
        pltpu.VMEM((2, rows, 2 * width), BF16),
        pltpu.VMEM((features, 4 * width), BF16),
        pltpu.VMEM((half, features), BF16),
        pltpu.VMEM((half, features), F32),
        pltpu.VMEM((features, rows), BF16),
        pltpu.VMEM((rows, features), BF16),
    )


def run_layer(ways, *args):
    (ids, decays, gain, tok, cot, wo, wl, wr, wd, wq) = args[:10]
    rows, features = tok.shape
    width, units = wq.shape[1], wl.shape[1]
    half, thirds, share = rows // 2, ways // 4, features // ways
    quarter = features // 4
    lane_rows = (rows // BLOCK, 8, 128)
    vmem = pl.BlockSpec(memory_space=pltpu.VMEM)
    hbm = pl.BlockSpec(memory_space=pl.ANY)
    shape = jax.ShapeDtypeStruct
    scratch = [
        ((rows, width), BF16), ((width, features), BF16), (lane_rows, F32),
        ((half, features), BF16), ((half, features), BF16),
        ((rows, width), BF16), (lane_rows, F32), ((share, width), BF16),
        ((3, 2 * quarter, units), BF16), ((3, quarter, units), BF16),
        ((3, quarter - share, units), BF16),
        ((3, 2 * quarter, 2 * width), BF16), ((3, quarter, 2 * width), BF16),
        ((3, quarter - share, 2 * width), BF16), ((thirds + 1, 8, width), F32),
        ((1, rows + 2 * BAND), F32), (lane_rows, F32), ((rows, width), BF16),
        ((width, features), BF16),
        ((half, features), BF16), ((half, features), F32), ((half, features), F32),
        (lane_rows, F32), ((2 * quarter, max(units, 2 * width)), BF16), ((3, 8, width), F32),
        ((share, width), BF16),
    ]
    return pl.pallas_call(
        functools.partial(layer, ways),
        in_specs=[vmem, pl.BlockSpec(memory_space=pltpu.SMEM), vmem] + [hbm] * (len(args) - 3),
        out_specs=[vmem] * 5 + [hbm] * 7,
        out_shape=[
            pltpu.VMEM((rows, features), BF16), pltpu.VMEM((rows, features), BF16),
            pltpu.VMEM((3, share, units), F32), pltpu.VMEM((3, share, 2 * width), F32),
            pltpu.VMEM((8, width), F32),
        ]
        + [shape((rows, width), BF16)] * 7,
        scratch_shapes=[pltpu.VMEM(size, dtype) for size, dtype in scratch]
        + [
            pltpu.SemaphoreType.DMA((27,)), pltpu.SemaphoreType.DMA((27,)),
            pltpu.SemaphoreType.DMA((3, 6)), pltpu.SemaphoreType.DMA((3, 6)),
            pltpu.SemaphoreType.DMA((7, thirds + 1)), pltpu.SemaphoreType.DMA((7, thirds + 1)),
            pltpu.SemaphoreType.DMA((12,)), pltpu.SemaphoreType.DMA((7,)),
        ],
        compiler_params=pltpu.CompilerParams(
            collective_id=1, has_side_effects=True, vmem_limit_bytes=VMEM_LIMIT
        ),
        cost_estimate=pl.CostEstimate(flops=5 * 10**10, bytes_accessed=60 * 2**20, transcendentals=10**6),
        name="layer",
    )(*args)


def finish(
    ways, out_in, tg_in, ffn, attn, gain_in,
    out, tg, query, key, value, gate, output, gain, left, right, down,
    tg_wide, stored,
):
    width = query.shape[1]
    blocks = 2
    size = tg.shape[0] // blocks
    places = [pl.ds(i * size, size) for i in range(blocks)]
    pairs = [(tg_wide.at[i, :], tg.at[i, :]) for i in places]
    pairs.append((out_in, out))
    pairs += [(ffn.at[i], target) for i, target in enumerate((left, right, down))]
    cuts = [(1, 0, query), (1, 1, key), (2, 0, value), (2, 1, gate), (0, 0, output)]
    pairs += [(attn.at[i, :, pl.ds(j * width, width)], target) for i, j, target in cuts]
    stores = [
        pltpu.make_async_copy(held, target, stored.at[i]) for i, (held, target) in enumerate(pairs)
    ]
    stores[blocks].start()
    for i in range(blocks):
        tg_wide[places[i], :] = tg_in[places[i], :].astype(F32)
        stores[i].start()
    for copy in stores[blocks + 1 :]:
        copy.start()
    heads, each = gain.shape
    rows_in = jnp.concatenate([gain_in[0:1, i * 128 : i * 128 + 128] for i in range(heads)], axis=0)
    lane = lax.broadcasted_iota(jnp.int32, rows_in.shape, 1)
    place = lax.broadcasted_iota(jnp.int32, gain.shape, 1)
    first = lax.axis_index("dp") * each
    found = jnp.zeros(gain.shape, F32)
    for i in range(each):
        column = jnp.sum(jnp.where(lane == first + i, rows_in, 0.0), axis=1, keepdims=True)
        found = jnp.where(place == i, column, found)
    gain[...] = found
    for copy in stores:
        copy.wait()


def run_finish(ways, heads, out_in, tg_in, ffn, attn, gain_in):
    rows, features = tg_in.shape
    share, units, width = ffn.shape[1], ffn.shape[2], attn.shape[2] // 2
    vmem = pl.BlockSpec(memory_space=pltpu.VMEM)
    hbm = pl.BlockSpec(memory_space=pl.ANY)
    shape = lambda *size: jax.ShapeDtypeStruct(size, F32)
    return pl.pallas_call(
        functools.partial(finish, ways),
        in_specs=[vmem] * 5,
        out_specs=[hbm] * 7 + [vmem] + [hbm] * 3,
        out_shape=[jax.ShapeDtypeStruct((rows, features), BF16), shape(rows, features)]
        + [shape(share, width)] * 5
        + [shape(heads, gain_in.shape[1] // heads // ways)]
        + [shape(share, units)] * 3,
        scratch_shapes=[
            pltpu.VMEM((rows, features), F32), pltpu.SemaphoreType.DMA((11,)),
        ],
        compiler_params=pltpu.CompilerParams(vmem_limit_bytes=16 * 1024 * 1024),
        name="finish",
    )(out_in, tg_in, ffn, attn, gain_in)


def local(
    ways, tokens, segment_ids, decay_rate, query_weight, key_weight, value_weight, gate_weight,
    output_weight, norm_gain, left_weight, right_weight, down_weight, cotangent,
):
    held = run_layer(
        ways, segment_ids, decay_rate, norm_gain, tokens, cotangent, output_weight,
        left_weight, right_weight, down_weight, query_weight, key_weight, value_weight, gate_weight,
    )[:5]
    results = list(run_finish(ways, norm_gain.shape[0], *held))
    for turned in (6, 10):
        results[turned] = results[turned].T
    return tuple(results)


def solution(mesh):
    dp, tensor = "dp", "tensor"
    in_specs = (
        P(dp, None), P(dp, None), P(tensor), P(None, tensor), P(None, tensor), P(None, tensor),
        P(None, tensor), P(tensor, None), P(tensor, None), P(None, tensor), P(None, tensor),
        P(tensor, None), P(dp, None),
    )
    out_specs = (
        P(dp, None), P(dp, None), P(dp, tensor), P(dp, tensor), P(dp, tensor), P(dp, tensor),
        P(tensor, dp), P(tensor, dp), P(dp, tensor), P(dp, tensor), P(tensor, dp),
    )
    return jax.shard_map(
        functools.partial(local, mesh.shape[dp]),
        mesh=mesh, in_specs=in_specs, out_specs=out_specs, check_vma=False,
    )
```
